32 devices in a mesh: seq: 4 (over x, core), grp: 8 (over z, y).
Axes of the slice: x: 2, y: 2, z: 4, core: 2. Of those that a mesh axis runs over, the one named last changes fastest.
Arguments:
- conv_input: bfloat16 [8, 512, 2688], P('grp', 'seq'), may hold values from -6 to 6
- conv_weight: float32 [4, 2688], replicated, may hold values from -3 to 3
- step_raw: float32 [8, 512, 40], P('grp', 'seq'), may hold values from -9 to 6
- rate_log: float32 [40], replicated, may hold values from -3 to 3.1
- skip_gain: float32 [40], replicated, may hold values from 0.5 to 1.5
- gate_input: bfloat16 [8, 512, 2560], P('grp', 'seq'), may hold values from -6 to 6
- norm_gain: float32 [2560], replicated, may hold values from 0.1 to 1.9
- out_weight: bfloat16 [2560, 2560], P('grp'), may hold values from -0.125 to 0.125
- residual: bfloat16 [8, 512, 2560], P('grp', 'seq'), may hold values from -6 to 6
- moe_gain: float32 [2560], replicated, may hold values from 0.1 to 1.9
- w_gate: bfloat16 [8, 2560, 512], P('grp'), may hold values from -0.125 to 0.125
- w_up: bfloat16 [8, 2560, 512], P('grp'), may hold values from -0.125 to 0.125
- w_down: bfloat16 [8, 512, 2560], P('grp'), may hold values from -0.25 to 0.25
- routes: int32 [8, 512, 2], P('grp', 'seq'), may hold values from 0 to 7, as said below
- route_weights: float32 [8, 512, 2], P('grp', 'seq'), may hold values from 0.2 to 1
Outputs:
- layer_out: bfloat16 [8, 512, 2560], P('grp', 'seq')
The draws below stay inside these ranges and needn't reach their ends.
Inputs may be any that keep to these rules, and one draw needn't show every extreme that they name: `routes`: within the rows of one device (each aligned block of 128 frames of one manuscript) no expert is named by more than 64 entries, and one expert, the same in every block, is named by exactly 64; the two entries of a frame differ.
All inputs are finite; a program needn't handle non-finite values.
Results may differ from the reference program's by a relative error of at most 0.012.
Values may be sent and summed in bfloat16 or wider, within the bound.
A program may use at most 128 MiB of HBM per device.

```python
import math
import jax
import jax.numpy as jnp
from jax import lax

D = 2560
HEADS = 40
HEAD_DIM = 64
STATE = 64
CONV = 4
FF = 512
TOK_DEV = 128
INNER = 2560
CHANNELS = 2688
FRAMES = 512
MSS = 8
EXPERTS = 8
MOST = 64


def draw_routes(key, part):
    hot_key = jax.random.fold_in(key, 11)
    hot_expert = jax.random.randint(hot_key, (), 0, EXPERTS)
    block_total = MSS * (FRAMES // TOK_DEV)
    block_keys = jax.random.split(jax.random.fold_in(key, 12), block_total)

    def one_block(block_key):
        order_key, shuffle_key = jax.random.split(block_key)
        order = jax.random.permutation(order_key, (EXPERTS - 1) * MOST)
        others = order[:2 * TOK_DEV - MOST] // MOST
        others = others + (others >= hot_expert).astype(others.dtype)
        labels = jnp.sort(jnp.concatenate([jnp.full((MOST,), hot_expert, jnp.int32), others.astype(jnp.int32)]))
        pairs = jnp.stack([labels[:TOK_DEV], labels[TOK_DEV:]], axis=1)
        shuffle = jax.random.permutation(shuffle_key, TOK_DEV)
        return pairs[shuffle]
    blocks = jax.vmap(one_block)(block_keys)
    return blocks.reshape(MSS, FRAMES, 2).astype(jnp.int32)


def draw_step_raw(key, part):
    noise_key, offset_key, place_key = jax.random.split(jax.random.fold_in(key, 21), 3)
    random_jitter = 0.5 * jnp.clip(jax.random.normal(noise_key, (MSS, FRAMES, HEADS), jnp.float32), -3.0, 3.0)
    shift_amounts = jax.random.uniform(offset_key, (MSS, FRAMES // TOK_DEV, 1, HEADS), jnp.float32, -0.7, 0.7)
    shift_amounts = jnp.broadcast_to(shift_amounts, (MSS, FRAMES // TOK_DEV, TOK_DEV, HEADS)).reshape(MSS, FRAMES, HEADS)
    destination_slots = jax.random.randint(place_key, (MSS, 3), 0, FRAMES)
    page_frame_index = jnp.arange(FRAMES)
    spike_mask = jnp.any(page_frame_index[None, :, None] == destination_slots[:, None, :], axis=2).astype(jnp.float32)
    return (-6.0 + random_jitter + shift_amounts + 9.0 * spike_mask[:, :, None]).astype(jnp.float32)


def draw_rate_log(key, part):
    pick_key, slow_key, fast_key = jax.random.split(jax.random.fold_in(key, 31), 3)
    fast_heads = jax.random.uniform(pick_key, (HEADS,), jnp.float32) < 0.5
    slow_rates = jax.random.uniform(slow_key, (HEADS,), jnp.float32, math.log(0.06), math.log(0.15))
    fast_rates = jax.random.uniform(fast_key, (HEADS,), jnp.float32, math.log(8.0), math.log(20.0))
    return jnp.where(fast_heads, fast_rates, slow_rates).astype(jnp.float32)


def block_scale(key, extent, cuts, smallest, top_value):
    gain, own = 1.0, jax.random.fold_in(key, 6)
    for axis_at, parts in cuts:
        heights = jnp.exp(jax.random.uniform(jax.random.fold_in(own, axis_at), (parts,), jnp.float32, smallest / len(cuts), top_value / len(cuts)))
        gain = gain * jnp.repeat(heights, extent[axis_at] // parts).reshape([-1 if axis == axis_at else 1 for axis in range(len(extent))])
    return gain


def bell_draw(key, shape, spread, most, cuts=(), held_as=jnp.bfloat16):
    values = spread * jax.random.normal(key, shape, jnp.float32)
    if cuts:
        values = values * block_scale(key, shape, cuts, -0.22, 0.18)
    return jnp.clip(values, -most, most).astype(held_as)


def setup_inputs(seed: int = 0) -> dict:
    splits = jax.random.split(jax.random.key(seed), 16)
    return {
        "conv_input": bell_draw(splits[0], (MSS, FRAMES, CHANNELS), 1.0, 6.0, ((0, 8), (1, 4))),
        "conv_weight": bell_draw(splits[1], (CONV, CHANNELS), CONV ** -0.5, 3.0, (), jnp.float32),
        "step_raw": draw_step_raw(jax.random.fold_in(splits[15], 71), 0),
        "rate_log": draw_rate_log(jax.random.fold_in(splits[15], 71), 0),
        "skip_gain": jnp.clip(jax.random.uniform(splits[4], (HEADS,), jnp.float32, 0.5, 1.5), 0.5, 1.5),
        "gate_input": bell_draw(splits[5], (MSS, FRAMES, INNER), 1.0, 6.0, ((0, 8), (1, 4))),
        "norm_gain": jnp.clip(1.0 + 0.18 * jax.random.normal(splits[6], (INNER,), jnp.float32), 0.1, 1.9),
        "out_weight": bell_draw(splits[7], (INNER, D), INNER ** -0.5, 0.125, ((0, 8),)),
        "residual": bell_draw(splits[8], (MSS, FRAMES, D), 1.0, 6.0, ((0, 8), (1, 4))),
        "moe_gain": jnp.clip(1.0 + 0.18 * jax.random.normal(splits[9], (D,), jnp.float32), 0.1, 1.9),
        "w_gate": bell_draw(splits[10], (EXPERTS, D, FF), D ** -0.5, 0.125, ((0, 8),)),
        "w_up": bell_draw(splits[11], (EXPERTS, D, FF), D ** -0.5, 0.125, ((0, 8),)),
        "w_down": bell_draw(splits[12], (EXPERTS, FF, D), FF ** -0.5, 0.25, ((0, 8),)),
        "routes": draw_routes(jax.random.fold_in(splits[15], 71), 0),
        "route_weights": jnp.clip(0.2 + 0.8 * jax.random.uniform(splits[14], (MSS, FRAMES, 2), jnp.float32) ** block_scale(splits[14], (MSS, FRAMES, 2), ((0, 8), (1, 4)), -0.2, 0.2), 0.2, 1.0),
    }


EPSILON = 1e-05

def reference(conv_input, conv_weight, step_raw, rate_log, skip_gain, gate_input, norm_gain, out_weight, residual, moe_gain, w_gate, w_up, w_down, routes, route_weights):
    highest = lax.Precision.HIGHEST
    block_count = FRAMES // TOK_DEV

    def ssd_block(ssm_state, pieces):
        x_block, b_block, c_block, step_block, log_block = pieces
        length = x_block.shape[0]
        cumulative = jnp.cumsum(log_block, axis=0)
        x_values = x_block.astype(jnp.float32).reshape(length, HEADS, HEAD_DIM)
        b_values = b_block.astype(jnp.float32)
        c_values = c_block.astype(jnp.float32)
        scores = jnp.dot(c_block, b_block.T, preferred_element_type=jnp.float32)
        positions = jnp.arange(length, dtype=jnp.int32)
        causal = positions[:, None] >= positions[None, :]
        by_head = cumulative.T
        gap_log = by_head[:, :, None] - by_head[:, None, :]
        decay_mask = jnp.where(causal[None], jnp.exp(jnp.where(causal[None], gap_log, jnp.float32(0.0))), jnp.float32(0.0))
        mixing = scores[None] * decay_mask * step_block.T[:, None, :]
        within = jnp.einsum('hts,shp->thp', mixing, x_values, precision=highest)
        carried = jnp.einsum('tn,hpn->thp', c_values, ssm_state, precision=highest) * jnp.exp(cumulative)[:, :, None]
        tail_weight = jnp.exp(cumulative[-1][None, :] - cumulative) * step_block
        local_state = jnp.einsum('shp,sn->hpn', x_values * tail_weight[:, :, None], b_values, precision=highest)
        new_state = jnp.exp(cumulative[-1])[:, None, None] * ssm_state + local_state
        block_out = within + carried + skip_gain[None, :, None] * x_values
        return (new_state, block_out.reshape(length, HEADS * HEAD_DIM))

    def mixer(pieces):
        frames_in, raw_steps, gate_rows, residual_rows = pieces
        padded = jnp.concatenate([jnp.zeros((CONV - 1, CHANNELS), jnp.float32), frames_in.astype(jnp.float32)], axis=0)
        summed = conv_weight[0][None, :] * padded[0:FRAMES]
        for offset in range(1, CONV):
            summed = summed + conv_weight[offset][None, :] * padded[offset:offset + FRAMES]
        signal = jax.nn.silu(summed).astype(jnp.bfloat16)
        x_part = signal[:, :INNER]
        b_part = signal[:, INNER:INNER + STATE]
        c_part = signal[:, INNER + STATE:]
        step_size = jax.nn.softplus(raw_steps)
        log_decay = -step_size * jnp.exp(rate_log)[None, :]
        blocks = (x_part.reshape(block_count, TOK_DEV, INNER), b_part.reshape(block_count, TOK_DEV, STATE), c_part.reshape(block_count, TOK_DEV, STATE), step_size.reshape(block_count, TOK_DEV, HEADS), log_decay.reshape(block_count, TOK_DEV, HEADS))
        start_state = jnp.zeros((HEADS, HEAD_DIM, STATE), jnp.float32)
        final_state, outputs = lax.scan(ssd_block, start_state, blocks)
        ssd_out = outputs.reshape(FRAMES, INNER)
        gated_out = ssd_out * jax.nn.silu(gate_rows.astype(jnp.float32))
        mean_square = lax.optimization_barrier(jnp.mean(gated_out * gated_out, axis=1, keepdims=True))
        normed = (gated_out * lax.rsqrt(mean_square + EPSILON) * norm_gain[None, :]).astype(jnp.bfloat16)
        projected = jnp.dot(normed, out_weight, preferred_element_type=jnp.float32)
        return (residual_rows.astype(jnp.float32) + projected).astype(jnp.bfloat16)
    mixed_out = lax.map(mixer, (conv_input, step_raw, gate_input, residual))
    total_rows = MSS * FRAMES
    mixed_flat = mixed_out.reshape(total_rows, D).astype(jnp.float32)
    mean_square = lax.optimization_barrier(jnp.mean(mixed_flat * mixed_flat, axis=1, keepdims=True))
    moe_in = (mixed_flat * lax.rsqrt(mean_square + EPSILON) * moe_gain[None, :]).astype(jnp.bfloat16)
    assigned = routes.reshape(-1).astype(jnp.int32)
    token_of = (jnp.arange(2 * total_rows, dtype=jnp.int32) // 2).astype(jnp.int32)
    weight_of = route_weights.reshape(-1)
    capacity = MOST * MSS * (FRAMES // TOK_DEV)

    def per_expert(running, expert):
        order = jnp.argsort((assigned != expert).astype(jnp.int32), stable=True)[:capacity].astype(jnp.int32)
        valid = assigned[order] == expert
        picked = token_of[order]
        incoming_rows = moe_in[picked]
        gate_part = jnp.dot(incoming_rows, w_gate[expert], preferred_element_type=jnp.float32)
        up_part = jnp.dot(incoming_rows, w_up[expert], preferred_element_type=jnp.float32)
        expert_hidden = (jax.nn.silu(gate_part) * up_part).astype(jnp.bfloat16)
        expert_out = jnp.dot(expert_hidden, w_down[expert], preferred_element_type=jnp.float32).astype(jnp.bfloat16)
        scale = jnp.where(valid, weight_of[order], jnp.float32(0.0))
        running = running.at[picked].add(scale[:, None] * expert_out.astype(jnp.float32))
        return (running, None)
    total, unused = lax.scan(per_expert, mixed_flat, jnp.arange(EXPERTS, dtype=jnp.int32))
    return total.astype(jnp.bfloat16).reshape(MSS, FRAMES, D)
```

```python
import functools

import jax
import jax.numpy as jnp
from jax import lax
from jax.experimental import pallas as pl
from jax.experimental.pallas import tpu as pltpu
from jax.sharding import PartitionSpec as P

EPSILON = 1e-05
LANES = 128
LINES = 4
MESH = pl.DeviceIdType.MESH


def layer_kernel(
    ring,
    experts,
    conv_hbm,
    taps_hbm,
    steps_hbm,
    rates_hbm,
    skip_ref,
    gate_hbm,
    norm_hbm,
    weight_hbm,
    residual_hbm,
    gain_hbm,
    expert_gate_hbm,
    expert_up_hbm,
    expert_down_hbm,
    routes_hbm,
    pair_hbm,
    out_ref,
    conv_ref,
    taps_ref,
    steps_ref,
    rates_ref,
    gate_ref,
    norm_ref,
    residual_ref,
    gain_ref,
    expert_gate,
    expert_up,
    expert_down,
    routes_ref,
    pair_ref,
    halo,
    padded,
    signal,
    base,
    scores_ref,
    c_ref,
    bt_ref,
    square,
    step_rows,
    cum_rows,
    cum_cols,
    tail_cols,
    reach_ref,
    totals,
    states,
    rows,
    weight,
    total,
    share_out,
    share_in,
    mixed_ref,
    moe_ref,
    send_pick,
    first_pick,
    second_pick,
    outgoing,
    arrived,
    result,
    returned,
    hub_rows,
    hub_pick,
    local_sem,
    halo_send,
    halo_recv,
    total_send,
    total_recv,
    near_state_send,
    far_state_send,
    state_recv,
    near_rows_send,
    far_rows_send,
    rows_recv,
    line_send,
    inner_send,
    weight_recv,
    share_send,
    share_recv,
    hub_send,
    hub_recv,
    out_send,
    out_recv,
    back_send,
    back_recv,
):
    half = jnp.bfloat16
    full = jnp.float32
    me = lax.axis_index("seq")
    mine = lax.axis_index("grp")
    chips = ring // 2
    chip, core = me // 2, lax.rem(me, 2)
    twin = chip * 2 + 1 - core
    inner = experts // LINES
    line, place = mine // inner, lax.rem(mine, inner)

    row_count, width = gate_ref.shape
    head_count = step_rows.shape[0]
    head_width = width // head_count
    per_tile = LANES // head_width
    state_width = states.shape[2]
    part = width // LINES
    tiles = part // LANES
    depth = weight.shape[0] // experts
    share = weight.shape[1]
    tap_count = taps_ref.shape[0]

    share_column = pl.multiple_of(me * share, LANES)
    locals_ = [
        pltpu.make_async_copy(source, target, local_sem.at[index])
        for index, (source, target) in enumerate(
            (
                (weight_hbm.at[:, pl.ds(share_column, share)], weight.at[pl.ds(mine * depth, depth)]),
                (steps_hbm, steps_ref),
                (rates_hbm, rates_ref),
                (conv_hbm, conv_ref),
                (taps_hbm, taps_ref),
                (routes_hbm, routes_ref),
                (pair_hbm, pair_ref),
                (gate_hbm, gate_ref),
                (norm_hbm, norm_ref),
                (residual_hbm, residual_ref),
                (gain_hbm, gain_ref),
                (expert_gate_hbm, expert_gate),
                (expert_up_hbm, expert_up),
                (expert_down_hbm, expert_down),
            )
        )
    ]
    for copy in locals_:
        copy.start()

    barrier = pltpu.get_barrier_semaphore()

    def greet(axis, own, count):
        def step(shift, carry):
            pl.semaphore_signal(
                barrier,
                inc=1,
                device_id={axis: lax.rem(own + shift, count)},
                device_id_type=MESH,
            )
            return carry

        lax.fori_loop(1, count, step, 0)

    greet("seq", me, ring)
    greet("grp", mine, experts)
    pl.semaphore_wait(barrier, ring - 1 + experts - 1)


    def far(step):
        return lax.rem(chip + step, chips) * 2 + core

    def source(slot):
        return lax.rem(chip + chips - slot // 2, chips) * 2 + lax.rem(me + slot, 2)

    def ring_copy(slots, sends, part_index, step, near):
        near_send, far_send, recv = sends
        return pltpu.make_async_remote_copy(
            src_ref=slots.at[part_index, 2 * step if near else 0],
            dst_ref=slots.at[part_index, 2 * step + 1 if near else 2 * step],
            send_sem=(near_send if near else far_send).at[part_index, step],
            recv_sem=recv.at[part_index, 2 * step + 1 if near else 2 * step],
            device_id={"seq": twin if near else far(step)},
            device_id_type=MESH,
        )

    state_copy = functools.partial(
        ring_copy, states, (near_state_send, far_state_send, state_recv)
    )
    rows_copy = functools.partial(ring_copy, rows, (near_rows_send, far_rows_send, rows_recv))

    def launch(copy, part_index):
        for step in range(1, chips):
            copy(part_index, step, False).start()
        copy(part_index, 0, True).start()

    def relay(copy, part_index):
        for step in range(1, chips):
            copy(part_index, step, False).wait_recv()
            copy(part_index, step, True).start()

    def drain_ring(copy):
        def body(part_index, carry):
            for step in range(1, chips):
                copy(part_index, step, False).wait_send()
            for step in range(chips):
                copy(part_index, step, True).wait_send()
            return carry

        lax.fori_loop(0, LINES, body, 0)

    def halo_copy(target):
        return pltpu.make_async_remote_copy(
            src_ref=conv_ref.at[pl.ds(row_count - 16, 16)],
            dst_ref=halo,
            send_sem=halo_send.at[0],
            recv_sem=halo_recv.at[0],
            device_id={"seq": target},
            device_id_type=MESH,
        )

    def total_copy(shift):
        return pltpu.make_async_remote_copy(
            src_ref=totals.at[me],
            dst_ref=totals.at[me],
            send_sem=total_send.at[shift],
            recv_sem=total_recv.at[me],
            device_id={"seq": lax.rem(me + shift, ring)},
            device_id_type=MESH,
        )

    def total_arrival(origin):
        return pltpu.make_async_remote_copy(
            src_ref=totals.at[origin],
            dst_ref=totals.at[origin],
            send_sem=total_send.at[0],
            recv_sem=total_recv.at[origin],
            device_id={"seq": twin},
            device_id_type=MESH,
        )

    def weight_rows(block):
        return weight.at[pl.ds(block * depth, depth)]

    def weight_copy(block, target, send_sem):
        return pltpu.make_async_remote_copy(
            src_ref=weight_rows(block),
            dst_ref=weight_rows(block),
            send_sem=send_sem,
            recv_sem=weight_recv.at[block],
            device_id={"grp": target},
            device_id_type=MESH,
        )

    def line_copy(at, up):
        step = 1 if up else -1
        return weight_copy(at * inner + place, mine + step * inner, line_send.at[at, 0 if up else 1])

    def inner_copy(at, shift):
        return weight_copy(
            at * inner + place,
            line * inner + lax.rem(place + shift, inner),
            inner_send.at[at, shift],
        )

    def each_weight_copy(do):
        def visit(at, carry):
            @pl.when((at <= line) & (line < LINES - 1))
            def _():
                do(line_copy(at, True))

            @pl.when((at >= line) & (line > 0))
            def _():
                do(line_copy(at, False))

            for shift in range(1, inner):
                do(inner_copy(at, shift))
            return carry

        return visit

    start_weight = each_weight_copy(lambda copy: copy.start())

    def relay_weight(step):
        for at in (line - step, line + step):

            @pl.when((at >= 0) & (at < LINES))
            def _():
                weight_copy(at * inner + place, mine, line_send.at[0, 0]).wait_recv()
                start_weight(at, 0)


    locals_[0].wait()
    start_weight(line, 0)
    locals_[3].wait()

    @pl.when(me < ring - 1)
    def _():
        halo_copy(me + 1).start()

    down = lax.broadcasted_iota(jnp.int32, (row_count, row_count), 0)
    across = lax.broadcasted_iota(jnp.int32, (row_count, row_count), 1)
    for index in (1, 2):
        locals_[index].wait()
    rate_square = jnp.where(
        down[:head_count, :head_count] == across[:head_count, :head_count], rates_ref[...], 0.0
    )
    rate = jnp.exp(jnp.sum(rate_square, axis=1, keepdims=True))
    raw = steps_ref[...]
    step_size = jnp.maximum(raw, 0.0) + jnp.log1p(jnp.exp(-jnp.abs(raw)))
    step_rows[...] = step_size
    log_decay = -step_size * rate
    cumulative = jnp.dot(
        log_decay,
        (down <= across).astype(full),
        preferred_element_type=full,
        precision=lax.Precision.HIGHEST,
    )
    cum_rows[...] = cumulative
    square[...] = jnp.zeros_like(square)
    square[:head_count, :] = cumulative
    cum_cols[...] = square[...].T
    totals[me] = jnp.broadcast_to(cum_cols[row_count - 1 : row_count, :], totals.shape[1:])
    square[:head_count, :] = jnp.exp(cumulative[:, row_count - 1 : row_count] - cumulative) * step_size
    tail_cols[...] = square[...].T
    for shift in range(1, ring):
        total_copy(shift).start()
    for index in (4, 5, 6):
        locals_[index].wait()

    capacity = outgoing.shape[1]
    names = lax.broadcasted_iota(jnp.int32, (experts, row_count), 0)
    members = [(names == routes_ref[k : k + 1, :]).astype(full) for k in range(2)]
    rank = jnp.dot(
        (members[0] + members[1]).astype(half),
        (down < across).astype(half),
        preferred_element_type=full,
    ) + (names * capacity).astype(full)
    targets = [jnp.sum(member * rank, axis=0, keepdims=True) for member in members]
    square[...] = jnp.zeros_like(square)
    for k in range(2):
        square[k : k + 1, :] = targets[k]
        square[2 + k : 3 + k, :] = pair_ref[k : k + 1, :]
    columns_of = square[...].T
    slot_lanes = lax.broadcasted_iota(jnp.int32, first_pick.shape, 1).astype(full)
    first_pick[...] = (columns_of[:, 0:1] == slot_lanes).astype(half)
    second_pick[...] = (columns_of[:, 1:2] == slot_lanes).astype(half)
    square[...] = columns_of
    slot_rows = lax.broadcasted_iota(jnp.int32, (capacity, row_count), 0)

    def pick(expert, carry):
        slot_of = (slot_rows + expert * capacity).astype(full)
        send_pick[expert] = (
            jnp.where(targets[0] == slot_of, 1.0, 0.0) + jnp.where(targets[1] == slot_of, 1.0, 0.0)
        ).astype(half)
        return carry

    lax.fori_loop(0, experts, pick, 0)

    @pl.when(me > 0)
    def _():
        halo_copy(me).wait_recv()

    first_half = lax.broadcasted_iota(jnp.int32, (row_count, LANES), 1) < head_width
    offset = 8

    def convolve(column):
        columns = pl.ds(column, LANES)
        before = halo[:, columns].astype(full)[16 - offset :]
        padded[:offset, :] = jnp.where(me > 0, before, 0.0)
        padded[offset:, :] = conv_ref[:, columns].astype(full)
        taps = taps_ref[:, columns]
        start = offset - tap_count + 1
        summed = taps[0:1] * padded[start : start + row_count, :]
        for k in range(1, tap_count):
            summed = summed + taps[k : k + 1] * padded[start + k : start + k + row_count, :]
        return (summed * jax.nn.sigmoid(summed)).astype(half)

    def by_head(columns_of_heads, pair):
        shifted = pltpu.roll(columns_of_heads, lax.rem(LANES - per_tile * pair, LANES), axis=1)
        return shifted[:, 0:1], shifted[:, 1:2]

    bc = convolve(width).astype(full)
    bt_ref[...] = bc.T[:state_width].astype(half)
    c_part = pltpu.roll(bc, LANES - state_width, axis=1)[:, :state_width].astype(half)
    c_ref[...] = c_part
    scores_ref[...] = jnp.dot(c_part, bt_ref[...], preferred_element_type=full)

    def take_in(part_index, carry):
        def tile(index, carry):
            pair = part_index * tiles + index
            column = pl.multiple_of(pair * LANES, LANES)
            x = convolve(column)
            signal[:, pl.ds(column, LANES)] = x
            left, right = by_head(tail_cols[...], pair)
            scaled = (x.astype(full) * jnp.where(first_half, left, right)).astype(half)
            states[part_index, 0, :, pl.ds(pl.multiple_of(index * LANES, LANES), LANES)] = jnp.dot(
                bt_ref[...], scaled, preferred_element_type=full
            ).astype(half)
            return carry

        lax.fori_loop(0, tiles, tile, 0)
        launch(state_copy, part_index)
        return carry

    lax.fori_loop(0, LINES, take_in, 0)

    def within(part_index, carry):
        def tile(index, carry):
            pair = part_index * tiles + index
            column = pl.multiple_of(pair * LANES, LANES)
            cum = by_head(cum_cols[...], pair)
            mixing = []
            for turn in range(2):
                head = per_tile * pair + turn
                gap = cum[turn] - cum_rows[pl.ds(head, 1), :]
                decay = jnp.exp(jnp.where(down >= across, gap, -1e30))
                mixing.append(scores_ref[...] * decay * step_rows[pl.ds(head, 1), :])
            x = signal[:, pl.ds(column, LANES)].astype(full)
            stacked = jnp.concatenate(
                [jnp.where(first_half, x, 0.0), jnp.where(first_half, 0.0, x)], axis=0
            ).astype(half)
            skip = jnp.where(first_half, skip_ref[per_tile * pair], skip_ref[per_tile * pair + 1])
            base[:, pl.ds(column, LANES)] = (
                jnp.dot(
                    jnp.concatenate(mixing, axis=1).astype(half), stacked, preferred_element_type=full
                )
                + skip * x
            )
            return carry

        lax.fori_loop(0, tiles, tile, 0)
        relay(state_copy, part_index)
        return carry

    lax.fori_loop(0, LINES, within, 0)
    relay_weight(1)

    for shift in range(1, ring):
        total_arrival(lax.rem(me + shift, ring)).wait_recv()
    for slot in range(1, ring):
        origin = source(slot)
        passed = jnp.zeros((1, LANES), full)
        for between in range(ring):
            passed = passed + jnp.where(
                (between > origin) & (between < me), totals[between, 0:1, :], 0.0
            )
        reach_ref[slot : slot + 1, :] = jnp.where(origin < me, jnp.exp(passed), 0.0)
    reach_ref[0:1, :] = jnp.zeros((1, LANES), full)
    for index in (7, 8):
        locals_[index].wait()

    def gather_in(part_index, squares):
        for step in range(chips):
            state_copy(part_index, step, True).wait_recv()

        def tile(index, squares):
            pair = part_index * tiles + index
            column = pl.multiple_of(pair * LANES, LANES)
            columns = pl.ds(column, LANES)
            local = pl.ds(pl.multiple_of(index * LANES, LANES), LANES)
            left, right = by_head(reach_ref[...], pair)
            reach = jnp.where(first_half[: reach_ref.shape[0]], left, right)
            entering = jnp.zeros((state_width, LANES), full)
            for slot in range(1, ring):
                entering = entering + reach[slot : slot + 1] * states[
                    part_index, slot, :, local
                ].astype(full)
            carried = jnp.dot(c_ref[...], entering.astype(half), preferred_element_type=full)
            left, right = by_head(cum_cols[...], pair)
            fade = jnp.exp(jnp.where(first_half, left, right))
            gate = gate_ref[:, columns].astype(full)
            value = (base[:, columns] + carried * fade) * (gate * jax.nn.sigmoid(gate))
            rows[part_index, 0, :, local] = (value * norm_ref[:, columns]).astype(half)
            return squares + jnp.sum(value * value, axis=1, keepdims=True)

        squares = lax.fori_loop(0, tiles, tile, squares)
        launch(rows_copy, part_index)
        return squares

    squares = lax.fori_loop(0, LINES, gather_in, jnp.zeros((row_count, 1), full))
    row_scale = lax.rsqrt(squares * (1.0 / width) + EPSILON)

    for part_index in range(LINES):
        relay(rows_copy, part_index)
        if 1 <= part_index < LINES - 2:
            relay_weight(part_index + 1)

    def rows_arrived(part_index, carry):
        for step in range(chips):
            rows_copy(part_index, step, True).wait_recv()
        return carry

    lax.fori_loop(0, LINES, rows_arrived, 0)
    relay_weight(LINES - 1)

    def project(index, carry):
        step = (index + 1) // 2
        at = line + jnp.where(lax.rem(index, 2) == 0, step, -step)

        @pl.when((at >= 0) & (at < LINES))
        def _():
            for shift in range(1, inner):
                weight_copy(
                    at * inner + lax.rem(place + shift, inner), mine, line_send.at[0, 0]
                ).wait_recv()
            product = jnp.dot(
                rows[at].reshape(ring * row_count, part),
                weight[pl.ds(pl.multiple_of(at * part, part), part), :],
                preferred_element_type=full,
            )
            total[...] = jnp.where(index == 0, 0.0, total[...]) + product

        return carry

    total[...] = jnp.zeros_like(total)
    lax.fori_loop(0, 2 * LINES - 1, project, 0)

    def share_copy(slot):
        return pltpu.make_async_remote_copy(
            src_ref=share_out.at[slot],
            dst_ref=share_in.at[me],
            send_sem=share_send.at[slot],
            recv_sem=share_recv.at[me],
            device_id={"seq": source(slot)},
            device_id_type=MESH,
        )

    def share_arrival(column):
        return pltpu.make_async_remote_copy(
            src_ref=share_out.at[0],
            dst_ref=share_in.at[column],
            send_sem=share_send.at[0],
            recv_sem=share_recv.at[column],
            device_id={"seq": source(1)},
            device_id_type=MESH,
        )

    def hand_out(index, carry):
        slot = ring - 1 - index
        share_out[slot] = total[pl.ds(pl.multiple_of(slot * row_count, row_count), row_count), :].astype(half)

        @pl.when(slot > 0)
        def _():
            share_copy(slot).start()

        return carry

    lax.fori_loop(0, ring, hand_out, 0)
    share_in[me] = share_out[0]
    for index in (9, 10):
        locals_[index].wait()

    def mix(index, squares):
        @pl.when(index != me)
        def _():
            share_arrival(index).wait_recv()

        column = pl.multiple_of(index * share, share)
        values = (
            residual_ref[:, pl.ds(column, share)].astype(full) + row_scale * share_in[index].astype(full)
        ).astype(half)
        mixed_ref[:, pl.ds(column, share)] = values
        wide = values.astype(full)
        return squares + jnp.sum(wide * wide, axis=1, keepdims=True)

    squares = lax.fori_loop(0, ring, mix, jnp.zeros((row_count, 1), full))
    scale = lax.rsqrt(squares * (1.0 / width) + EPSILON)
    moe_ref[...] = (mixed_ref[:, :width].astype(full) * scale * gain_ref[...]).astype(half)

    side = experts // 2
    hub = lax.rem(mine + side, experts)

    def out_copy(buffer, target, slot):
        return pltpu.make_async_remote_copy(
            src_ref=outgoing.at[buffer],
            dst_ref=arrived.at[slot],
            send_sem=out_send.at[buffer],
            recv_sem=out_recv.at[slot],
            device_id={"grp": target},
            device_id_type=pl.DeviceIdType.MESH,
        )

    hub_copies = [
        pltpu.make_async_remote_copy(
            src_ref=source_ref,
            dst_ref=target_ref,
            send_sem=hub_send.at[index],
            recv_sem=hub_recv.at[index],
            device_id={"grp": hub},
            device_id_type=pl.DeviceIdType.MESH,
        )
        for index, (source_ref, target_ref) in enumerate(
            (
                (moe_ref, hub_rows),
                (send_pick.at[pl.ds(hub // side * side, side)], hub_pick),
            )
        )
    ]

    def back_copy(target, slot):
        return pltpu.make_async_remote_copy(
            src_ref=result.at[target],
            dst_ref=returned.at[slot],
            send_sem=back_send.at[target],
            recv_sem=back_recv.at[slot],
            device_id={"grp": target},
            device_id_type=pl.DeviceIdType.MESH,
        )

    pairs = experts // 2
    other = lax.rem(mine + 1, experts)

    def partner(step):
        here = mine // 2
        if pairs & (pairs - 1):
            return lax.rem(here + step, pairs)
        place = 0
        bit = 1
        while bit < pairs:
            place = place + lax.rem(here // bit + step // bit, 2) * bit
            bit *= 2
        return place

    for copy in hub_copies:
        copy.start()

    def fill(low, picks, rows):
        outgoing[pl.ds(low, 2)] = (
            jnp.dot(
                picks.reshape(2 * capacity, moe_ref.shape[0]), rows, preferred_element_type=full
            )
            .astype(half)
            .reshape(2, capacity, width)
        )

    def dispatch(index, carry):
        low = partner(pairs // 2 - 1 - index) * 2
        fill(low, send_pick[pl.ds(low, 2)], moe_ref[...])
        for target in (low, low + 1):

            @pl.when(target != mine)
            def _():
                out_copy(target, target, mine).start()

        return carry

    def forward(index, carry):
        low = partner(pairs // 2 - 1 - index) * 2
        buffer = lax.rem(low + side, experts)
        fill(buffer, hub_pick[pl.ds(lax.rem(low, side), 2)], hub_rows[...])
        for turn in range(2):

            @pl.when(low + turn != mine)
            def _():
                out_copy(buffer + turn, low + turn, hub).start()

        return carry

    lax.fori_loop(0, pairs // 2, dispatch, 0)
    arrived[mine] = outgoing[mine]
    for copy in hub_copies:
        copy.wait_recv()
    lax.fori_loop(0, pairs // 2, forward, 0)
    arrived[hub] = outgoing[hub]
    for copy in locals_[11:]:
        copy.wait()

    def run_expert(step, carry):
        low = partner(step) * 2
        for origin in (low, low + 1):

            @pl.when((origin != mine) & (origin != hub))
            def _():
                out_copy(other, other, origin).wait_recv()

        rows = arrived[pl.ds(low, 2)].reshape(2 * capacity, width)
        gate_part = jnp.dot(rows, expert_gate[...], preferred_element_type=full)
        up_part = jnp.dot(rows, expert_up[...], preferred_element_type=full)
        hidden = (gate_part * jax.nn.sigmoid(gate_part) * up_part).astype(half)
        made = jnp.dot(hidden, expert_down[...], preferred_element_type=full).astype(half)
        result[pl.ds(low, 2)] = made.reshape(2, capacity, width)
        for origin in (low, low + 1):

            @pl.when(origin != mine)
            def _():
                back_copy(origin, mine).start()

        return carry

    lax.fori_loop(0, pairs, run_expert, 0)
    returned[mine] = result[mine]

    def take_back(slot, carry):
        @pl.when(slot != mine)
        def _():
            back_copy(other, slot).wait_recv()

        return carry

    lax.fori_loop(0, experts, take_back, 0)
    first_weight = square[:, 2:3]
    second_weight = square[:, 3:4]

    stretch = 512 if width % 512 == 0 else LANES

    def combine(tile, carry):
        column = pl.multiple_of(tile * stretch, stretch)
        rows = returned[:, :, pl.ds(column, stretch)].reshape(experts * capacity, stretch)
        first = jnp.dot(first_pick[...], rows, preferred_element_type=full)
        second = jnp.dot(second_pick[...], rows, preferred_element_type=full)
        out_ref[:, pl.ds(column, stretch)] = (
            mixed_ref[:, pl.ds(column, stretch)].astype(full)
            + first_weight * first
            + second_weight * second
        ).astype(half)
        return carry

    lax.fori_loop(0, width // stretch, combine, 0)

    def drain_seq(shift, carry):
        share_copy(shift).wait_send()
        return carry

    def drain_grp(target, carry):
        @pl.when(target != mine)
        def _():
            back_copy(target, mine).wait_send()

        @pl.when((target != mine) & (target != hub))
        def _():
            out_copy(target, other, mine).wait_send()

        return carry

    lax.fori_loop(1, ring, drain_seq, 0)
    lax.fori_loop(0, experts, drain_grp, 0)
    for copy in hub_copies:
        copy.wait_send()

    @pl.when(me < ring - 1)
    def _():
        halo_copy(me + 1).wait_send()

    for shift in range(1, ring):
        total_copy(shift).wait_send()
    drain_ring(state_copy)
    drain_ring(rows_copy)
    lax.fori_loop(0, LINES, each_weight_copy(lambda copy: copy.wait_send()), 0)


def on_device(
    conv_input,
    conv_weight,
    step_raw,
    rate_log,
    skip_gain,
    gate_input,
    norm_gain,
    out_weight,
    residual,
    moe_gain,
    w_gate,
    w_up,
    w_down,
    routes,
    route_weights,
):
    half = jnp.bfloat16
    full = jnp.float32
    ring = lax.axis_size("seq")
    experts = lax.axis_size("grp")
    share = -(-out_weight.shape[1] // (ring * LANES)) * LANES
    extra = ring * share - out_weight.shape[1]
    row_count, channel_count = conv_input.shape[1:]
    tap_count = conv_weight.shape[0]
    head_count = rate_log.shape[0]
    inner_width = gate_input.shape[2]
    state_width = (channel_count - inner_width) // 2
    model_width = residual.shape[2]
    hidden_width = w_gate.shape[2]
    capacity = 4 * row_count // experts
    part = inner_width // LINES
    padded_residual, padded_weight = residual[0], out_weight
    if extra:
        padded_residual = jnp.pad(padded_residual, ((0, 0), (0, extra)))
        padded_weight = jnp.pad(padded_weight, ((0, 0), (0, extra)))
    vmem = pl.BlockSpec(memory_space=pltpu.VMEM)
    smem = pl.BlockSpec(memory_space=pltpu.SMEM)
    anywhere = pl.BlockSpec(memory_space=pl.ANY)
    slab = pltpu.VMEM((experts, capacity, model_width), half)
    piece = pltpu.VMEM((ring, row_count, share), half)
    whole_rows = pltpu.VMEM((row_count, model_width), half)
    square = pltpu.VMEM((row_count, LANES), full)
    picks = pltpu.VMEM((row_count, experts * capacity), half)
    dma = pltpu.SemaphoreType.DMA
    layer_out = pl.pallas_call(
        functools.partial(layer_kernel, ring, experts),
        out_shape=jax.ShapeDtypeStruct((row_count, model_width), half),
        in_specs=[anywhere] * 4 + [smem] + [anywhere] * 10,
        out_specs=vmem,
        scratch_shapes=[
            pltpu.VMEM((row_count, channel_count), half),
            pltpu.VMEM((tap_count, channel_count), full),
            pltpu.VMEM((head_count, row_count), full),
            pltpu.VMEM((1, head_count), full),
            pltpu.VMEM((row_count, inner_width), half),
            pltpu.VMEM((1, inner_width), full),
            pltpu.VMEM((row_count, ring * share), half),
            pltpu.VMEM((1, model_width), full),
            pltpu.VMEM((model_width, hidden_width), half),
            pltpu.VMEM((model_width, hidden_width), half),
            pltpu.VMEM((hidden_width, model_width), half),
            pltpu.VMEM((2, row_count), jnp.int32),
            pltpu.VMEM((2, row_count), full),
            pltpu.VMEM((16, channel_count), half),
            pltpu.VMEM((row_count + 8, LANES), full),
            pltpu.VMEM((row_count, inner_width), half),
            pltpu.VMEM((row_count, inner_width), full),
            square,
            pltpu.VMEM((row_count, state_width), half),
            pltpu.VMEM((state_width, row_count), half),
            square,
            pltpu.VMEM((head_count, row_count), full),
            pltpu.VMEM((head_count, row_count), full),
            square,
            square,
            pltpu.VMEM((8, LANES), full),
            pltpu.VMEM((ring, 8, LANES), full),
            pltpu.VMEM((LINES, ring, state_width, part), half),
            pltpu.VMEM((LINES, ring, row_count, part), half),
            pltpu.VMEM((inner_width, share), half),
            pltpu.VMEM((ring * row_count, share), full),
            piece,
            piece,
            pltpu.VMEM((row_count, ring * share), half),
            whole_rows,
            pltpu.VMEM((experts, capacity, row_count), half),
            picks,
            picks,
            slab,
            slab,
            slab,
            slab,
            whole_rows,
            pltpu.VMEM((experts // 2, capacity, row_count), half),
            dma((14,)),
            dma((1,)),
            dma((1,)),
            dma((ring,)),
            dma((ring,)),
            dma((LINES, ring // 2)),
            dma((LINES, ring // 2)),
            dma((LINES, ring)),
            dma((LINES, ring // 2)),
            dma((LINES, ring // 2)),
            dma((LINES, ring)),
            dma((LINES, 2)),
            dma((LINES, experts // LINES)),
            dma((experts,)),
            dma((ring,)),
            dma((ring,)),
            dma((2,)),
            dma((2,)),
            dma((experts,)),
            dma((experts,)),
            dma((experts,)),
            dma((experts,)),
        ],
        compiler_params=pltpu.CompilerParams(
            collective_id=0, has_side_effects=True, vmem_limit_bytes=56 * 1024 * 1024
        ),
        cost_estimate=pl.CostEstimate(
            flops=6 * 1024 * 1024 * 1024, bytes_accessed=64 * 1024 * 1024, transcendentals=0
        ),
    )(
        conv_input[0],
        conv_weight,
        step_raw[0].T,
        rate_log[None, :],
        skip_gain,
        gate_input[0],
        norm_gain[None, :],
        padded_weight,
        padded_residual,
        moe_gain[None, :],
        w_gate[0],
        w_up[0],
        w_down[0],
        routes[0].T,
        route_weights[0].T,
    )
    return layer_out[None]


def solution(mesh):
    in_specs = (
        P("grp", "seq", None),
        P(),
        P("grp", "seq", None),
        P(),
        P(),
        P("grp", "seq", None),
        P(),
        P("grp", None),
        P("grp", "seq", None),
        P(),
        P("grp", None, None),
        P("grp", None, None),
        P("grp", None, None),
        P("grp", "seq", None),
        P("grp", "seq", None),
    )
    out_specs = P("grp", "seq", None)
    return jax.shard_map(
        on_device, mesh=mesh, in_specs=in_specs, out_specs=out_specs, check_vma=False
    )
```

```python
import functools

import jax
import jax.numpy as jnp
from jax import lax
from jax.experimental import pallas as pl
from jax.experimental.pallas import tpu as pltpu
from jax.sharding import PartitionSpec as P

EPSILON = 1e-05
LANES = 128
LINES = 4
MESH = pl.DeviceIdType.MESH


def layer_kernel(
    ring,
    experts,
    conv_hbm,
    taps_hbm,
    steps_hbm,
    rates_hbm,
    skip_ref,
    gate_hbm,
    norm_hbm,
    weight_hbm,
    residual_hbm,
    gain_hbm,
    expert_gate_hbm,
    expert_up_hbm,
    expert_down_hbm,
    routes_hbm,
    pair_hbm,
    out_ref,
    conv_ref,
    taps_ref,
    steps_ref,
    rates_ref,
    gate_ref,
    norm_ref,
    residual_ref,
    gain_ref,
    expert_gate,
    expert_up,
    expert_down,
    routes_ref,
    pair_ref,
    halo,
    padded,
    signal,
    base,
    scores_ref,
    c_ref,
    bt_ref,
    square,
    step_rows,
    cum_rows,
    cum_cols,
    tail_cols,
    reach_ref,
    totals,
    states,
    rows,
    weight,
    total,
    share_out,
    share_in,
    mixed_ref,
    plans,
    pick_rows,
    place_back,
    line_rows,
    outgoing,
    arrived,
    result,
    returned,
    sums_out,
    sums_in,
    sum_here,
    local_sem,
    halo_send,
    halo_recv,
    total_send,
    total_recv,
    near_state_send,
    far_state_send,
    state_recv,
    near_rows_send,
    far_rows_send,
    rows_recv,
    line_send,
    inner_send,
    weight_recv,
    share_send,
    share_recv,
    plan_send,
    plan_recv,
    row_send,
    row_recv,
    pick_send,
    pick_recv,
    made_send,
    made_recv,
    sum_send,
    sum_recv,
):
    half = jnp.bfloat16
    full = jnp.float32
    me = lax.axis_index("seq")
    mine = lax.axis_index("grp")
    chips = ring // 2
    chip, core = me // 2, lax.rem(me, 2)
    twin = chip * 2 + 1 - core
    inner = experts // LINES
    line, place = mine // inner, lax.rem(mine, inner)

    row_count, width = gate_ref.shape
    head_count = step_rows.shape[0]
    head_width = width // head_count
    per_tile = LANES // head_width
    state_width = states.shape[2]
    part = width // LINES
    tiles = part // LANES
    depth = weight.shape[0] // experts
    share = weight.shape[1]
    tap_count = taps_ref.shape[0]

    share_column = pl.multiple_of(me * share, LANES)
    locals_ = [
        pltpu.make_async_copy(source, target, local_sem.at[index])
        for index, (source, target) in enumerate(
            (
                (weight_hbm.at[:, pl.ds(share_column, share)], weight.at[pl.ds(mine * depth, depth)]),
                (steps_hbm, steps_ref),
                (rates_hbm, rates_ref),
                (conv_hbm, conv_ref),
                (taps_hbm, taps_ref),
                (routes_hbm, routes_ref),
                (pair_hbm, pair_ref),
                (gate_hbm, gate_ref),
                (norm_hbm, norm_ref),
                (residual_hbm, residual_ref),
                (gain_hbm, gain_ref),
                (expert_gate_hbm, expert_gate),
                (expert_up_hbm, expert_up),
                (expert_down_hbm, expert_down),
            )
        )
    ]
    for copy in locals_:
        copy.start()

    barrier = pltpu.get_barrier_semaphore()

    def greet(axis, own, count):
        def step(shift, carry):
            pl.semaphore_signal(
                barrier,
                inc=1,
                device_id={axis: lax.rem(own + shift, count)},
                device_id_type=MESH,
            )
            return carry

        lax.fori_loop(1, count, step, 0)

    greet("seq", me, ring)
    greet("grp", mine, experts)
    pl.semaphore_wait(barrier, ring - 1 + experts - 1)


    def far(step):
        return lax.rem(chip + step, chips) * 2 + core

    def source(slot):
        return lax.rem(chip + chips - slot // 2, chips) * 2 + lax.rem(me + slot, 2)

    def ring_copy(slots, sends, part_index, step, near):
        near_send, far_send, recv = sends
        return pltpu.make_async_remote_copy(
            src_ref=slots.at[part_index, 2 * step if near else 0],
            dst_ref=slots.at[part_index, 2 * step + 1 if near else 2 * step],
            send_sem=(near_send if near else far_send).at[part_index, step],
            recv_sem=recv.at[part_index, 2 * step + 1 if near else 2 * step],
            device_id={"seq": twin if near else far(step)},
            device_id_type=MESH,
        )

    state_copy = functools.partial(
        ring_copy, states, (near_state_send, far_state_send, state_recv)
    )
    rows_copy = functools.partial(ring_copy, rows, (near_rows_send, far_rows_send, rows_recv))

    def launch(copy, part_index):
        for step in range(1, chips):
            copy(part_index, step, False).start()
        copy(part_index, 0, True).start()

    def relay(copy, part_index):
        for step in range(1, chips):
            copy(part_index, step, False).wait_recv()
            copy(part_index, step, True).start()

    def drain_ring(copy):
        def body(part_index, carry):
            for step in range(1, chips):
                copy(part_index, step, False).wait_send()
            for step in range(chips):
                copy(part_index, step, True).wait_send()
            return carry

        lax.fori_loop(0, LINES, body, 0)

    def halo_copy(target):
        return pltpu.make_async_remote_copy(
            src_ref=conv_ref.at[pl.ds(row_count - 16, 16)],
            dst_ref=halo,
            send_sem=halo_send.at[0],
            recv_sem=halo_recv.at[0],
            device_id={"seq": target},
            device_id_type=MESH,
        )

    def total_copy(shift):
        return pltpu.make_async_remote_copy(
            src_ref=totals.at[me],
            dst_ref=totals.at[me],
            send_sem=total_send.at[shift],
            recv_sem=total_recv.at[me],
            device_id={"seq": lax.rem(me + shift, ring)},
            device_id_type=MESH,
        )

    def total_arrival(origin):
        return pltpu.make_async_remote_copy(
            src_ref=totals.at[origin],
            dst_ref=totals.at[origin],
            send_sem=total_send.at[0],
            recv_sem=total_recv.at[origin],
            device_id={"seq": twin},
            device_id_type=MESH,
        )

    def weight_rows(block):
        return weight.at[pl.ds(block * depth, depth)]

    def weight_copy(block, target, send_sem):
        return pltpu.make_async_remote_copy(
            src_ref=weight_rows(block),
            dst_ref=weight_rows(block),
            send_sem=send_sem,
            recv_sem=weight_recv.at[block],
            device_id={"grp": target},
            device_id_type=MESH,
        )

    def line_copy(at, up):
        step = 1 if up else -1
        return weight_copy(at * inner + place, mine + step * inner, line_send.at[at, 0 if up else 1])

    def inner_copy(at, shift):
        return weight_copy(
            at * inner + place,
            line * inner + lax.rem(place + shift, inner),
            inner_send.at[at, shift],
        )

    def each_weight_copy(do):
        def visit(at, carry):
            @pl.when((at <= line) & (line < LINES - 1))
            def _():
                do(line_copy(at, True))

            @pl.when((at >= line) & (line > 0))
            def _():
                do(line_copy(at, False))

            for shift in range(1, inner):
                do(inner_copy(at, shift))
            return carry

        return visit

    start_weight = each_weight_copy(lambda copy: copy.start())

    def relay_weight(step):
        for at in (line - step, line + step):

            @pl.when((at >= 0) & (at < LINES))
            def _():
                weight_copy(at * inner + place, mine, line_send.at[0, 0]).wait_recv()
                start_weight(at, 0)


    locals_[0].wait()
    start_weight(line, 0)
    locals_[3].wait()

    @pl.when(me < ring - 1)
    def _():
        halo_copy(me + 1).start()

    down = lax.broadcasted_iota(jnp.int32, (row_count, row_count), 0)
    across = lax.broadcasted_iota(jnp.int32, (row_count, row_count), 1)
    for index in (1, 2):
        locals_[index].wait()
    rate_square = jnp.where(
        down[:head_count, :head_count] == across[:head_count, :head_count], rates_ref[...], 0.0
    )
    rate = jnp.exp(jnp.sum(rate_square, axis=1, keepdims=True))
    raw = steps_ref[...]
    step_size = jnp.maximum(raw, 0.0) + jnp.log1p(jnp.exp(-jnp.abs(raw)))
    step_rows[...] = step_size
    log_decay = -step_size * rate
    cumulative = jnp.dot(
        log_decay,
        (down <= across).astype(full),
        preferred_element_type=full,
        precision=lax.Precision.HIGHEST,
    )
    cum_rows[...] = cumulative
    square[...] = jnp.zeros_like(square)
    square[:head_count, :] = cumulative
    cum_cols[...] = square[...].T
    totals[me] = jnp.broadcast_to(cum_cols[row_count - 1 : row_count, :], totals.shape[1:])
    square[:head_count, :] = jnp.exp(cumulative[:, row_count - 1 : row_count] - cumulative) * step_size
    tail_cols[...] = square[...].T
    for shift in range(1, ring):
        total_copy(shift).start()
    for index in (4, 5, 6):
        locals_[index].wait()

    capacity = 4 * row_count // experts
    names = lax.broadcasted_iota(jnp.int32, (experts, row_count), 0)
    members = [(names == routes_ref[k : k + 1, :]).astype(full) for k in range(2)]
    rank = jnp.dot(
        (members[0] + members[1]).astype(half),
        (down < across).astype(half),
        preferred_element_type=full,
    ) + (names * capacity).astype(full)
    plans[mine] = jnp.zeros_like(plans[mine])
    for k in range(2):
        plans[mine, k : k + 1, :] = jnp.sum(members[k] * rank, axis=0, keepdims=True)
        plans[mine, 2 + k : 3 + k, :] = pair_ref[k : k + 1, :]

    def plan_copy(shift):
        return pltpu.make_async_remote_copy(
            src_ref=plans.at[mine],
            dst_ref=plans.at[mine],
            send_sem=plan_send.at[shift],
            recv_sem=plan_recv.at[mine],
            device_id={"grp": lax.rem(mine + shift, experts)},
            device_id_type=MESH,
        )

    def plan_arrival(origin):
        return pltpu.make_async_remote_copy(
            src_ref=plans.at[origin],
            dst_ref=plans.at[origin],
            send_sem=plan_send.at[0],
            recv_sem=plan_recv.at[origin],
            device_id={"grp": lax.rem(mine + 1, experts)},
            device_id_type=MESH,
        )

    def send_plan(shift, carry):
        plan_copy(shift).start()
        return carry

    lax.fori_loop(1, experts, send_plan, 0)

    @pl.when(me > 0)
    def _():
        halo_copy(me).wait_recv()

    first_half = lax.broadcasted_iota(jnp.int32, (row_count, LANES), 1) < head_width
    offset = 8

    def convolve(column, padded):
        columns = pl.ds(column, LANES)
        before = halo[:, columns].astype(full)[16 - offset :]
        padded[:offset, :] = jnp.where(me > 0, before, 0.0)
        padded[offset:, :] = conv_ref[:, columns].astype(full)
        taps = taps_ref[:, columns]
        start = offset - tap_count + 1
        summed = taps[0:1] * padded[start : start + row_count, :]
        for k in range(1, tap_count):
            summed = summed + taps[k : k + 1] * padded[start + k : start + k + row_count, :]
        return (summed * jax.nn.sigmoid(summed)).astype(half)

    def by_head(columns_of_heads, pair):
        shifted = pltpu.roll(columns_of_heads, lax.rem(LANES - per_tile * pair, LANES), axis=1)
        return shifted[:, 0:1], shifted[:, 1:2]

    bc = convolve(width, padded.at[0]).astype(full)
    bt_ref[...] = bc.T[:state_width].astype(half)
    c_part = pltpu.roll(bc, LANES - state_width, axis=1)[:, :state_width].astype(half)
    c_ref[...] = c_part
    scores_ref[...] = jnp.dot(c_part, bt_ref[...], preferred_element_type=full)

    def take_in(part_index, carry):
        def tile(index, carry):
            pair = part_index * tiles + index
            column = pl.multiple_of(pair * LANES, LANES)
            x = convolve(column, padded.at[index])
            signal[:, pl.ds(column, LANES)] = x
            left, right = by_head(tail_cols[...], pair)
            scaled = (x.astype(full) * jnp.where(first_half, left, right)).astype(half)
            states[part_index, 0, :, pl.ds(pl.multiple_of(index * LANES, LANES), LANES)] = jnp.dot(
                bt_ref[...], scaled, preferred_element_type=full
            ).astype(half)
            return carry

        lax.fori_loop(0, tiles, tile, 0, unroll=True)
        launch(state_copy, part_index)
        return carry

    lax.fori_loop(0, LINES, take_in, 0)

    def within(part_index, carry):
        def tile(index, carry):
            pair = part_index * tiles + index
            column = pl.multiple_of(pair * LANES, LANES)
            cum = by_head(cum_cols[...], pair)
            mixing = []
            for turn in range(2):
                head = per_tile * pair + turn
                gap = cum[turn] - cum_rows[pl.ds(head, 1), :]
                decay = jnp.exp(jnp.where(down >= across, gap, -1e30))
                mixing.append(scores_ref[...] * decay * step_rows[pl.ds(head, 1), :])
            x = signal[:, pl.ds(column, LANES)].astype(full)
            stacked = jnp.concatenate(
                [jnp.where(first_half, x, 0.0), jnp.where(first_half, 0.0, x)], axis=0
            ).astype(half)
            skip = jnp.where(first_half, skip_ref[per_tile * pair], skip_ref[per_tile * pair + 1])
            base[:, pl.ds(column, LANES)] = (
                jnp.dot(
                    jnp.concatenate(mixing, axis=1).astype(half), stacked, preferred_element_type=full
                )
                + skip * x
            )
            return carry

        lax.fori_loop(0, tiles, tile, 0, unroll=True)
        relay(state_copy, part_index)
        return carry

    lax.fori_loop(0, LINES, within, 0)
    relay_weight(1)

    for shift in range(1, ring):
        total_arrival(lax.rem(me + shift, ring)).wait_recv()
    for slot in range(1, ring):
        origin = source(slot)
        passed = jnp.zeros((1, LANES), full)
        for between in range(ring):
            passed = passed + jnp.where(
                (between > origin) & (between < me), totals[between, 0:1, :], 0.0
            )
        reach_ref[slot : slot + 1, :] = jnp.where(origin < me, jnp.exp(passed), 0.0)
    reach_ref[0:1, :] = jnp.zeros((1, LANES), full)
    for index in (7, 8):
        locals_[index].wait()

    def gather_in(part_index, squares):
        for step in range(chips):
            state_copy(part_index, step, True).wait_recv()

        def tile(index, squares):
            pair = part_index * tiles + index
            column = pl.multiple_of(pair * LANES, LANES)
            columns = pl.ds(column, LANES)
            local = pl.ds(pl.multiple_of(index * LANES, LANES), LANES)
            left, right = by_head(reach_ref[...], pair)
            reach = jnp.where(first_half[: reach_ref.shape[0]], left, right)
            entering = jnp.zeros((state_width, LANES), full)
            for slot in range(1, ring):
                entering = entering + reach[slot : slot + 1] * states[
                    part_index, slot, :, local
                ].astype(full)
            carried = jnp.dot(c_ref[...], entering.astype(half), preferred_element_type=full)
            left, right = by_head(cum_cols[...], pair)
            fade = jnp.exp(jnp.where(first_half, left, right))
            gate = gate_ref[:, columns].astype(full)
            value = (base[:, columns] + carried * fade) * (gate * jax.nn.sigmoid(gate))
            rows[part_index, 0, :, local] = (value * norm_ref[pl.ds(pair, 1), :]).astype(half)
            return squares + jnp.sum(value * value, axis=1, keepdims=True)

        squares = lax.fori_loop(0, tiles, tile, squares, unroll=True)
        launch(rows_copy, part_index)
        return squares

    squares = lax.fori_loop(0, LINES, gather_in, jnp.zeros((row_count, 1), full))
    row_scale = lax.rsqrt(squares * (1.0 / width) + EPSILON)

    for part_index in range(LINES):
        relay(rows_copy, part_index)
        if 1 <= part_index < LINES - 2:
            relay_weight(part_index + 1)

    def rows_arrived(part_index, carry):
        for step in range(chips):
            rows_copy(part_index, step, True).wait_recv()
        return carry

    lax.fori_loop(0, LINES, rows_arrived, 0)
    relay_weight(LINES - 1)

    def project(index, carry):
        step = (index + 1) // 2
        at = line + jnp.where(lax.rem(index, 2) == 0, step, -step)

        @pl.when((at >= 0) & (at < LINES))
        def _():
            for shift in range(1, inner):
                weight_copy(
                    at * inner + lax.rem(place + shift, inner), mine, line_send.at[0, 0]
                ).wait_recv()
            product = jnp.dot(
                rows[at].reshape(ring * row_count, part),
                weight[pl.ds(pl.multiple_of(at * part, part), part), :],
                preferred_element_type=full,
            )
            total[...] = jnp.where(index == 0, 0.0, total[...]) + product

        return carry

    total[...] = jnp.zeros_like(total)
    lax.fori_loop(0, 2 * LINES - 1, project, 0)

    def share_copy(slot):
        return pltpu.make_async_remote_copy(
            src_ref=share_out.at[slot],
            dst_ref=share_in.at[me],
            send_sem=share_send.at[slot],
            recv_sem=share_recv.at[me],
            device_id={"seq": source(slot)},
            device_id_type=MESH,
        )

    def share_arrival(column):
        return pltpu.make_async_remote_copy(
            src_ref=share_out.at[0],
            dst_ref=share_in.at[column],
            send_sem=share_send.at[0],
            recv_sem=share_recv.at[column],
            device_id={"seq": source(1)},
            device_id_type=MESH,
        )

    def hand_out(index, carry):
        slot = ring - 1 - index
        share_out[slot] = total[pl.ds(pl.multiple_of(slot * row_count, row_count), row_count), :].astype(half)

        @pl.when(slot > 0)
        def _():
            share_copy(slot).start()

        return carry

    lax.fori_loop(0, ring, hand_out, 0)
    share_in[me] = share_out[0]
    for index in (9, 10):
        locals_[index].wait()

    def mix(index, squares):
        @pl.when(index != me)
        def _():
            share_arrival(index).wait_recv()

        column = pl.multiple_of(index * share, share)
        values = (
            residual_ref[:, pl.ds(column, share)].astype(full) + row_scale * share_in[index].astype(full)
        ).astype(half)
        mixed_ref[:, pl.ds(column, share)] = values
        wide = values.astype(full)
        return squares + jnp.sum(wide * wide, axis=1, keepdims=True)

    squares = lax.fori_loop(0, ring, mix, jnp.zeros((row_count, 1), full))
    scale = lax.rsqrt(squares * (1.0 / width) + EPSILON)
    for tile in range(width // LANES):
        local = tile % tiles * LANES
        line_rows[line, tile // tiles, :, local : local + LANES] = (
            mixed_ref[:, tile * LANES : (tile + 1) * LANES].astype(full)
            * scale
            * gain_ref[tile : tile + 1, :]
        ).astype(half)

    def row_copy(at, up, index):
        return pltpu.make_async_remote_copy(
            src_ref=line_rows.at[at, index],
            dst_ref=line_rows.at[at, index],
            send_sem=row_send.at[at, 0 if up else 1, index],
            recv_sem=row_recv.at[at, index],
            device_id={"grp": mine + (inner if up else -inner)},
            device_id_type=MESH,
        )

    def slots_of(owner):
        return pl.ds(pl.multiple_of(owner * capacity, capacity), capacity)

    def across_copy(source, target, sends, recvs, at, shift, index):
        other = lax.rem(place + shift, inner)
        return pltpu.make_async_remote_copy(
            src_ref=source.at[at, index, slots_of(other)],
            dst_ref=target.at[at, index, slots_of(place)],
            send_sem=sends.at[at, shift, index],
            recv_sem=recvs.at[at, place, index],
            device_id={"grp": line * inner + other},
            device_id_type=MESH,
        )

    def across_arrival(source, target, sends, recvs, at, shift, index):
        other = lax.rem(place + shift, inner)
        return pltpu.make_async_remote_copy(
            src_ref=source.at[at, index, slots_of(other)],
            dst_ref=target.at[at, index, slots_of(other)],
            send_sem=sends.at[at, shift, index],
            recv_sem=recvs.at[at, other, index],
            device_id={"grp": line * inner + other},
            device_id_type=MESH,
        )

    pick_parts = (outgoing, arrived, pick_send, pick_recv)
    made_parts = (result, returned, made_send, made_recv)

    def sum_copy(to, up, index):
        return pltpu.make_async_remote_copy(
            src_ref=sums_out.at[to, index],
            dst_ref=sums_in.at[0 if up else 1, to, index],
            send_sem=sum_send.at[to, index],
            recv_sem=sum_recv.at[0 if up else 1, to, index],
            device_id={"grp": mine + (inner if up else -inner)},
            device_id_type=MESH,
        )

    def sum_arrival(to, up, index):
        return pltpu.make_async_remote_copy(
            src_ref=sums_out.at[to, index],
            dst_ref=sums_in.at[0 if up else 1, to, index],
            send_sem=sum_send.at[to, index],
            recv_sem=sum_recv.at[0 if up else 1, to, index],
            device_id={"grp": mine},
            device_id_type=MESH,
        )

    def take_plan(shift, carry):
        plan_arrival(lax.rem(mine + shift, experts)).wait_recv()
        return carry

    lax.fori_loop(1, experts, take_plan, 0)
    slot_count = inner * capacity
    slot_ids = lax.broadcasted_iota(jnp.int32, (slot_count, row_count), 0)

    def forward(at, up, index):
        @pl.when((at <= line) & (line < LINES - 1) if up else (at >= line) & (line > 0))
        def _():
            row_copy(at, up, index).start()

    def plan_rows(at):
        plan = plans[at * inner + place]
        slot_of = (slot_ids + line * slot_count).astype(full)
        picks = jnp.where(plan[0:1] == slot_of, 1.0, 0.0) + jnp.where(plan[1:2] == slot_of, 1.0, 0.0)
        place_back[at] = picks.T.astype(half)
        pick_rows[at] = picks.astype(half)

    def take_piece(at, step, index):
        @pl.when(step > 0)
        def _():
            row_copy(at, True, index).wait_recv()

        forward(at, True, index)
        forward(at, False, index)
        outgoing[at, index] = jnp.dot(
            pick_rows[at], line_rows[at, index], preferred_element_type=full
        ).astype(half)
        for shift in range(1, inner):
            across_copy(*pick_parts, at, shift, index).start()
        arrived[at, index, slots_of(place)] = outgoing[at, index, slots_of(place)]

    def run_expert(at, step):
        scales = []
        own_ids = lax.broadcasted_iota(jnp.int32, (capacity, row_count), 0) + mine * capacity
        for origin in range(inner):
            plan = plans[at * inner + origin]
            own_slots = own_ids.astype(full)
            scales.append(
                jnp.sum(
                    jnp.where(plan[0:1] == own_slots, plan[2:3], 0.0)
                    + jnp.where(plan[1:2] == own_slots, plan[3:4], 0.0),
                    axis=1,
                    keepdims=True,
                )
            )
        scale = jnp.concatenate(scales, axis=0)
        gate_part = jnp.zeros((slot_count, expert_gate.shape[1]), full)
        up_part = gate_part
        for index in range(LINES):
            for shift in range(1, inner):
                across_arrival(*pick_parts, at, shift, index).wait_recv()
            rows_here = arrived[at, index]
            depth_here = slice(index * part, (index + 1) * part)
            gate_part = gate_part + jnp.dot(
                rows_here, expert_gate[depth_here, :], preferred_element_type=full
            )
            up_part = up_part + jnp.dot(
                rows_here, expert_up[depth_here, :], preferred_element_type=full
            )
        hidden = (gate_part * jax.nn.sigmoid(gate_part) * up_part).astype(half)
        for index in range(LINES):
            made = jnp.dot(
                hidden, expert_down[:, index * part : (index + 1) * part], preferred_element_type=full
            )
            result[at, index] = (made * scale).astype(half)
            for shift in range(1, inner):
                if index > 0:

                    @pl.when(step == LINES - 1)
                    def _():
                        across_copy(*made_parts, at, shift, index - 1).wait_send()

                across_copy(*made_parts, at, shift, index).start()
            returned[at, index, slots_of(place)] = result[at, index, slots_of(place)]

    def share_of(to, index):
        for shift in range(1, inner):
            across_arrival(*made_parts, to, shift, index).wait_recv()
        return jnp.dot(place_back[to], returned[to, index], preferred_element_type=full)

    def send_sums(to, up, index):
        behind = (line > 0) if up else (line < LINES - 1)
        sums_out[to, index] = share_of(to, index).astype(half)

        @pl.when(behind)
        def _():
            sum_arrival(to, up, index).wait_recv()
            sums_out[to, index] = (
                sums_out[to, index].astype(full) + sums_in[0 if up else 1, to, index].astype(full)
            ).astype(half)

        @pl.when((to == (LINES - 1 if up else 0)) & (index > 0))
        def _():
            sum_copy(to, up, index - 1).wait_send()

        sum_copy(to, up, index).start()

    def plan_block(at, carry):
        plan_rows(at)
        return carry

    lax.fori_loop(0, LINES, plan_block, 0)

    def round_trip(step, carry):
        def take(index, carry):
            for at, wanted in ((line - step, True), (line + step, step > 0)):

                @pl.when((at >= 0) & (at < LINES) & wanted)
                def _():
                    take_piece(at, step, index)

            return carry

        lax.fori_loop(0, LINES, take, 0)

        @pl.when(step == 0)
        def _():
            for copy in locals_[11:]:
                copy.wait()

        def turn(way, carry):
            at = line + jnp.where(way == 0, -step, step)

            @pl.when((at >= 0) & (at < LINES) & ((way == 0) | (step > 0)))
            def _():
                run_expert(at, step)

            return carry

        lax.fori_loop(0, 2, turn, 0)

        lag = jnp.where(line >= LINES // 2, 0, 1)

        def pass_on(index, carry):
            down_index, up_index = index - lag, index - 1 + lag

            @pl.when((step > 0) & (LINES - 1 - step < line) & (down_index >= 0) & (down_index < LINES))
            def _():
                send_sums(LINES - 1 - step, False, down_index)

            @pl.when((step > 0) & (step > line) & (up_index >= 0) & (up_index < LINES))
            def _():
                send_sums(step, True, up_index)

            return carry

        lax.fori_loop(0, LINES + 1, pass_on, 0)
        return carry

    lax.fori_loop(0, LINES, round_trip, 0)

    for index in range(LINES):
        columns = slice(index * part, (index + 1) * part)
        made_here = mixed_ref[:, columns].astype(full) + share_of(line, index)
        sum_here[...] = made_here

        @pl.when(line > 0)
        def _():
            sum_arrival(line, True, index).wait_recv()
            sum_here[...] += sums_in[0, line, index].astype(full)

        @pl.when(line < LINES - 1)
        def _():
            sum_arrival(line, False, index).wait_recv()
            sum_here[...] += sums_in[1, line, index].astype(full)

        out_ref[:, columns] = sum_here[...].astype(half)

    @pl.when(me < ring - 1)
    def _():
        halo_copy(me + 1).wait_send()

    for shift in range(1, ring):
        total_copy(shift).wait_send()
        share_copy(shift).wait_send()

    def sent_plan(shift, carry):
        plan_copy(shift).wait_send()
        return carry

    lax.fori_loop(1, experts, sent_plan, 0)
    drain_ring(state_copy)
    drain_ring(rows_copy)
    lax.fori_loop(0, LINES, each_weight_copy(lambda copy: copy.wait_send()), 0)

    def drain(at, carry):
        distance = jnp.maximum(at - line, line - at)
        last_sum = ((at == 0) & (line > 0)) | ((at == LINES - 1) & (line < LINES - 1))

        def piece(index, carry):
            @pl.when((at <= line) & (line < LINES - 1))
            def _():
                row_copy(at, True, index).wait_send()

            @pl.when((at >= line) & (line > 0))
            def _():
                row_copy(at, False, index).wait_send()

            for shift in range(1, inner):
                across_copy(*pick_parts, at, shift, index).wait_send()

                @pl.when((distance < LINES - 1) | (index == LINES - 1))
                def _():
                    across_copy(*made_parts, at, shift, index).wait_send()

            @pl.when((at != line) & (jnp.logical_not(last_sum) | (index == LINES - 1)))
            def _():
                sum_copy(at, True, index).wait_send()

            return carry

        lax.fori_loop(0, LINES, piece, 0)
        return carry

    lax.fori_loop(0, LINES, drain, 0)


def on_device(
    conv_input,
    conv_weight,
    step_raw,
    rate_log,
    skip_gain,
    gate_input,
    norm_gain,
    out_weight,
    residual,
    moe_gain,
    w_gate,
    w_up,
    w_down,
    routes,
    route_weights,
):
    half = jnp.bfloat16
    full = jnp.float32
    ring = lax.axis_size("seq")
    experts = lax.axis_size("grp")
    share = -(-out_weight.shape[1] // (ring * LANES)) * LANES
    extra = ring * share - out_weight.shape[1]
    row_count, channel_count = conv_input.shape[1:]
    tap_count = conv_weight.shape[0]
    head_count = rate_log.shape[0]
    inner_width = gate_input.shape[2]
    state_width = (channel_count - inner_width) // 2
    model_width = residual.shape[2]
    hidden_width = w_gate.shape[2]
    capacity = 4 * row_count // experts
    part = inner_width // LINES
    padded_residual, padded_weight = residual[0], out_weight
    if extra:
        padded_residual = jnp.pad(padded_residual, ((0, 0), (0, extra)))
        padded_weight = jnp.pad(padded_weight, ((0, 0), (0, extra)))
    vmem = pl.BlockSpec(memory_space=pltpu.VMEM)
    smem = pl.BlockSpec(memory_space=pltpu.SMEM)
    anywhere = pl.BlockSpec(memory_space=pl.ANY)
    inner = experts // LINES
    slot_count = inner * capacity
    row_slab = pltpu.VMEM((LINES, LINES, row_count, part), half)
    slot_slab = pltpu.VMEM((LINES, LINES, slot_count, part), half)
    piece = pltpu.VMEM((ring, row_count, share), half)
    square = pltpu.VMEM((row_count, LANES), full)
    dma = pltpu.SemaphoreType.DMA
    layer_out = pl.pallas_call(
        functools.partial(layer_kernel, ring, experts),
        out_shape=jax.ShapeDtypeStruct((row_count, model_width), half),
        in_specs=[anywhere] * 4 + [smem] + [anywhere] * 10,
        out_specs=vmem,
        scratch_shapes=[
            pltpu.VMEM((row_count, channel_count), half),
            pltpu.VMEM((tap_count, channel_count), full),
            pltpu.VMEM((head_count, row_count), full),
            pltpu.VMEM((1, head_count), full),
            pltpu.VMEM((row_count, inner_width), half),
            pltpu.VMEM((inner_width // LANES, LANES), full),
            pltpu.VMEM((row_count, ring * share), half),
            pltpu.VMEM((model_width // LANES, LANES), full),
            pltpu.VMEM((model_width, hidden_width), half),
            pltpu.VMEM((model_width, hidden_width), half),
            pltpu.VMEM((hidden_width, model_width), half),
            pltpu.VMEM((2, row_count), jnp.int32),
            pltpu.VMEM((2, row_count), full),
            pltpu.VMEM((16, channel_count), half),
            pltpu.VMEM((part // LANES, row_count + 8, LANES), full),
            pltpu.VMEM((row_count, inner_width), half),
            pltpu.VMEM((row_count, inner_width), full),
            square,
            pltpu.VMEM((row_count, state_width), half),
            pltpu.VMEM((state_width, row_count), half),
            square,
            pltpu.VMEM((head_count, row_count), full),
            pltpu.VMEM((head_count, row_count), full),
            square,
            square,
            pltpu.VMEM((8, LANES), full),
            pltpu.VMEM((ring, 8, LANES), full),
            pltpu.VMEM((LINES, ring, state_width, part), half),
            pltpu.VMEM((LINES, ring, row_count, part), half),
            pltpu.VMEM((inner_width, share), half),
            pltpu.VMEM((ring * row_count, share), full),
            piece,
            piece,
            pltpu.VMEM((row_count, ring * share), half),
            pltpu.VMEM((experts, 8, row_count), full),
            pltpu.VMEM((LINES, slot_count, row_count), half),
            pltpu.VMEM((LINES, row_count, slot_count), half),
            row_slab,
            slot_slab,
            slot_slab,
            slot_slab,
            slot_slab,
            row_slab,
            pltpu.VMEM((2, LINES, LINES, row_count, part), half),
            pltpu.VMEM((row_count, part), full),
            dma((14,)),
            dma((1,)),
            dma((1,)),
            dma((ring,)),
            dma((ring,)),
            dma((LINES, ring // 2)),
            dma((LINES, ring // 2)),
            dma((LINES, ring)),
            dma((LINES, ring // 2)),
            dma((LINES, ring // 2)),
            dma((LINES, ring)),
            dma((LINES, 2)),
            dma((LINES, experts // LINES)),
            dma((experts,)),
            dma((ring,)),
            dma((ring,)),
            dma((experts,)),
            dma((experts,)),
            dma((LINES, 2, LINES)),
            dma((LINES, LINES)),
            dma((LINES, inner, LINES)),
            dma((LINES, inner, LINES)),
            dma((LINES, inner, LINES)),
            dma((LINES, inner, LINES)),
            dma((LINES, LINES)),
            dma((2, LINES, LINES)),
        ],
        compiler_params=pltpu.CompilerParams(
            collective_id=0, has_side_effects=True, vmem_limit_bytes=48 * 1024 * 1024
        ),
        cost_estimate=pl.CostEstimate(
            flops=6 * 1024 * 1024 * 1024, bytes_accessed=64 * 1024 * 1024, transcendentals=0
        ),
    )(
        conv_input[0],
        conv_weight,
        step_raw[0].T,
        rate_log[None, :],
        skip_gain,
        gate_input[0],
        norm_gain.reshape(-1, LANES),
        padded_weight,
        padded_residual,
        moe_gain.reshape(-1, LANES),
        w_gate[0],
        w_up[0],
        w_down[0],
        routes[0].T,
        route_weights[0].T,
    )
    return layer_out[None]


def solution(mesh):
    in_specs = (
        P("grp", "seq", None),
        P(),
        P("grp", "seq", None),
        P(),
        P(),
        P("grp", "seq", None),
        P(),
        P("grp", None),
        P("grp", "seq", None),
        P(),
        P("grp", None, None),
        P("grp", None, None),
        P("grp", None, None),
        P("grp", "seq", None),
        P("grp", "seq", None),
    )
    out_specs = P("grp", "seq", None)
    return jax.shard_map(
        on_device, mesh=mesh, in_specs=in_specs, out_specs=out_specs, check_vma=False
    )
```

```python
import functools

import jax
import jax.numpy as jnp
from jax import lax
from jax.experimental import pallas as pl
from jax.experimental.pallas import tpu as pltpu
from jax.sharding import PartitionSpec as P

EPSILON = 1e-05
LANES = 128
LINES = 4
SPLIT = 1
STAGES = 2
MESH = pl.DeviceIdType.MESH


def column_groups(share):
    tiles = share // LANES
    first = max(1, (tiles * 4) // 5)
    return [first * LANES, (tiles - first) * LANES]


def layer_kernel(
    ring,
    experts,
    conv_hbm,
    taps_hbm,
    steps_hbm,
    rates_hbm,
    skip_ref,
    gate_hbm,
    norm_hbm,
    weight_hbm,
    residual_hbm,
    gain_hbm,
    expert_gate_hbm,
    expert_up_hbm,
    expert_down_hbm,
    routes_hbm,
    pair_hbm,
    out_ref,
    conv_ref,
    taps_ref,
    steps_ref,
    rates_ref,
    gate_ref,
    norm_ref,
    residual_ref,
    gain_ref,
    expert_gate,
    expert_up,
    expert_down,
    routes_ref,
    pair_ref,
    halo,
    padded,
    signal,
    base,
    scores_ref,
    c_ref,
    bt_ref,
    square,
    step_rows,
    cum_rows,
    cum_cols,
    tail_cols,
    reach_ref,
    totals,
    states,
    rows,
    weight_first,
    weight_second,
    total,
    share_out_first,
    share_out_second,
    share_in_first,
    share_in_second,
    mixed_ref,
    plans,
    pick_rows,
    place_back,
    line_rows,
    outgoing,
    arrived,
    result,
    returned,
    sums_out,
    sums_in,
    sum_here,
    local_sem,
    halo_send,
    halo_recv,
    total_send,
    total_recv,
    near_state_send,
    far_state_send,
    state_recv,
    near_rows_send,
    far_rows_send,
    rows_recv,
    line_send,
    inner_send,
    weight_recv,
    share_send,
    share_recv,
    plan_send,
    plan_recv,
    row_send,
    row_recv,
    pick_send,
    pick_recv,
    made_send,
    made_recv,
    sum_send,
    sum_recv,
):
    half = jnp.bfloat16
    full = jnp.float32
    me = lax.axis_index("seq")
    mine = lax.axis_index("grp")
    chips = ring // 2
    chip, core = me // 2, lax.rem(me, 2)
    twin = chip * 2 + 1 - core
    inner = experts // LINES
    line, place = mine // inner, lax.rem(mine, inner)

    row_count, width = gate_ref.shape
    head_count = step_rows.shape[0]
    head_width = width // head_count
    per_tile = LANES // head_width
    state_width = states.shape[2]
    part = width // LINES
    tiles = part // LANES
    weights = (weight_first, weight_second)
    shares_out = (share_out_first, share_out_second)
    shares_in = (share_in_first, share_in_second)
    depth = weight_first.shape[0] // experts
    share = total.shape[1]
    tap_count = taps_ref.shape[0]

    share_column = pl.multiple_of(me * share, LANES)
    locals_ = [
        pltpu.make_async_copy(source, target, local_sem.at[index])
        for index, (source, target) in enumerate(
            (
                *(
                    (
                        weight_hbm.at[:, pl.ds(share_column + start, ref.shape[1])],
                        ref.at[pl.ds(mine * depth, depth)],
                    )
                    for start, ref in zip((0, weight_first.shape[1]), weights)
                ),
                (steps_hbm, steps_ref),
                (rates_hbm, rates_ref),
                (conv_hbm, conv_ref),
                (taps_hbm, taps_ref),
                (routes_hbm, routes_ref),
                (pair_hbm, pair_ref),
                (gate_hbm, gate_ref),
                (norm_hbm, norm_ref),
                (residual_hbm, residual_ref),
                (gain_hbm, gain_ref),
                (expert_gate_hbm, expert_gate),
                (expert_up_hbm, expert_up),
                (expert_down_hbm, expert_down),
            )
        )
    ]
    for copy in locals_:
        copy.start()

    barrier = pltpu.get_barrier_semaphore()

    def greet(axis, own, count):
        def step(shift, carry):
            pl.semaphore_signal(
                barrier,
                inc=1,
                device_id={axis: lax.rem(own + shift, count)},
                device_id_type=MESH,
            )
            return carry

        lax.fori_loop(1, count, step, 0)

    greet("seq", me, ring)
    greet("grp", mine, experts)
    pl.semaphore_wait(barrier, ring - 1 + experts - 1)


    def far(step):
        return lax.rem(chip + step, chips) * 2 + core

    def source(slot):
        return lax.rem(chip + chips - slot // 2, chips) * 2 + lax.rem(me + slot, 2)

    def ring_copy(slots, sends, part_index, step, near):
        near_send, far_send, recv = sends
        return pltpu.make_async_remote_copy(
            src_ref=slots.at[part_index, 2 * step if near else 0],
            dst_ref=slots.at[part_index, 2 * step + 1 if near else 2 * step],
            send_sem=(near_send if near else far_send).at[part_index, step],
            recv_sem=recv.at[part_index, 2 * step + 1 if near else 2 * step],
            device_id={"seq": twin if near else far(step)},
            device_id_type=MESH,
        )

    state_copy = functools.partial(
        ring_copy, states, (near_state_send, far_state_send, state_recv)
    )
    rows_copy = functools.partial(ring_copy, rows, (near_rows_send, far_rows_send, rows_recv))

    def launch(copy, part_index):
        for step in range(1, chips):
            copy(part_index, step, False).start()
        copy(part_index, 0, True).start()

    def relay(copy, part_index):
        for step in range(1, chips):
            copy(part_index, step, False).wait_recv()
            copy(part_index, step, True).start()

    def drain_ring(copy):
        def body(part_index, carry):
            for step in range(1, chips):
                copy(part_index, step, False).wait_send()
            for step in range(chips):
                copy(part_index, step, True).wait_send()
            return carry

        lax.fori_loop(0, LINES, body, 0)

    def halo_copy(target):
        return pltpu.make_async_remote_copy(
            src_ref=conv_ref.at[pl.ds(row_count - 16, 16)],
            dst_ref=halo,
            send_sem=halo_send.at[0],
            recv_sem=halo_recv.at[0],
            device_id={"seq": target},
            device_id_type=MESH,
        )

    def total_copy(shift):
        return pltpu.make_async_remote_copy(
            src_ref=totals.at[me],
            dst_ref=totals.at[me],
            send_sem=total_send.at[shift],
            recv_sem=total_recv.at[me],
            device_id={"seq": lax.rem(me + shift, ring)},
            device_id_type=MESH,
        )

    def total_arrival(origin):
        return pltpu.make_async_remote_copy(
            src_ref=totals.at[origin],
            dst_ref=totals.at[origin],
            send_sem=total_send.at[0],
            recv_sem=total_recv.at[origin],
            device_id={"seq": twin},
            device_id_type=MESH,
        )

    def weight_copy(stage, block, target, send_sem):
        block_rows = weights[stage].at[pl.ds(block * depth, depth)]
        return pltpu.make_async_remote_copy(
            src_ref=block_rows,
            dst_ref=block_rows,
            send_sem=send_sem,
            recv_sem=weight_recv.at[stage, block],
            device_id={"grp": target},
            device_id_type=MESH,
        )

    def line_copy(stage, at, up):
        step = 1 if up else -1
        return weight_copy(
            stage,
            at * inner + place,
            mine + step * inner,
            line_send.at[stage, at, 0 if up else 1],
        )

    def inner_copy(stage, at, shift):
        return weight_copy(
            stage,
            at * inner + place,
            line * inner + lax.rem(place + shift, inner),
            inner_send.at[stage, at, shift],
        )

    def weight_arrival(stage, block):
        return weight_copy(stage, block, mine, line_send.at[stage, 0, 0])

    def each_weight_copy(do):
        def visit(stage, at):
            @pl.when((at <= line) & (line < LINES - 1))
            def _():
                do(line_copy(stage, at, True))

            @pl.when((at >= line) & (line > 0))
            def _():
                do(line_copy(stage, at, False))

            for shift in range(1, inner):
                do(inner_copy(stage, at, shift))

        return visit

    start_weight = each_weight_copy(lambda copy: copy.start())
    drain_weight = each_weight_copy(lambda copy: copy.wait_send())

    def relay_weight(stage, step):
        for at in (line - step, line + step):

            @pl.when((at >= 0) & (at < LINES))
            def _():
                weight_arrival(stage, at * inner + place).wait_recv()
                start_weight(stage, at)


    for index in (0, 1, 4):
        locals_[index].wait()
    start_weight(0, line)

    @pl.when(me < ring - 1)
    def _():
        halo_copy(me + 1).start()

    down = lax.broadcasted_iota(jnp.int32, (row_count, row_count), 0)
    across = lax.broadcasted_iota(jnp.int32, (row_count, row_count), 1)
    for index in (2, 3):
        locals_[index].wait()
    rate_square = jnp.where(
        down[:head_count, :head_count] == across[:head_count, :head_count], rates_ref[...], 0.0
    )
    rate = jnp.exp(jnp.sum(rate_square, axis=1, keepdims=True))
    raw = steps_ref[...]
    step_size = jnp.maximum(raw, 0.0) + jnp.log1p(jnp.exp(-jnp.abs(raw)))
    step_rows[...] = step_size
    log_decay = -step_size * rate
    cumulative = jnp.dot(
        log_decay,
        (down <= across).astype(full),
        preferred_element_type=full,
        precision=lax.Precision.HIGHEST,
    )
    cum_rows[...] = cumulative
    square[...] = jnp.zeros_like(square)
    square[:head_count, :] = cumulative
    cum_cols[...] = square[...].T
    totals[me] = jnp.broadcast_to(cum_cols[row_count - 1 : row_count, :], totals.shape[1:])
    square[:head_count, :] = jnp.exp(cumulative[:, row_count - 1 : row_count] - cumulative) * step_size
    tail_cols[...] = square[...].T
    for shift in range(1, ring):
        total_copy(shift).start()
    for index in (5, 6, 7):
        locals_[index].wait()

    capacity = 4 * row_count // experts
    names = lax.broadcasted_iota(jnp.int32, (experts, row_count), 0)
    members = [(names == routes_ref[k : k + 1, :]).astype(full) for k in range(2)]
    rank = jnp.dot(
        (members[0] + members[1]).astype(half),
        (down < across).astype(half),
        preferred_element_type=full,
    ) + (names * capacity).astype(full)
    plans[mine] = jnp.zeros_like(plans[mine])
    for k in range(2):
        plans[mine, k : k + 1, :] = jnp.sum(members[k] * rank, axis=0, keepdims=True)
        plans[mine, 2 + k : 3 + k, :] = pair_ref[k : k + 1, :]

    def plan_copy(shift):
        return pltpu.make_async_remote_copy(
            src_ref=plans.at[mine],
            dst_ref=plans.at[mine],
            send_sem=plan_send.at[shift],
            recv_sem=plan_recv.at[mine],
            device_id={"grp": lax.rem(mine + shift, experts)},
            device_id_type=MESH,
        )

    def plan_arrival(origin):
        return pltpu.make_async_remote_copy(
            src_ref=plans.at[origin],
            dst_ref=plans.at[origin],
            send_sem=plan_send.at[0],
            recv_sem=plan_recv.at[origin],
            device_id={"grp": lax.rem(mine + 1, experts)},
            device_id_type=MESH,
        )

    def send_plan(shift, carry):
        plan_copy(shift).start()
        return carry

    lax.fori_loop(1, experts, send_plan, 0)

    @pl.when(me > 0)
    def _():
        halo_copy(me).wait_recv()

    first_half = lax.broadcasted_iota(jnp.int32, (row_count, LANES), 1) < head_width
    offset = 8

    def convolve(column, padded):
        columns = pl.ds(column, LANES)
        before = halo[:, columns].astype(full)[16 - offset :]
        padded[:offset, :] = jnp.where(me > 0, before, 0.0)
        padded[offset:, :] = conv_ref[:, columns].astype(full)
        taps = taps_ref[:, columns]
        start = offset - tap_count + 1
        summed = taps[0:1] * padded[start : start + row_count, :]
        for k in range(1, tap_count):
            summed = summed + taps[k : k + 1] * padded[start + k : start + k + row_count, :]
        return (summed * jax.nn.sigmoid(summed)).astype(half)

    def by_head(columns_of_heads, pair):
        shifted = pltpu.roll(columns_of_heads, lax.rem(LANES - per_tile * pair, LANES), axis=1)
        return shifted[:, 0:1], shifted[:, 1:2]

    bc = convolve(width, padded.at[0]).astype(full)
    bt_ref[...] = bc.T[:state_width].astype(half)
    c_part = pltpu.roll(bc, LANES - state_width, axis=1)[:, :state_width].astype(half)
    c_ref[...] = c_part
    scores_ref[...] = jnp.dot(c_part, bt_ref[...], preferred_element_type=full)

    def take_in(part_index, carry):
        def tile(index, carry):
            pair = part_index * tiles + index
            column = pl.multiple_of(pair * LANES, LANES)
            x = convolve(column, padded.at[index])
            signal[:, pl.ds(column, LANES)] = x
            left, right = by_head(tail_cols[...], pair)
            scaled = (x.astype(full) * jnp.where(first_half, left, right)).astype(half)
            states[part_index, 0, :, pl.ds(pl.multiple_of(index * LANES, LANES), LANES)] = jnp.dot(
                bt_ref[...], scaled, preferred_element_type=full
            ).astype(half)
            return carry

        lax.fori_loop(0, tiles, tile, 0, unroll=True)
        launch(state_copy, part_index)
        return carry

    lax.fori_loop(0, LINES, take_in, 0)

    def within(part_index, carry):
        def tile(index, carry):
            pair = part_index * tiles + index
            column = pl.multiple_of(pair * LANES, LANES)
            cum = by_head(cum_cols[...], pair)
            mixing = []
            for turn in range(2):
                head = per_tile * pair + turn
                gap = cum[turn] - cum_rows[pl.ds(head, 1), :]
                decay = jnp.exp(jnp.where(down >= across, gap, -1e30))
                mixing.append(scores_ref[...] * decay * step_rows[pl.ds(head, 1), :])
            x = signal[:, pl.ds(column, LANES)].astype(full)
            stacked = jnp.concatenate(
                [jnp.where(first_half, x, 0.0), jnp.where(first_half, 0.0, x)], axis=0
            ).astype(half)
            skip = jnp.where(first_half, skip_ref[per_tile * pair], skip_ref[per_tile * pair + 1])
            base[:, pl.ds(column, LANES)] = (
                jnp.dot(
                    jnp.concatenate(mixing, axis=1).astype(half), stacked, preferred_element_type=full
                )
                + skip * x
            )
            return carry

        lax.fori_loop(0, tiles, tile, 0, unroll=True)
        relay(state_copy, part_index)
        return carry

    lax.fori_loop(0, LINES, within, 0)
    relay_weight(0, 1)

    for shift in range(1, ring):
        total_arrival(lax.rem(me + shift, ring)).wait_recv()
    for slot in range(1, ring):
        origin = source(slot)
        passed = jnp.zeros((1, LANES), full)
        for between in range(ring):
            passed = passed + jnp.where(
                (between > origin) & (between < me), totals[between, 0:1, :], 0.0
            )
        reach_ref[slot : slot + 1, :] = jnp.where(origin < me, jnp.exp(passed), 0.0)
    reach_ref[0:1, :] = jnp.zeros((1, LANES), full)
    for index in (8, 9):
        locals_[index].wait()

    def gather_in(part_index, squares):
        for step in range(chips):
            state_copy(part_index, step, True).wait_recv()

        def tile(index, squares):
            pair = part_index * tiles + index
            column = pl.multiple_of(pair * LANES, LANES)
            columns = pl.ds(column, LANES)
            local = pl.ds(pl.multiple_of(index * LANES, LANES), LANES)
            left, right = by_head(reach_ref[...], pair)
            reach = jnp.where(first_half[: reach_ref.shape[0]], left, right)
            entering = jnp.zeros((state_width, LANES), full)
            for slot in range(1, ring):
                entering = entering + reach[slot : slot + 1] * states[
                    part_index, slot, :, local
                ].astype(full)
            carried = jnp.dot(c_ref[...], entering.astype(half), preferred_element_type=full)
            left, right = by_head(cum_cols[...], pair)
            fade = jnp.exp(jnp.where(first_half, left, right))
            gate = gate_ref[:, columns].astype(full)
            value = (base[:, columns] + carried * fade) * (gate * jax.nn.sigmoid(gate))
            rows[part_index, 0, :, local] = (value * norm_ref[pl.ds(pair, 1), :]).astype(half)
            return squares + jnp.sum(value * value, axis=1, keepdims=True)

        squares = lax.fori_loop(0, tiles, tile, squares, unroll=True)
        launch(rows_copy, part_index)
        return squares

    squares = lax.fori_loop(0, LINES, gather_in, jnp.zeros((row_count, 1), full))
    row_scale = lax.rsqrt(squares * (1.0 / width) + EPSILON)

    relay_weight(0, 2)
    start_weight(1, line)
    relay(rows_copy, 0)
    relay_weight(0, 3)
    relay(rows_copy, 1)
    relay(rows_copy, 2)
    relay_weight(1, 1)
    relay_weight(1, 2)
    relay(rows_copy, 3)
    relay_weight(1, 3)

    def rows_arrived(part_index, carry):
        for step in range(chips):
            rows_copy(part_index, step, True).wait_recv()
        return carry

    lax.fori_loop(0, LINES, rows_arrived, 0)

    def share_copy(stage, slot):
        return pltpu.make_async_remote_copy(
            src_ref=shares_out[stage].at[slot],
            dst_ref=shares_in[stage].at[me],
            send_sem=share_send.at[stage, slot],
            recv_sem=share_recv.at[stage, me],
            device_id={"seq": source(slot)},
            device_id_type=MESH,
        )

    def share_arrival(stage, column):
        return pltpu.make_async_remote_copy(
            src_ref=shares_out[stage].at[0],
            dst_ref=shares_in[stage].at[column],
            send_sem=share_send.at[stage, 0],
            recv_sem=share_recv.at[stage, column],
            device_id={"seq": source(1)},
            device_id_type=MESH,
        )

    starts = (0, weight_first.shape[1])
    for stage in range(STAGES):
        breadth = weights[stage].shape[1]
        columns_here = slice(starts[stage], starts[stage] + breadth)

        def project(index, carry):
            step = (index + 1) // 2
            at = line + jnp.where(lax.rem(index, 2) == 0, step, -step)

            @pl.when((at >= 0) & (at < LINES))
            def _():
                for shift in range(1, inner):
                    weight_arrival(stage, at * inner + lax.rem(place + shift, inner)).wait_recv()
                product = jnp.dot(
                    rows[at].reshape(ring * row_count, part),
                    weights[stage][pl.ds(pl.multiple_of(at * part, part), part), :],
                    preferred_element_type=full,
                )
                total[:, columns_here] += product

            return carry

        total[:, columns_here] = jnp.zeros((ring * row_count, breadth), full)
        lax.fori_loop(0, 2 * LINES - 1, project, 0)

        def hand_out(index, carry):
            slot = ring - 1 - index
            shares_out[stage][slot] = total[
                pl.ds(pl.multiple_of(slot * row_count, row_count), row_count), columns_here
            ].astype(half)

            @pl.when(slot > 0)
            def _():
                share_copy(stage, slot).start()

            return carry

        lax.fori_loop(0, ring, hand_out, 0)
        shares_in[stage][me] = shares_out[stage][0]

    for index in (10, 11):
        locals_[index].wait()
    squares = jnp.zeros((row_count, 1), full)
    for stage in range(STAGES):
        breadth = weights[stage].shape[1]

        def mix(index, squares):
            @pl.when(index != me)
            def _():
                share_arrival(stage, index).wait_recv()

            column = pl.multiple_of(index * share + starts[stage], LANES)
            values = (
                residual_ref[:, pl.ds(column, breadth)].astype(full)
                + row_scale * shares_in[stage][index].astype(full)
            ).astype(half)
            mixed_ref[:, pl.ds(column, breadth)] = values
            wide = values.astype(full)
            return squares + jnp.sum(wide * wide, axis=1, keepdims=True)

        squares = lax.fori_loop(0, ring, mix, squares)
    scale = lax.rsqrt(squares * (1.0 / width) + EPSILON)
    for tile in range(width // LANES):
        local = tile % tiles * LANES
        line_rows[line, tile // tiles, :, local : local + LANES] = (
            mixed_ref[:, tile * LANES : (tile + 1) * LANES].astype(full)
            * scale
            * gain_ref[tile : tile + 1, :]
        ).astype(half)

    def row_copy(at, up, index):
        return pltpu.make_async_remote_copy(
            src_ref=line_rows.at[at, index],
            dst_ref=line_rows.at[at, index],
            send_sem=row_send.at[at, 0 if up else 1, index],
            recv_sem=row_recv.at[at, index],
            device_id={"grp": mine + (inner if up else -inner)},
            device_id_type=MESH,
        )

    def slots_of(owner):
        return pl.ds(pl.multiple_of(owner * capacity, capacity), capacity)

    def across_copy(source, target, sends, recvs, at, shift, index):
        other = lax.rem(place + shift, inner)
        return pltpu.make_async_remote_copy(
            src_ref=source.at[at, index, slots_of(other)],
            dst_ref=target.at[at, index, slots_of(place)],
            send_sem=sends.at[at, shift, index],
            recv_sem=recvs.at[at, place, index],
            device_id={"grp": line * inner + other},
            device_id_type=MESH,
        )

    def across_arrival(source, target, sends, recvs, at, shift, index):
        other = lax.rem(place + shift, inner)
        return pltpu.make_async_remote_copy(
            src_ref=source.at[at, index, slots_of(other)],
            dst_ref=target.at[at, index, slots_of(other)],
            send_sem=sends.at[at, shift, index],
            recv_sem=recvs.at[at, other, index],
            device_id={"grp": line * inner + other},
            device_id_type=MESH,
        )

    pick_parts = (outgoing, arrived, pick_send, pick_recv)
    made_parts = (result, returned, made_send, made_recv)

    sum_rows = row_count // SPLIT
    sum_pieces = SPLIT * LINES

    def sum_part(ref, index):
        return ref.at[index // SPLIT, pl.ds(pl.multiple_of(lax.rem(index, SPLIT) * sum_rows, 16), sum_rows)]

    def sum_copy(to, up, index):
        way = 0 if up else 1
        return pltpu.make_async_remote_copy(
            src_ref=sum_part(sums_out.at[to], index),
            dst_ref=sum_part(sums_in.at[way, to], index),
            send_sem=sum_send.at[to, index],
            recv_sem=sum_recv.at[way, to, index],
            device_id={"grp": mine + (inner if up else -inner)},
            device_id_type=MESH,
        )

    def sum_arrival(to, up, index):
        way = 0 if up else 1
        return pltpu.make_async_remote_copy(
            src_ref=sum_part(sums_out.at[to], index),
            dst_ref=sum_part(sums_in.at[way, to], index),
            send_sem=sum_send.at[to, index],
            recv_sem=sum_recv.at[way, to, index],
            device_id={"grp": mine},
            device_id_type=MESH,
        )

    def take_plan(shift, carry):
        plan_arrival(lax.rem(mine + shift, experts)).wait_recv()
        return carry

    lax.fori_loop(1, experts, take_plan, 0)
    slot_count = inner * capacity
    slot_ids = lax.broadcasted_iota(jnp.int32, (slot_count, row_count), 0)

    at_end = (line == 0) | (line == LINES - 1)

    def forward(at, up, index):
        @pl.when((at <= line) & (line < LINES - 1) if up else (at >= line) & (line > 0))
        def _():
            row_copy(at, up, index).start()

    def plan_rows(at):
        plan = plans[at * inner + place]
        slot_of = (slot_ids + line * slot_count).astype(full)
        picks = jnp.where(plan[0:1] == slot_of, 1.0, 0.0) + jnp.where(plan[1:2] == slot_of, 1.0, 0.0)
        place_back[at] = picks.T.astype(half)
        pick_rows[at] = picks.astype(half)

    def take_piece(at, step, index):
        @pl.when(step > 0)
        def _():
            row_copy(at, True, index).wait_recv()

        forward(at, True, index)
        forward(at, False, index)
        outgoing[at, index] = jnp.dot(
            pick_rows[at], line_rows[at, index], preferred_element_type=full
        ).astype(half)
        for shift in range(1, inner):
            across_copy(*pick_parts, at, shift, index).start()
        arrived[at, index, slots_of(place)] = outgoing[at, index, slots_of(place)]

    def made_arrived(to, index):
        for shift in range(1, inner):
            across_arrival(*made_parts, to, shift, index).wait_recv()

    def send_sums(to, up, index):
        way = 0 if up else 1
        column = index // SPLIT
        some = pl.ds(pl.multiple_of(lax.rem(index, SPLIT) * sum_rows, 16), sum_rows)

        @pl.when(lax.rem(index, SPLIT) == 0)
        def _():
            made_arrived(to, column)

        share = jnp.dot(place_back[to, some], returned[to, column], preferred_element_type=full)
        behind = (line > 0) if up else (line < LINES - 1)

        @pl.when(behind)
        def _():
            sum_arrival(to, up, index).wait_recv()
            sums_out[to, column, some] = (share + sums_in[way, to, column, some].astype(full)).astype(half)

        @pl.when(jnp.logical_not(behind))
        def _():
            sums_out[to, column, some] = share.astype(half)

        sum_copy(to, up, index).start()

    def run_expert(at):
        scales = []
        own_ids = lax.broadcasted_iota(jnp.int32, (capacity, row_count), 0) + mine * capacity
        for origin in range(inner):
            plan = plans[at * inner + origin]
            own_slots = own_ids.astype(full)
            scales.append(
                jnp.sum(
                    jnp.where(plan[0:1] == own_slots, plan[2:3], 0.0)
                    + jnp.where(plan[1:2] == own_slots, plan[3:4], 0.0),
                    axis=1,
                    keepdims=True,
                )
            )
        scale = jnp.concatenate(scales, axis=0)
        gate_part = jnp.zeros((slot_count, expert_gate.shape[1]), full)
        up_part = gate_part
        for index in range(LINES):
            for shift in range(1, inner):
                across_arrival(*pick_parts, at, shift, index).wait_recv()
            rows_here = arrived[at, index]
            depth_here = slice(index * part, (index + 1) * part)
            gate_part = gate_part + jnp.dot(
                rows_here, expert_gate[depth_here, :], preferred_element_type=full
            )
            up_part = up_part + jnp.dot(
                rows_here, expert_up[depth_here, :], preferred_element_type=full
            )
        hidden = (gate_part * jax.nn.sigmoid(gate_part) * up_part).astype(half)
        for index in range(LINES):
            made = jnp.dot(
                hidden, expert_down[:, index * part : (index + 1) * part], preferred_element_type=full
            )
            result[at, index] = (made * scale).astype(half)
            for shift in range(1, inner):
                across_copy(*made_parts, at, shift, index).start()
            returned[at, index, slots_of(place)] = result[at, index, slots_of(place)]

    def plan_block(at, carry):
        plan_rows(at)
        return carry

    lax.fori_loop(0, LINES, plan_block, 0)

    def round_trip(step, carry):
        def take(turn, carry):
            ahead, index = step + turn // LINES, lax.rem(turn, LINES)
            for at, wanted in ((line - ahead, True), (line + ahead, ahead > 0)):

                @pl.when((at >= 0) & (at < LINES) & wanted)
                def _():
                    take_piece(at, ahead, index)

            return carry

        steps_here = jnp.where(at_end | (step == 0), 1, jnp.where(step == 1, LINES - 2, 0))
        lax.fori_loop(0, steps_here * LINES, take, 0)

        @pl.when(step == 0)
        def _():
            for copy in locals_[12:]:
                copy.wait()

        def turn(way, carry):
            at = line + jnp.where(way == 0, -step, step)

            @pl.when((at >= 0) & (at < LINES) & ((way == 0) | (step > 0)))
            def _():
                run_expert(at)

            return carry

        lax.fori_loop(0, 2, turn, 0)

        lag = jnp.where(line >= LINES // 2, 0, 1)

        def pass_on(index, carry):
            down_index, up_index = index - lag, index - 1 + lag

            between = step > 0

            @pl.when(between & (LINES - 1 - step < line) & (down_index >= 0) & (down_index < sum_pieces))
            def _():
                send_sums(LINES - 1 - step, False, down_index)

            @pl.when(between & (step > line) & (up_index >= 0) & (up_index < sum_pieces))
            def _():
                send_sums(step, True, up_index)

            return carry

        lax.fori_loop(0, sum_pieces + 1, pass_on, 0)
        return carry

    lax.fori_loop(0, LINES, round_trip, 0)

    for index in range(LINES):
        columns = slice(index * part, (index + 1) * part)
        made_arrived(line, index)
        sum_here[...] = mixed_ref[:, columns].astype(full) + jnp.dot(
            place_back[line], returned[line, index], preferred_element_type=full
        )

        @pl.when(line > 0)
        def _():
            for turn in range(SPLIT):
                sum_arrival(line, True, index * SPLIT + turn).wait_recv()
            sum_here[...] += sums_in[0, line, index].astype(full)

        @pl.when(line < LINES - 1)
        def _():
            for turn in range(SPLIT):
                sum_arrival(line, False, index * SPLIT + turn).wait_recv()
            sum_here[...] += sums_in[1, line, index].astype(full)

        out_ref[:, columns] = sum_here[...].astype(half)

    @pl.when(me < ring - 1)
    def _():
        halo_copy(me + 1).wait_send()

    for shift in range(1, ring):
        total_copy(shift).wait_send()
        for stage in range(STAGES):
            share_copy(stage, shift).wait_send()

    def sent_plan(shift, carry):
        plan_copy(shift).wait_send()
        return carry

    lax.fori_loop(1, experts, sent_plan, 0)
    drain_ring(state_copy)
    drain_ring(rows_copy)

    def weight_left(at, carry):
        for stage in range(STAGES):
            drain_weight(stage, at)
        return carry

    lax.fori_loop(0, LINES, weight_left, 0)

    def drain(at, carry):
        def piece(index, carry):
            @pl.when((at <= line) & (line < LINES - 1))
            def _():
                row_copy(at, True, index).wait_send()

            @pl.when((at >= line) & (line > 0))
            def _():
                row_copy(at, False, index).wait_send()

            for shift in range(1, inner):
                across_copy(*pick_parts, at, shift, index).wait_send()
                across_copy(*made_parts, at, shift, index).wait_send()

            return carry

        def sum_piece(index, carry):
            @pl.when(at != line)
            def _():
                sum_copy(at, True, index).wait_send()

            return carry

        lax.fori_loop(0, sum_pieces, sum_piece, 0)

        lax.fori_loop(0, LINES, piece, 0)
        return carry

    lax.fori_loop(0, LINES, drain, 0)


def on_device(
    conv_input,
    conv_weight,
    step_raw,
    rate_log,
    skip_gain,
    gate_input,
    norm_gain,
    out_weight,
    residual,
    moe_gain,
    w_gate,
    w_up,
    w_down,
    routes,
    route_weights,
):
    half = jnp.bfloat16
    full = jnp.float32
    ring = lax.axis_size("seq")
    experts = lax.axis_size("grp")
    share = -(-out_weight.shape[1] // (ring * LANES)) * LANES
    extra = ring * share - out_weight.shape[1]
    row_count, channel_count = conv_input.shape[1:]
    tap_count = conv_weight.shape[0]
    head_count = rate_log.shape[0]
    inner_width = gate_input.shape[2]
    state_width = (channel_count - inner_width) // 2
    model_width = residual.shape[2]
    hidden_width = w_gate.shape[2]
    capacity = 4 * row_count // experts
    part = inner_width // LINES
    padded_residual, padded_weight = residual[0], out_weight
    if extra:
        padded_residual = jnp.pad(padded_residual, ((0, 0), (0, extra)))
        padded_weight = jnp.pad(padded_weight, ((0, 0), (0, extra)))
    vmem = pl.BlockSpec(memory_space=pltpu.VMEM)
    smem = pl.BlockSpec(memory_space=pltpu.SMEM)
    anywhere = pl.BlockSpec(memory_space=pl.ANY)
    inner = experts // LINES
    slot_count = inner * capacity
    row_slab = pltpu.VMEM((LINES, LINES, row_count, part), half)
    slot_slab = pltpu.VMEM((LINES, LINES, slot_count, part), half)
    pieces = [pltpu.VMEM((ring, row_count, breadth), half) for breadth in column_groups(share)]
    square = pltpu.VMEM((row_count, LANES), full)
    dma = pltpu.SemaphoreType.DMA
    layer_out = pl.pallas_call(
        functools.partial(layer_kernel, ring, experts),
        out_shape=jax.ShapeDtypeStruct((row_count, model_width), half),
        in_specs=[anywhere] * 4 + [smem] + [anywhere] * 10,
        out_specs=vmem,
        scratch_shapes=[
            pltpu.VMEM((row_count, channel_count), half),
            pltpu.VMEM((tap_count, channel_count), full),
            pltpu.VMEM((head_count, row_count), full),
            pltpu.VMEM((1, head_count), full),
            pltpu.VMEM((row_count, inner_width), half),
            pltpu.VMEM((inner_width // LANES, LANES), full),
            pltpu.VMEM((row_count, ring * share), half),
            pltpu.VMEM((model_width // LANES, LANES), full),
            pltpu.VMEM((model_width, hidden_width), half),
            pltpu.VMEM((model_width, hidden_width), half),
            pltpu.VMEM((hidden_width, model_width), half),
            pltpu.VMEM((2, row_count), jnp.int32),
            pltpu.VMEM((2, row_count), full),
            pltpu.VMEM((16, channel_count), half),
            pltpu.VMEM((part // LANES, row_count + 8, LANES), full),
            pltpu.VMEM((row_count, inner_width), half),
            pltpu.VMEM((row_count, inner_width), full),
            square,
            pltpu.VMEM((row_count, state_width), half),
            pltpu.VMEM((state_width, row_count), half),
            square,
            pltpu.VMEM((head_count, row_count), full),
            pltpu.VMEM((head_count, row_count), full),
            square,
            square,
            pltpu.VMEM((8, LANES), full),
            pltpu.VMEM((ring, 8, LANES), full),
            pltpu.VMEM((LINES, ring, state_width, part), half),
            pltpu.VMEM((LINES, ring, row_count, part), half),
            *[pltpu.VMEM((inner_width, breadth), half) for breadth in column_groups(share)],
            pltpu.VMEM((ring * row_count, share), full),
            *pieces,
            *pieces,
            pltpu.VMEM((row_count, ring * share), half),
            pltpu.VMEM((experts, 8, row_count), full),
            pltpu.VMEM((LINES, slot_count, row_count), half),
            pltpu.VMEM((LINES, row_count, slot_count), half),
            row_slab,
            slot_slab,
            slot_slab,
            slot_slab,
            slot_slab,
            row_slab,
            pltpu.VMEM((2, LINES, LINES, row_count, part), half),
            pltpu.VMEM((row_count, part), full),
            dma((15,)),
            dma((1,)),
            dma((1,)),
            dma((ring,)),
            dma((ring,)),
            dma((LINES, ring // 2)),
            dma((LINES, ring // 2)),
            dma((LINES, ring)),
            dma((LINES, ring // 2)),
            dma((LINES, ring // 2)),
            dma((LINES, ring)),
            dma((STAGES, LINES, 2)),
            dma((STAGES, LINES, experts // LINES)),
            dma((STAGES, experts)),
            dma((STAGES, ring)),
            dma((STAGES, ring)),
            dma((experts,)),
            dma((experts,)),
            dma((LINES, 2, LINES)),
            dma((LINES, LINES)),
            dma((LINES, inner, LINES)),
            dma((LINES, inner, LINES)),
            dma((LINES, inner, LINES)),
            dma((LINES, inner, LINES)),
            dma((LINES, SPLIT * LINES)),
            dma((2, LINES, SPLIT * LINES)),
        ],
        compiler_params=pltpu.CompilerParams(
            collective_id=0, has_side_effects=True, vmem_limit_bytes=56 * 1024 * 1024
        ),
        cost_estimate=pl.CostEstimate(
            flops=6 * 1024 * 1024 * 1024, bytes_accessed=64 * 1024 * 1024, transcendentals=0
        ),
    )(
        conv_input[0],
        conv_weight,
        step_raw[0].T,
        rate_log[None, :],
        skip_gain,
        gate_input[0],
        norm_gain.reshape(-1, LANES),
        padded_weight,
        padded_residual,
        moe_gain.reshape(-1, LANES),
        w_gate[0],
        w_up[0],
        w_down[0],
        routes[0].T,
        route_weights[0].T,
    )
    return layer_out[None]


def solution(mesh):
    in_specs = (
        P("grp", "seq", None),
        P(),
        P("grp", "seq", None),
        P(),
        P(),
        P("grp", "seq", None),
        P(),
        P("grp", None),
        P("grp", "seq", None),
        P(),
        P("grp", None, None),
        P("grp", None, None),
        P("grp", None, None),
        P("grp", "seq", None),
        P("grp", "seq", None),
    )
    out_specs = P("grp", "seq", None)
    return jax.shard_map(
        on_device, mesh=mesh, in_specs=in_specs, out_specs=out_specs, check_vma=False
    )
```

```python
import functools

import jax
import jax.numpy as jnp
from jax import lax
from jax.experimental import pallas as pl
from jax.experimental.pallas import tpu as pltpu
from jax.sharding import PartitionSpec as P

EPSILON = 1e-05
LANES = 128
LINES = 4
SPLIT = 1
STAGES = 2
MESH = pl.DeviceIdType.MESH


def column_groups(share):
    tiles = share // LANES
    first = max(1, (tiles * 4) // 5)
    return [first * LANES, (tiles - first) * LANES]


def layer_kernel(
    ring,
    experts,
    conv_hbm,
    taps_hbm,
    steps_hbm,
    rates_hbm,
    skip_ref,
    gate_hbm,
    norm_hbm,
    weight_hbm,
    residual_hbm,
    gain_hbm,
    expert_gate_hbm,
    expert_up_hbm,
    expert_down_hbm,
    routes_hbm,
    pair_hbm,
    out_ref,
    conv_ref,
    taps_ref,
    steps_ref,
    rates_ref,
    gate_ref,
    norm_ref,
    residual_ref,
    gain_ref,
    expert_gate,
    expert_up,
    expert_down,
    routes_ref,
    pair_ref,
    halo,
    padded,
    signal,
    base,
    scores_ref,
    c_ref,
    bt_ref,
    square,
    step_rows,
    cum_rows,
    cum_cols,
    tail_cols,
    reach_ref,
    totals,
    states,
    rows,
    weight_first,
    weight_second,
    total,
    share_out_first,
    share_out_second,
    share_in_first,
    share_in_second,
    mixed_ref,
    plans,
    pick_rows,
    place_back,
    line_rows,
    outgoing,
    arrived,
    result,
    returned,
    sums_out,
    sums_in,
    sum_here,
    local_sem,
    halo_send,
    halo_recv,
    total_send,
    total_recv,
    near_state_send,
    far_state_send,
    state_recv,
    near_rows_send,
    far_rows_send,
    rows_recv,
    line_send,
    inner_send,
    weight_recv,
    share_send,
    share_recv,
    plan_send,
    plan_recv,
    row_send,
    row_recv,
    pick_send,
    pick_recv,
    made_send,
    made_recv,
    sum_send,
    sum_recv,
):
    half = jnp.bfloat16
    full = jnp.float32
    me = lax.axis_index("seq")
    mine = lax.axis_index("grp")
    chips = ring // 2
    chip, core = me // 2, lax.rem(me, 2)
    twin = chip * 2 + 1 - core
    inner = experts // LINES
    line, place = mine // inner, lax.rem(mine, inner)

    row_count, width = gate_ref.shape
    head_count = step_rows.shape[0]
    head_width = width // head_count
    per_tile = LANES // head_width
    state_width = states.shape[2]
    part = width // LINES
    tiles = part // LANES
    weights = (weight_first, weight_second)
    shares_out = (share_out_first, share_out_second)
    shares_in = (share_in_first, share_in_second)
    depth = weight_first.shape[0] // experts
    share = total.shape[1]
    tap_count = taps_ref.shape[0]

    share_column = pl.multiple_of(me * share, LANES)
    locals_ = [
        pltpu.make_async_copy(source, target, local_sem.at[index])
        for index, (source, target) in enumerate(
            (
                *(
                    (
                        weight_hbm.at[:, pl.ds(share_column + start, ref.shape[1])],
                        ref.at[pl.ds(mine * depth, depth)],
                    )
                    for start, ref in zip((0, weight_first.shape[1]), weights)
                ),
                (steps_hbm, steps_ref),
                (rates_hbm, rates_ref),
                (conv_hbm, conv_ref),
                (taps_hbm, taps_ref),
                (routes_hbm, routes_ref),
                (pair_hbm, pair_ref),
                (gate_hbm, gate_ref),
                (norm_hbm, norm_ref),
                (residual_hbm, residual_ref),
                (gain_hbm, gain_ref),
                (expert_gate_hbm, expert_gate),
                (expert_up_hbm, expert_up),
                (expert_down_hbm, expert_down),
            )
        )
    ]
    for copy in locals_[:12]:
        copy.start()

    barrier = pltpu.get_barrier_semaphore()

    def greet(axis, own, count):
        def step(shift, carry):
            pl.semaphore_signal(
                barrier,
                inc=1,
                device_id={axis: lax.rem(own + shift, count)},
                device_id_type=MESH,
            )
            return carry

        lax.fori_loop(1, count, step, 0)

    greet("seq", me, ring)
    greet("grp", mine, experts)


    def far(step):
        return lax.rem(chip + step, chips) * 2 + core

    def source(slot):
        return lax.rem(chip + chips - slot // 2, chips) * 2 + lax.rem(me + slot, 2)

    def ring_copy(slots, sends, part_index, step, near):
        near_send, far_send, recv = sends
        return pltpu.make_async_remote_copy(
            src_ref=slots.at[part_index, 2 * step if near else 0],
            dst_ref=slots.at[part_index, 2 * step + 1 if near else 2 * step],
            send_sem=(near_send if near else far_send).at[part_index, step],
            recv_sem=recv.at[part_index, 2 * step + 1 if near else 2 * step],
            device_id={"seq": twin if near else far(step)},
            device_id_type=MESH,
        )

    state_copy = functools.partial(
        ring_copy, states, (near_state_send, far_state_send, state_recv)
    )
    rows_copy = functools.partial(ring_copy, rows, (near_rows_send, far_rows_send, rows_recv))

    def launch(copy, part_index):
        for step in range(1, chips):
            copy(part_index, step, False).start()
        copy(part_index, 0, True).start()

    def relay(copy, part_index):
        for step in range(1, chips):
            copy(part_index, step, False).wait_recv()
            copy(part_index, step, True).start()

    def drain_ring(copy):
        def body(part_index, carry):
            for step in range(1, chips):
                copy(part_index, step, False).wait_send()
            for step in range(chips):
                copy(part_index, step, True).wait_send()
            return carry

        lax.fori_loop(0, LINES, body, 0)

    def halo_copy(target):
        return pltpu.make_async_remote_copy(
            src_ref=conv_ref.at[pl.ds(row_count - 16, 16)],
            dst_ref=halo,
            send_sem=halo_send.at[0],
            recv_sem=halo_recv.at[0],
            device_id={"seq": target},
            device_id_type=MESH,
        )

    def total_copy(shift):
        return pltpu.make_async_remote_copy(
            src_ref=totals.at[me],
            dst_ref=totals.at[me],
            send_sem=total_send.at[shift],
            recv_sem=total_recv.at[me],
            device_id={"seq": lax.rem(me + shift, ring)},
            device_id_type=MESH,
        )

    def total_arrival(origin):
        return pltpu.make_async_remote_copy(
            src_ref=totals.at[origin],
            dst_ref=totals.at[origin],
            send_sem=total_send.at[0],
            recv_sem=total_recv.at[origin],
            device_id={"seq": twin},
            device_id_type=MESH,
        )

    def weight_copy(stage, block, target, send_sem):
        block_rows = weights[stage].at[pl.ds(block * depth, depth)]
        return pltpu.make_async_remote_copy(
            src_ref=block_rows,
            dst_ref=block_rows,
            send_sem=send_sem,
            recv_sem=weight_recv.at[stage, block],
            device_id={"grp": target},
            device_id_type=MESH,
        )

    def line_copy(stage, at, up):
        step = 1 if up else -1
        return weight_copy(
            stage,
            at * inner + place,
            mine + step * inner,
            line_send.at[stage, at, 0 if up else 1],
        )

    def inner_copy(stage, at, shift):
        return weight_copy(
            stage,
            at * inner + place,
            line * inner + lax.rem(place + shift, inner),
            inner_send.at[stage, at, shift],
        )

    def weight_arrival(stage, block):
        return weight_copy(stage, block, mine, line_send.at[stage, 0, 0])

    def each_weight_copy(do):
        def visit(stage, at):
            @pl.when((at <= line) & (line < LINES - 1))
            def _():
                do(line_copy(stage, at, True))

            @pl.when((at >= line) & (line > 0))
            def _():
                do(line_copy(stage, at, False))

            for shift in range(1, inner):
                do(inner_copy(stage, at, shift))

        return visit

    start_weight = each_weight_copy(lambda copy: copy.start())
    drain_weight = each_weight_copy(lambda copy: copy.wait_send())

    def relay_weight(stage, step):
        for at in (line - step, line + step):

            @pl.when((at >= 0) & (at < LINES))
            def _():
                weight_arrival(stage, at * inner + place).wait_recv()
                start_weight(stage, at)


    down = lax.broadcasted_iota(jnp.int32, (row_count, row_count), 0)
    across = lax.broadcasted_iota(jnp.int32, (row_count, row_count), 1)
    for index in (2, 3):
        locals_[index].wait()
    rate_square = jnp.where(
        down[:head_count, :head_count] == across[:head_count, :head_count], rates_ref[...], 0.0
    )
    rate = jnp.exp(jnp.sum(rate_square, axis=1, keepdims=True))
    raw = steps_ref[...]
    step_size = jnp.maximum(raw, 0.0) + jnp.log1p(jnp.exp(-jnp.abs(raw)))
    step_rows[...] = step_size
    log_decay = -step_size * rate
    cumulative = jnp.dot(
        log_decay,
        (down <= across).astype(full),
        preferred_element_type=full,
        precision=lax.Precision.HIGHEST,
    )
    cum_rows[...] = cumulative
    square[...] = jnp.zeros_like(square)
    square[:head_count, :] = cumulative
    cum_cols[...] = square[...].T
    totals[me] = jnp.broadcast_to(cum_cols[row_count - 1 : row_count, :], totals.shape[1:])
    square[:head_count, :] = jnp.exp(cumulative[:, row_count - 1 : row_count] - cumulative) * step_size
    tail_cols[...] = square[...].T
    for index in (0, 1, 4):
        locals_[index].wait()
    pl.semaphore_wait(barrier, ring - 1 + experts - 1)
    start_weight(0, line)
    for copy in locals_[12:]:
        copy.start()

    @pl.when(me < ring - 1)
    def _():
        halo_copy(me + 1).start()

    for shift in range(1, ring):
        total_copy(shift).start()
    for index in (5, 6, 7):
        locals_[index].wait()

    capacity = 4 * row_count // experts
    names = lax.broadcasted_iota(jnp.int32, (experts, row_count), 0)
    members = [(names == routes_ref[k : k + 1, :]).astype(full) for k in range(2)]
    rank = jnp.dot(
        (members[0] + members[1]).astype(half),
        (down < across).astype(half),
        preferred_element_type=full,
    ) + (names * capacity).astype(full)
    plans[mine] = jnp.zeros_like(plans[mine])
    for k in range(2):
        plans[mine, k : k + 1, :] = jnp.sum(members[k] * rank, axis=0, keepdims=True)
        plans[mine, 2 + k : 3 + k, :] = pair_ref[k : k + 1, :]

    def plan_copy(shift):
        return pltpu.make_async_remote_copy(
            src_ref=plans.at[mine],
            dst_ref=plans.at[mine],
            send_sem=plan_send.at[shift],
            recv_sem=plan_recv.at[mine],
            device_id={"grp": lax.rem(mine + shift, experts)},
            device_id_type=MESH,
        )

    def plan_arrival(origin):
        return pltpu.make_async_remote_copy(
            src_ref=plans.at[origin],
            dst_ref=plans.at[origin],
            send_sem=plan_send.at[0],
            recv_sem=plan_recv.at[origin],
            device_id={"grp": lax.rem(mine + 1, experts)},
            device_id_type=MESH,
        )

    def send_plan(shift, carry):
        plan_copy(shift).start()
        return carry

    lax.fori_loop(1, experts, send_plan, 0)

    @pl.when(me > 0)
    def _():
        halo_copy(me).wait_recv()

    first_half = lax.broadcasted_iota(jnp.int32, (row_count, LANES), 1) < head_width
    offset = 8

    def convolve(column, padded):
        columns = pl.ds(column, LANES)
        before = halo[:, columns].astype(full)[16 - offset :]
        padded[:offset, :] = jnp.where(me > 0, before, 0.0)
        padded[offset:, :] = conv_ref[:, columns].astype(full)
        taps = taps_ref[:, columns]
        start = offset - tap_count + 1
        summed = taps[0:1] * padded[start : start + row_count, :]
        for k in range(1, tap_count):
            summed = summed + taps[k : k + 1] * padded[start + k : start + k + row_count, :]
        return (summed * jax.nn.sigmoid(summed)).astype(half)

    def by_head(columns_of_heads, pair):
        shifted = pltpu.roll(columns_of_heads, lax.rem(LANES - per_tile * pair, LANES), axis=1)
        return shifted[:, 0:1], shifted[:, 1:2]

    bc = convolve(width, padded.at[0]).astype(full)
    bt_ref[...] = bc.T[:state_width].astype(half)
    c_part = pltpu.roll(bc, LANES - state_width, axis=1)[:, :state_width].astype(half)
    c_ref[...] = c_part
    scores_ref[...] = jnp.dot(c_part, bt_ref[...], preferred_element_type=full)

    def take_in(part_index, carry):
        def tile(index, carry):
            pair = part_index * tiles + index
            column = pl.multiple_of(pair * LANES, LANES)
            x = convolve(column, padded.at[index])
            signal[:, pl.ds(column, LANES)] = x
            left, right = by_head(tail_cols[...], pair)
            scaled = (x.astype(full) * jnp.where(first_half, left, right)).astype(half)
            states[part_index, 0, :, pl.ds(pl.multiple_of(index * LANES, LANES), LANES)] = jnp.dot(
                bt_ref[...], scaled, preferred_element_type=full
            ).astype(half)
            return carry

        lax.fori_loop(0, tiles, tile, 0, unroll=True)
        launch(state_copy, part_index)
        return carry

    lax.fori_loop(0, LINES, take_in, 0)

    def within(part_index, carry):
        def tile(index, carry):
            pair = part_index * tiles + index
            column = pl.multiple_of(pair * LANES, LANES)
            cum = by_head(cum_cols[...], pair)
            mixing = []
            for turn in range(2):
                head = per_tile * pair + turn
                gap = cum[turn] - cum_rows[pl.ds(head, 1), :]
                decay = jnp.exp(jnp.where(down >= across, gap, -1e30))
                mixing.append(scores_ref[...] * decay * step_rows[pl.ds(head, 1), :])
            x = signal[:, pl.ds(column, LANES)].astype(full)
            stacked = jnp.concatenate(
                [jnp.where(first_half, x, 0.0), jnp.where(first_half, 0.0, x)], axis=0
            ).astype(half)
            skip = jnp.where(first_half, skip_ref[per_tile * pair], skip_ref[per_tile * pair + 1])
            base[:, pl.ds(column, LANES)] = (
                jnp.dot(
                    jnp.concatenate(mixing, axis=1).astype(half), stacked, preferred_element_type=full
                )
                + skip * x
            )
            return carry

        lax.fori_loop(0, tiles, tile, 0, unroll=True)
        relay(state_copy, part_index)
        return carry

    relay_weight(0, 1)
    lax.fori_loop(0, LINES, within, 0)

    for shift in range(1, ring):
        total_arrival(lax.rem(me + shift, ring)).wait_recv()
    for slot in range(1, ring):
        origin = source(slot)
        passed = jnp.zeros((1, LANES), full)
        for between in range(ring):
            passed = passed + jnp.where(
                (between > origin) & (between < me), totals[between, 0:1, :], 0.0
            )
        reach_ref[slot : slot + 1, :] = jnp.where(origin < me, jnp.exp(passed), 0.0)
    reach_ref[0:1, :] = jnp.zeros((1, LANES), full)
    for index in (8, 9):
        locals_[index].wait()

    def gather_in(part_index, squares):
        for step in range(chips):
            state_copy(part_index, step, True).wait_recv()

        def tile(index, squares):
            pair = part_index * tiles + index
            column = pl.multiple_of(pair * LANES, LANES)
            columns = pl.ds(column, LANES)
            local = pl.ds(pl.multiple_of(index * LANES, LANES), LANES)
            left, right = by_head(reach_ref[...], pair)
            reach = jnp.where(first_half[: reach_ref.shape[0]], left, right)
            entering = jnp.zeros((state_width, LANES), full)
            for slot in range(1, ring):
                entering = entering + reach[slot : slot + 1] * states[
                    part_index, slot, :, local
                ].astype(full)
            carried = jnp.dot(c_ref[...], entering.astype(half), preferred_element_type=full)
            left, right = by_head(cum_cols[...], pair)
            fade = jnp.exp(jnp.where(first_half, left, right))
            gate = gate_ref[:, columns].astype(full)
            value = (base[:, columns] + carried * fade) * (gate * jax.nn.sigmoid(gate))
            rows[part_index, 0, :, local] = (value * norm_ref[pl.ds(pair, 1), :]).astype(half)
            return squares + jnp.sum(value * value, axis=1, keepdims=True)

        squares = lax.fori_loop(0, tiles, tile, squares, unroll=True)
        launch(rows_copy, part_index)
        return squares

    squares = lax.fori_loop(0, LINES, gather_in, jnp.zeros((row_count, 1), full))
    row_scale = lax.rsqrt(squares * (1.0 / width) + EPSILON)

    relay_weight(0, 2)
    start_weight(1, line)
    relay(rows_copy, 0)
    relay_weight(0, 3)
    relay(rows_copy, 1)
    relay(rows_copy, 2)
    relay_weight(1, 1)
    relay_weight(1, 2)
    relay(rows_copy, 3)
    relay_weight(1, 3)

    def rows_arrived(part_index, carry):
        for step in range(chips):
            rows_copy(part_index, step, True).wait_recv()
        return carry

    lax.fori_loop(0, LINES, rows_arrived, 0)

    def share_copy(stage, slot):
        return pltpu.make_async_remote_copy(
            src_ref=shares_out[stage].at[slot],
            dst_ref=shares_in[stage].at[me],
            send_sem=share_send.at[stage, slot],
            recv_sem=share_recv.at[stage, me],
            device_id={"seq": source(slot)},
            device_id_type=MESH,
        )

    def share_arrival(stage, column):
        return pltpu.make_async_remote_copy(
            src_ref=shares_out[stage].at[0],
            dst_ref=shares_in[stage].at[column],
            send_sem=share_send.at[stage, 0],
            recv_sem=share_recv.at[stage, column],
            device_id={"seq": source(1)},
            device_id_type=MESH,
        )

    starts = (0, weight_first.shape[1])
    for stage in range(STAGES):
        breadth = weights[stage].shape[1]
        columns_here = slice(starts[stage], starts[stage] + breadth)

        def project(index, carry):
            step = (index + 1) // 2
            at = line + jnp.where(lax.rem(index, 2) == 0, step, -step)

            @pl.when((at >= 0) & (at < LINES))
            def _():
                for shift in range(1, inner):
                    weight_arrival(stage, at * inner + lax.rem(place + shift, inner)).wait_recv()
                product = jnp.dot(
                    rows[at].reshape(ring * row_count, part),
                    weights[stage][pl.ds(pl.multiple_of(at * part, part), part), :],
                    preferred_element_type=full,
                )
                total[:, columns_here] += product

            return carry

        total[:, columns_here] = jnp.zeros((ring * row_count, breadth), full)
        lax.fori_loop(0, 2 * LINES - 1, project, 0)

        def hand_out(index, carry):
            slot = ring - 1 - index
            shares_out[stage][slot] = total[
                pl.ds(pl.multiple_of(slot * row_count, row_count), row_count), columns_here
            ].astype(half)

            @pl.when(slot > 0)
            def _():
                share_copy(stage, slot).start()

            return carry

        lax.fori_loop(0, ring, hand_out, 0)
        shares_in[stage][me] = shares_out[stage][0]

    for index in (10, 11):
        locals_[index].wait()
    squares = jnp.zeros((row_count, 1), full)
    for stage in range(STAGES):
        breadth = weights[stage].shape[1]

        def mix(index, squares):
            @pl.when(index != me)
            def _():
                share_arrival(stage, index).wait_recv()

            column = pl.multiple_of(index * share + starts[stage], LANES)
            values = (
                residual_ref[:, pl.ds(column, breadth)].astype(full)
                + row_scale * shares_in[stage][index].astype(full)
            ).astype(half)
            mixed_ref[:, pl.ds(column, breadth)] = values
            wide = values.astype(full)
            return squares + jnp.sum(wide * wide, axis=1, keepdims=True)

        squares = lax.fori_loop(0, ring, mix, squares)
    scale = lax.rsqrt(squares * (1.0 / width) + EPSILON)
    for tile in range(width // LANES):
        local = tile % tiles * LANES
        line_rows[line, tile // tiles, :, local : local + LANES] = (
            mixed_ref[:, tile * LANES : (tile + 1) * LANES].astype(full)
            * scale
            * gain_ref[tile : tile + 1, :]
        ).astype(half)

    def row_copy(at, up, index):
        return pltpu.make_async_remote_copy(
            src_ref=line_rows.at[at, index],
            dst_ref=line_rows.at[at, index],
            send_sem=row_send.at[at, 0 if up else 1, index],
            recv_sem=row_recv.at[at, index],
            device_id={"grp": mine + (inner if up else -inner)},
            device_id_type=MESH,
        )

    def slots_of(owner):
        return pl.ds(pl.multiple_of(owner * capacity, capacity), capacity)

    def across_copy(source, target, sends, recvs, at, shift, index):
        other = lax.rem(place + shift, inner)
        return pltpu.make_async_remote_copy(
            src_ref=source.at[at, index, slots_of(other)],
            dst_ref=target.at[at, index, slots_of(place)],
            send_sem=sends.at[at, shift, index],
            recv_sem=recvs.at[at, place, index],
            device_id={"grp": line * inner + other},
            device_id_type=MESH,
        )

    def across_arrival(source, target, sends, recvs, at, shift, index):
        other = lax.rem(place + shift, inner)
        return pltpu.make_async_remote_copy(
            src_ref=source.at[at, index, slots_of(other)],
            dst_ref=target.at[at, index, slots_of(other)],
            send_sem=sends.at[at, shift, index],
            recv_sem=recvs.at[at, other, index],
            device_id={"grp": line * inner + other},
            device_id_type=MESH,
        )

    pick_parts = (outgoing, arrived, pick_send, pick_recv)
    made_parts = (result, returned, made_send, made_recv)

    sum_rows = row_count // SPLIT
    sum_pieces = SPLIT * LINES

    def sum_part(ref, index):
        return ref.at[index // SPLIT, pl.ds(pl.multiple_of(lax.rem(index, SPLIT) * sum_rows, 16), sum_rows)]

    def sum_copy(to, up, index):
        way = 0 if up else 1
        return pltpu.make_async_remote_copy(
            src_ref=sum_part(sums_out.at[to], index),
            dst_ref=sum_part(sums_in.at[way, to], index),
            send_sem=sum_send.at[to, index],
            recv_sem=sum_recv.at[way, to, index],
            device_id={"grp": mine + (inner if up else -inner)},
            device_id_type=MESH,
        )

    def sum_arrival(to, up, index):
        way = 0 if up else 1
        return pltpu.make_async_remote_copy(
            src_ref=sum_part(sums_out.at[to], index),
            dst_ref=sum_part(sums_in.at[way, to], index),
            send_sem=sum_send.at[to, index],
            recv_sem=sum_recv.at[way, to, index],
            device_id={"grp": mine},
            device_id_type=MESH,
        )

    def take_plan(shift, carry):
        plan_arrival(lax.rem(mine + shift, experts)).wait_recv()
        return carry

    lax.fori_loop(1, experts, take_plan, 0)
    slot_count = inner * capacity
    slot_ids = lax.broadcasted_iota(jnp.int32, (slot_count, row_count), 0)

    at_end = (line == 0) | (line == LINES - 1)

    def forward(at, up, index):
        @pl.when((at <= line) & (line < LINES - 1) if up else (at >= line) & (line > 0))
        def _():
            row_copy(at, up, index).start()

    def plan_rows(at):
        plan = plans[at * inner + place]
        slot_of = (slot_ids + line * slot_count).astype(full)
        picks = jnp.where(plan[0:1] == slot_of, 1.0, 0.0) + jnp.where(plan[1:2] == slot_of, 1.0, 0.0)
        place_back[at] = picks.T.astype(half)
        pick_rows[at] = picks.astype(half)

    def take_piece(at, step, index):
        @pl.when(step > 0)
        def _():
            row_copy(at, True, index).wait_recv()

        forward(at, True, index)
        forward(at, False, index)
        outgoing[at, index] = jnp.dot(
            pick_rows[at], line_rows[at, index], preferred_element_type=full
        ).astype(half)
        for shift in range(1, inner):
            across_copy(*pick_parts, at, shift, index).start()
        arrived[at, index, slots_of(place)] = outgoing[at, index, slots_of(place)]

    def made_arrived(to, index):
        for shift in range(1, inner):
            across_arrival(*made_parts, to, shift, index).wait_recv()

    def send_sums(to, up, index):
        way = 0 if up else 1
        column = index // SPLIT
        some = pl.ds(pl.multiple_of(lax.rem(index, SPLIT) * sum_rows, 16), sum_rows)

        @pl.when(lax.rem(index, SPLIT) == 0)
        def _():
            made_arrived(to, column)

        share = jnp.dot(place_back[to, some], returned[to, column], preferred_element_type=full)
        behind = (line > 0) if up else (line < LINES - 1)

        @pl.when(behind)
        def _():
            sum_arrival(to, up, index).wait_recv()
            sums_out[to, column, some] = (share + sums_in[way, to, column, some].astype(full)).astype(half)

        @pl.when(jnp.logical_not(behind))
        def _():
            sums_out[to, column, some] = share.astype(half)

        sum_copy(to, up, index).start()

    def run_expert(at):
        scales = []
        own_ids = lax.broadcasted_iota(jnp.int32, (capacity, row_count), 0) + mine * capacity
        for origin in range(inner):
            plan = plans[at * inner + origin]
            own_slots = own_ids.astype(full)
            scales.append(
                jnp.sum(
                    jnp.where(plan[0:1] == own_slots, plan[2:3], 0.0)
                    + jnp.where(plan[1:2] == own_slots, plan[3:4], 0.0),
                    axis=1,
                    keepdims=True,
                )
            )
        scale = jnp.concatenate(scales, axis=0)
        gate_part = jnp.zeros((slot_count, expert_gate.shape[1]), full)
        up_part = gate_part
        for index in range(LINES):
            for shift in range(1, inner):
                across_arrival(*pick_parts, at, shift, index).wait_recv()
            rows_here = arrived[at, index]
            depth_here = slice(index * part, (index + 1) * part)
            gate_part = gate_part + jnp.dot(
                rows_here, expert_gate[depth_here, :], preferred_element_type=full
            )
            up_part = up_part + jnp.dot(
                rows_here, expert_up[depth_here, :], preferred_element_type=full
            )
        hidden = (gate_part * jax.nn.sigmoid(gate_part) * up_part).astype(half)
        for index in range(LINES):
            made = jnp.dot(
                hidden, expert_down[:, index * part : (index + 1) * part], preferred_element_type=full
            )
            result[at, index] = (made * scale).astype(half)
            for shift in range(1, inner):
                across_copy(*made_parts, at, shift, index).start()
            returned[at, index, slots_of(place)] = result[at, index, slots_of(place)]

    def plan_block(at, carry):
        plan_rows(at)
        return carry

    lax.fori_loop(0, LINES, plan_block, 0)

    def round_trip(step, carry):
        def take(turn, carry):
            ahead, index = step + turn // LINES, lax.rem(turn, LINES)
            for at, wanted in ((line - ahead, True), (line + ahead, ahead > 0)):

                @pl.when((at >= 0) & (at < LINES) & wanted)
                def _():
                    take_piece(at, ahead, index)

            return carry

        steps_here = jnp.where(at_end | (step == 0), 1, jnp.where(step == 1, LINES - 2, 0))
        lax.fori_loop(0, steps_here * LINES, take, 0)

        @pl.when(step == 0)
        def _():
            for copy in locals_[12:]:
                copy.wait()

        def turn(way, carry):
            at = line + jnp.where(way == 0, -step, step)

            @pl.when((at >= 0) & (at < LINES) & ((way == 0) | (step > 0)))
            def _():
                run_expert(at)

            return carry

        lax.fori_loop(0, 2, turn, 0)

        lag = jnp.where(line >= LINES // 2, 0, 1)

        def pass_on(index, carry):
            down_index, up_index = index - lag, index - 1 + lag

            between = step > 0

            @pl.when(between & (LINES - 1 - step < line) & (down_index >= 0) & (down_index < sum_pieces))
            def _():
                send_sums(LINES - 1 - step, False, down_index)

            @pl.when(between & (step > line) & (up_index >= 0) & (up_index < sum_pieces))
            def _():
                send_sums(step, True, up_index)

            return carry

        lax.fori_loop(0, sum_pieces + 1, pass_on, 0)
        return carry

    lax.fori_loop(0, LINES, round_trip, 0)

    for index in range(LINES):
        columns = slice(index * part, (index + 1) * part)
        made_arrived(line, index)
        sum_here[...] = mixed_ref[:, columns].astype(full) + jnp.dot(
            place_back[line], returned[line, index], preferred_element_type=full
        )

        @pl.when(line > 0)
        def _():
            for turn in range(SPLIT):
                sum_arrival(line, True, index * SPLIT + turn).wait_recv()
            sum_here[...] += sums_in[0, line, index].astype(full)

        @pl.when(line < LINES - 1)
        def _():
            for turn in range(SPLIT):
                sum_arrival(line, False, index * SPLIT + turn).wait_recv()
            sum_here[...] += sums_in[1, line, index].astype(full)

        out_ref[:, columns] = sum_here[...].astype(half)

    @pl.when(me < ring - 1)
    def _():
        halo_copy(me + 1).wait_send()

    for shift in range(1, ring):
        total_copy(shift).wait_send()
        for stage in range(STAGES):
            share_copy(stage, shift).wait_send()

    def sent_plan(shift, carry):
        plan_copy(shift).wait_send()
        return carry

    lax.fori_loop(1, experts, sent_plan, 0)
    drain_ring(state_copy)
    drain_ring(rows_copy)

    def weight_left(at, carry):
        for stage in range(STAGES):
            drain_weight(stage, at)
        return carry

    lax.fori_loop(0, LINES, weight_left, 0)

    def drain(at, carry):
        def piece(index, carry):
            @pl.when((at <= line) & (line < LINES - 1))
            def _():
                row_copy(at, True, index).wait_send()

            @pl.when((at >= line) & (line > 0))
            def _():
                row_copy(at, False, index).wait_send()

            for shift in range(1, inner):
                across_copy(*pick_parts, at, shift, index).wait_send()
                across_copy(*made_parts, at, shift, index).wait_send()

            return carry

        def sum_piece(index, carry):
            @pl.when(at != line)
            def _():
                sum_copy(at, True, index).wait_send()

            return carry

        lax.fori_loop(0, sum_pieces, sum_piece, 0)

        lax.fori_loop(0, LINES, piece, 0)
        return carry

    lax.fori_loop(0, LINES, drain, 0)


def on_device(
    conv_input,
    conv_weight,
    step_raw,
    rate_log,
    skip_gain,
    gate_input,
    norm_gain,
    out_weight,
    residual,
    moe_gain,
    w_gate,
    w_up,
    w_down,
    routes,
    route_weights,
):
    half = jnp.bfloat16
    full = jnp.float32
    ring = lax.axis_size("seq")
    experts = lax.axis_size("grp")
    share = -(-out_weight.shape[1] // (ring * LANES)) * LANES
    extra = ring * share - out_weight.shape[1]
    row_count, channel_count = conv_input.shape[1:]
    tap_count = conv_weight.shape[0]
    head_count = rate_log.shape[0]
    inner_width = gate_input.shape[2]
    state_width = (channel_count - inner_width) // 2
    model_width = residual.shape[2]
    hidden_width = w_gate.shape[2]
    capacity = 4 * row_count // experts
    part = inner_width // LINES
    padded_residual, padded_weight = residual[0], out_weight
    if extra:
        padded_residual = jnp.pad(padded_residual, ((0, 0), (0, extra)))
        padded_weight = jnp.pad(padded_weight, ((0, 0), (0, extra)))
    vmem = pl.BlockSpec(memory_space=pltpu.VMEM)
    smem = pl.BlockSpec(memory_space=pltpu.SMEM)
    anywhere = pl.BlockSpec(memory_space=pl.ANY)
    inner = experts // LINES
    slot_count = inner * capacity
    row_slab = pltpu.VMEM((LINES, LINES, row_count, part), half)
    slot_slab = pltpu.VMEM((LINES, LINES, slot_count, part), half)
    pieces = [pltpu.VMEM((ring, row_count, breadth), half) for breadth in column_groups(share)]
    square = pltpu.VMEM((row_count, LANES), full)
    dma = pltpu.SemaphoreType.DMA
    layer_out = pl.pallas_call(
        functools.partial(layer_kernel, ring, experts),
        out_shape=jax.ShapeDtypeStruct((row_count, model_width), half),
        in_specs=[anywhere] * 4 + [smem] + [anywhere] * 10,
        out_specs=vmem,
        scratch_shapes=[
            pltpu.VMEM((row_count, channel_count), half),
            pltpu.VMEM((tap_count, channel_count), full),
            pltpu.VMEM((head_count, row_count), full),
            pltpu.VMEM((1, head_count), full),
            pltpu.VMEM((row_count, inner_width), half),
            pltpu.VMEM((inner_width // LANES, LANES), full),
            pltpu.VMEM((row_count, ring * share), half),
            pltpu.VMEM((model_width // LANES, LANES), full),
            pltpu.VMEM((model_width, hidden_width), half),
            pltpu.VMEM((model_width, hidden_width), half),
            pltpu.VMEM((hidden_width, model_width), half),
            pltpu.VMEM((2, row_count), jnp.int32),
            pltpu.VMEM((2, row_count), full),
            pltpu.VMEM((16, channel_count), half),
            pltpu.VMEM((part // LANES, row_count + 8, LANES), full),
            pltpu.VMEM((row_count, inner_width), half),
            pltpu.VMEM((row_count, inner_width), full),
            square,
            pltpu.VMEM((row_count, state_width), half),
            pltpu.VMEM((state_width, row_count), half),
            square,
            pltpu.VMEM((head_count, row_count), full),
            pltpu.VMEM((head_count, row_count), full),
            square,
            square,
            pltpu.VMEM((8, LANES), full),
            pltpu.VMEM((ring, 8, LANES), full),
            pltpu.VMEM((LINES, ring, state_width, part), half),
            pltpu.VMEM((LINES, ring, row_count, part), half),
            *[pltpu.VMEM((inner_width, breadth), half) for breadth in column_groups(share)],
            pltpu.VMEM((ring * row_count, share), full),
            *pieces,
            *pieces,
            pltpu.VMEM((row_count, ring * share), half),
            pltpu.VMEM((experts, 8, row_count), full),
            pltpu.VMEM((LINES, slot_count, row_count), half),
            pltpu.VMEM((LINES, row_count, slot_count), half),
            row_slab,
            slot_slab,
            slot_slab,
            slot_slab,
            slot_slab,
            row_slab,
            pltpu.VMEM((2, LINES, LINES, row_count, part), half),
            pltpu.VMEM((row_count, part), full),
            dma((15,)),
            dma((1,)),
            dma((1,)),
            dma((ring,)),
            dma((ring,)),
            dma((LINES, ring // 2)),
            dma((LINES, ring // 2)),
            dma((LINES, ring)),
            dma((LINES, ring // 2)),
            dma((LINES, ring // 2)),
            dma((LINES, ring)),
            dma((STAGES, LINES, 2)),
            dma((STAGES, LINES, experts // LINES)),
            dma((STAGES, experts)),
            dma((STAGES, ring)),
            dma((STAGES, ring)),
            dma((experts,)),
            dma((experts,)),
            dma((LINES, 2, LINES)),
            dma((LINES, LINES)),
            dma((LINES, inner, LINES)),
            dma((LINES, inner, LINES)),
            dma((LINES, inner, LINES)),
            dma((LINES, inner, LINES)),
            dma((LINES, SPLIT * LINES)),
            dma((2, LINES, SPLIT * LINES)),
        ],
        compiler_params=pltpu.CompilerParams(
            collective_id=0, has_side_effects=True, vmem_limit_bytes=56 * 1024 * 1024
        ),
        cost_estimate=pl.CostEstimate(
            flops=6 * 1024 * 1024 * 1024, bytes_accessed=64 * 1024 * 1024, transcendentals=0
        ),
    )(
        conv_input[0],
        conv_weight,
        step_raw[0].T,
        rate_log[None, :],
        skip_gain,
        gate_input[0],
        norm_gain.reshape(-1, LANES),
        padded_weight,
        padded_residual,
        moe_gain.reshape(-1, LANES),
        w_gate[0],
        w_up[0],
        w_down[0],
        routes[0].T,
        route_weights[0].T,
    )
    return layer_out[None]


def solution(mesh):
    in_specs = (
        P("grp", "seq", None),
        P(),
        P("grp", "seq", None),
        P(),
        P(),
        P("grp", "seq", None),
        P(),
        P("grp", None),
        P("grp", "seq", None),
        P(),
        P("grp", None, None),
        P("grp", None, None),
        P("grp", None, None),
        P("grp", "seq", None),
        P("grp", "seq", None),
    )
    out_specs = P("grp", "seq", None)
    return jax.shard_map(
        on_device, mesh=mesh, in_specs=in_specs, out_specs=out_specs, check_vma=False
    )
```

```python
import functools

import jax
import jax.numpy as jnp
from jax import lax
from jax.experimental import pallas as pl
from jax.experimental.pallas import tpu as pltpu
from jax.sharding import PartitionSpec as P

EPSILON = 1e-05
LANES = 128
LINES = 4
SPLIT = 1
STAGES = 2
MESH = pl.DeviceIdType.MESH


def column_groups(share):
    tiles = share // LANES
    first = max(1, (tiles * 4) // 5)
    return [first * LANES, (tiles - first) * LANES]


def layer_kernel(
    ring,
    experts,
    conv_hbm,
    taps_hbm,
    steps_hbm,
    rates_hbm,
    skip_ref,
    gate_hbm,
    norm_hbm,
    weight_hbm,
    residual_hbm,
    gain_hbm,
    expert_gate_hbm,
    expert_up_hbm,
    expert_down_hbm,
    routes_hbm,
    pair_hbm,
    out_ref,
    conv_ref,
    taps_ref,
    steps_ref,
    rates_ref,
    gate_ref,
    norm_ref,
    residual_ref,
    gain_ref,
    expert_gate,
    expert_up,
    expert_down,
    routes_ref,
    pair_ref,
    halo,
    padded,
    signal,
    base,
    scores_ref,
    c_ref,
    bt_ref,
    square,
    step_rows,
    cum_rows,
    cum_cols,
    tail_cols,
    reach_ref,
    totals,
    states,
    rows,
    weight_first,
    weight_second,
    total,
    share_out_first,
    share_out_second,
    share_in_first,
    share_in_second,
    mixed_ref,
    plans,
    pick_rows,
    place_back,
    line_rows,
    outgoing,
    arrived,
    result,
    returned,
    sums_out,
    sums_in,
    sum_here,
    local_sem,
    halo_send,
    halo_recv,
    total_send,
    total_recv,
    near_state_send,
    far_state_send,
    state_recv,
    near_rows_send,
    far_rows_send,
    rows_recv,
    line_send,
    inner_send,
    weight_recv,
    share_send,
    share_recv,
    plan_send,
    plan_recv,
    row_send,
    row_recv,
    pick_send,
    pick_recv,
    made_send,
    made_recv,
    sum_send,
    sum_recv,
):
    half = jnp.bfloat16
    full = jnp.float32
    me = lax.axis_index("seq")
    mine = lax.axis_index("grp")
    chips = ring // 2
    chip, core = me // 2, lax.rem(me, 2)
    twin = chip * 2 + 1 - core
    inner = experts // LINES
    line, place = mine // inner, lax.rem(mine, inner)

    row_count, width = gate_ref.shape
    head_count = step_rows.shape[0]
    head_width = width // head_count
    per_tile = LANES // head_width
    state_width = states.shape[2]
    part = width // LINES
    tiles = part // LANES
    weights = (weight_first, weight_second)
    shares_out = (share_out_first, share_out_second)
    shares_in = (share_in_first, share_in_second)
    depth = weight_first.shape[0] // experts
    share = total.shape[1]
    tap_count = taps_ref.shape[0]

    share_column = pl.multiple_of(me * share, LANES)
    locals_ = [
        pltpu.make_async_copy(source, target, local_sem.at[index])
        for index, (source, target) in enumerate(
            (
                *(
                    (
                        weight_hbm.at[:, pl.ds(share_column + start, ref.shape[1])],
                        ref.at[pl.ds(mine * depth, depth)],
                    )
                    for start, ref in zip((0, weight_first.shape[1]), weights)
                ),
                (steps_hbm, steps_ref),
                (rates_hbm, rates_ref),
                (conv_hbm, conv_ref),
                (taps_hbm, taps_ref),
                (routes_hbm, routes_ref),
                (pair_hbm, pair_ref),
                (gate_hbm, gate_ref),
                (norm_hbm, norm_ref),
                (residual_hbm, residual_ref),
                (gain_hbm, gain_ref),
                (expert_gate_hbm, expert_gate),
                (expert_up_hbm, expert_up),
                (expert_down_hbm, expert_down),
            )
        )
    ]
    for copy in locals_[:12]:
        copy.start()

    barrier = pltpu.get_barrier_semaphore()

    def greet(axis, own, count):
        def step(shift, carry):
            pl.semaphore_signal(
                barrier,
                inc=1,
                device_id={axis: lax.rem(own + shift, count)},
                device_id_type=MESH,
            )
            return carry

        lax.fori_loop(1, count, step, 0)

    greet("seq", me, ring)
    greet("grp", mine, experts)


    def far(step):
        return lax.rem(chip + step, chips) * 2 + core

    def source(slot):
        return lax.rem(chip + chips - slot // 2, chips) * 2 + lax.rem(me + slot, 2)

    def ring_copy(slots, sends, part_index, step, near):
        near_send, far_send, recv = sends
        return pltpu.make_async_remote_copy(
            src_ref=slots.at[part_index, 2 * step if near else 0],
            dst_ref=slots.at[part_index, 2 * step + 1 if near else 2 * step],
            send_sem=(near_send if near else far_send).at[part_index, step],
            recv_sem=recv.at[part_index, 2 * step + 1 if near else 2 * step],
            device_id={"seq": twin if near else far(step)},
            device_id_type=MESH,
        )

    state_copy = functools.partial(
        ring_copy, states, (near_state_send, far_state_send, state_recv)
    )
    rows_copy = functools.partial(ring_copy, rows, (near_rows_send, far_rows_send, rows_recv))

    def launch(copy, part_index):
        for step in range(1, chips):
            copy(part_index, step, False).start()
        copy(part_index, 0, True).start()

    def relay(copy, part_index):
        for step in range(1, chips):
            copy(part_index, step, False).wait_recv()
            copy(part_index, step, True).start()

    def drain_ring(copy):
        def body(part_index, carry):
            for step in range(1, chips):
                copy(part_index, step, False).wait_send()
            for step in range(chips):
                copy(part_index, step, True).wait_send()
            return carry

        lax.fori_loop(0, LINES, body, 0)

    def halo_copy(target):
        return pltpu.make_async_remote_copy(
            src_ref=conv_ref.at[pl.ds(row_count - 16, 16)],
            dst_ref=halo,
            send_sem=halo_send.at[0],
            recv_sem=halo_recv.at[0],
            device_id={"seq": target},
            device_id_type=MESH,
        )

    def total_copy(shift):
        return pltpu.make_async_remote_copy(
            src_ref=totals.at[me],
            dst_ref=totals.at[me],
            send_sem=total_send.at[shift],
            recv_sem=total_recv.at[me],
            device_id={"seq": lax.rem(me + shift, ring)},
            device_id_type=MESH,
        )

    def total_arrival(origin):
        return pltpu.make_async_remote_copy(
            src_ref=totals.at[origin],
            dst_ref=totals.at[origin],
            send_sem=total_send.at[0],
            recv_sem=total_recv.at[origin],
            device_id={"seq": twin},
            device_id_type=MESH,
        )

    def weight_copy(stage, block, target, send_sem):
        block_rows = weights[stage].at[pl.ds(block * depth, depth)]
        return pltpu.make_async_remote_copy(
            src_ref=block_rows,
            dst_ref=block_rows,
            send_sem=send_sem,
            recv_sem=weight_recv.at[stage, block],
            device_id={"grp": target},
            device_id_type=MESH,
        )

    def line_copy(stage, at, up):
        step = 1 if up else -1
        return weight_copy(
            stage,
            at * inner + place,
            mine + step * inner,
            line_send.at[stage, at, 0 if up else 1],
        )

    def inner_copy(stage, at, shift):
        return weight_copy(
            stage,
            at * inner + place,
            line * inner + lax.rem(place + shift, inner),
            inner_send.at[stage, at, shift],
        )

    def weight_arrival(stage, block):
        return weight_copy(stage, block, mine, line_send.at[stage, 0, 0])

    def each_weight_copy(do):
        def visit(stage, at):
            @pl.when((at <= line) & (line < LINES - 1))
            def _():
                do(line_copy(stage, at, True))

            @pl.when((at >= line) & (line > 0))
            def _():
                do(line_copy(stage, at, False))

            for shift in range(1, inner):
                do(inner_copy(stage, at, shift))

        return visit

    start_weight = each_weight_copy(lambda copy: copy.start())
    drain_weight = each_weight_copy(lambda copy: copy.wait_send())

    def relay_weight(stage, step):
        for at in (line - step, line + step):

            @pl.when((at >= 0) & (at < LINES))
            def _():
                weight_arrival(stage, at * inner + place).wait_recv()
                start_weight(stage, at)


    down = lax.broadcasted_iota(jnp.int32, (row_count, row_count), 0)
    across = lax.broadcasted_iota(jnp.int32, (row_count, row_count), 1)
    for index in (2, 3):
        locals_[index].wait()
    rate_square = jnp.where(
        down[:head_count, :head_count] == across[:head_count, :head_count], rates_ref[...], 0.0
    )
    rate = jnp.exp(jnp.sum(rate_square, axis=1, keepdims=True))
    raw = steps_ref[...]
    step_size = jnp.maximum(raw, 0.0) + jnp.log1p(jnp.exp(-jnp.abs(raw)))
    step_rows[...] = step_size
    log_decay = -step_size * rate
    cumulative = jnp.dot(
        log_decay,
        (down <= across).astype(full),
        preferred_element_type=full,
        precision=lax.Precision.HIGHEST,
    )
    cum_rows[...] = cumulative
    square[...] = jnp.zeros_like(square)
    square[:head_count, :] = cumulative
    cum_cols[...] = square[...].T
    totals[me] = jnp.broadcast_to(cum_cols[row_count - 1 : row_count, :], totals.shape[1:])
    square[:head_count, :] = jnp.exp(cumulative[:, row_count - 1 : row_count] - cumulative) * step_size
    tail_cols[...] = square[...].T
    for index in (0, 1, 4):
        locals_[index].wait()
    pl.semaphore_wait(barrier, ring - 1 + experts - 1)
    start_weight(0, line)
    for copy in locals_[12:]:
        copy.start()

    @pl.when(me < ring - 1)
    def _():
        halo_copy(me + 1).start()

    for shift in range(1, ring):
        total_copy(shift).start()
    for index in (5, 6, 7):
        locals_[index].wait()

    capacity = 4 * row_count // experts
    names = lax.broadcasted_iota(jnp.int32, (experts, row_count), 0)
    members = [(names == routes_ref[k : k + 1, :]).astype(full) for k in range(2)]
    rank = jnp.dot(
        (members[0] + members[1]).astype(half),
        (down < across).astype(half),
        preferred_element_type=full,
    ) + (names * capacity).astype(full)
    plans[mine] = jnp.zeros_like(plans[mine])
    for k in range(2):
        plans[mine, k : k + 1, :] = jnp.sum(members[k] * rank, axis=0, keepdims=True)
        plans[mine, 2 + k : 3 + k, :] = pair_ref[k : k + 1, :]

    def plan_copy(shift):
        return pltpu.make_async_remote_copy(
            src_ref=plans.at[mine],
            dst_ref=plans.at[mine],
            send_sem=plan_send.at[shift],
            recv_sem=plan_recv.at[mine],
            device_id={"grp": lax.rem(mine + shift, experts)},
            device_id_type=MESH,
        )

    def plan_arrival(origin):
        return pltpu.make_async_remote_copy(
            src_ref=plans.at[origin],
            dst_ref=plans.at[origin],
            send_sem=plan_send.at[0],
            recv_sem=plan_recv.at[origin],
            device_id={"grp": lax.rem(mine + 1, experts)},
            device_id_type=MESH,
        )

    def send_plan(shift, carry):
        plan_copy(shift).start()
        return carry

    lax.fori_loop(1, experts, send_plan, 0)

    @pl.when(me > 0)
    def _():
        halo_copy(me).wait_recv()

    first_half = lax.broadcasted_iota(jnp.int32, (row_count, LANES), 1) < head_width
    offset = 8

    def convolve(column, padded):
        columns = pl.ds(column, LANES)
        before = halo[:, columns].astype(full)[16 - offset :]
        padded[:offset, :] = jnp.where(me > 0, before, 0.0)
        padded[offset:, :] = conv_ref[:, columns].astype(full)
        taps = taps_ref[:, columns]
        start = offset - tap_count + 1
        summed = taps[0:1] * padded[start : start + row_count, :]
        for k in range(1, tap_count):
            summed = summed + taps[k : k + 1] * padded[start + k : start + k + row_count, :]
        return (summed * jax.nn.sigmoid(summed)).astype(half)

    def by_head(columns_of_heads, pair):
        shifted = pltpu.roll(columns_of_heads, lax.rem(LANES - per_tile * pair, LANES), axis=1)
        return shifted[:, 0:1], shifted[:, 1:2]

    bc = convolve(width, padded.at[0]).astype(full)
    bt_ref[...] = bc.T[:state_width].astype(half)
    c_part = pltpu.roll(bc, LANES - state_width, axis=1)[:, :state_width].astype(half)
    c_ref[...] = c_part
    scores_ref[...] = jnp.dot(c_part, bt_ref[...], preferred_element_type=full)

    def take_in(part_index, carry):
        def tile(index, carry):
            pair = part_index * tiles + index
            column = pl.multiple_of(pair * LANES, LANES)
            x = convolve(column, padded.at[index])
            signal[:, pl.ds(column, LANES)] = x
            left, right = by_head(tail_cols[...], pair)
            scaled = (x.astype(full) * jnp.where(first_half, left, right)).astype(half)
            states[part_index, 0, :, pl.ds(pl.multiple_of(index * LANES, LANES), LANES)] = jnp.dot(
                bt_ref[...], scaled, preferred_element_type=full
            ).astype(half)
            return carry

        lax.fori_loop(0, tiles, tile, 0, unroll=True)
        launch(state_copy, part_index)
        return carry

    lax.fori_loop(0, LINES, take_in, 0)

    def within(part_index, carry):
        def tile(index, carry):
            pair = part_index * tiles + index
            column = pl.multiple_of(pair * LANES, LANES)
            cum = by_head(cum_cols[...], pair)
            mixing = []
            for turn in range(2):
                head = per_tile * pair + turn
                gap = cum[turn] - cum_rows[pl.ds(head, 1), :]
                decay = jnp.exp(jnp.where(down >= across, gap, -1e30))
                mixing.append(scores_ref[...] * decay * step_rows[pl.ds(head, 1), :])
            x = signal[:, pl.ds(column, LANES)].astype(full)
            stacked = jnp.concatenate(
                [jnp.where(first_half, x, 0.0), jnp.where(first_half, 0.0, x)], axis=0
            ).astype(half)
            skip = jnp.where(first_half, skip_ref[per_tile * pair], skip_ref[per_tile * pair + 1])
            base[:, pl.ds(column, LANES)] = (
                jnp.dot(
                    jnp.concatenate(mixing, axis=1).astype(half), stacked, preferred_element_type=full
                )
                + skip * x
            )
            return carry

        lax.fori_loop(0, tiles, tile, 0, unroll=True)
        relay(state_copy, part_index)
        return carry

    lax.fori_loop(0, 1, within, 0)
    relay_weight(0, 1)
    lax.fori_loop(1, LINES, within, 0)

    for shift in range(1, ring):
        total_arrival(lax.rem(me + shift, ring)).wait_recv()
    for slot in range(1, ring):
        origin = source(slot)
        passed = jnp.zeros((1, LANES), full)
        for between in range(ring):
            passed = passed + jnp.where(
                (between > origin) & (between < me), totals[between, 0:1, :], 0.0
            )
        reach_ref[slot : slot + 1, :] = jnp.where(origin < me, jnp.exp(passed), 0.0)
    reach_ref[0:1, :] = jnp.zeros((1, LANES), full)
    for index in (8, 9):
        locals_[index].wait()

    def gather_in(part_index, squares):
        for step in range(chips):
            state_copy(part_index, step, True).wait_recv()

        def tile(index, squares):
            pair = part_index * tiles + index
            column = pl.multiple_of(pair * LANES, LANES)
            columns = pl.ds(column, LANES)
            local = pl.ds(pl.multiple_of(index * LANES, LANES), LANES)
            left, right = by_head(reach_ref[...], pair)
            reach = jnp.where(first_half[: reach_ref.shape[0]], left, right)
            entering = jnp.zeros((state_width, LANES), full)
            for slot in range(1, ring):
                entering = entering + reach[slot : slot + 1] * states[
                    part_index, slot, :, local
                ].astype(full)
            carried = jnp.dot(c_ref[...], entering.astype(half), preferred_element_type=full)
            left, right = by_head(cum_cols[...], pair)
            fade = jnp.exp(jnp.where(first_half, left, right))
            gate = gate_ref[:, columns].astype(full)
            value = (base[:, columns] + carried * fade) * (gate * jax.nn.sigmoid(gate))
            rows[part_index, 0, :, local] = (value * norm_ref[pl.ds(pair, 1), :]).astype(half)
            return squares + jnp.sum(value * value, axis=1, keepdims=True)

        squares = lax.fori_loop(0, tiles, tile, squares, unroll=True)
        launch(rows_copy, part_index)
        return squares

    squares = lax.fori_loop(0, LINES, gather_in, jnp.zeros((row_count, 1), full))
    row_scale = lax.rsqrt(squares * (1.0 / width) + EPSILON)

    relay_weight(0, 2)
    start_weight(1, line)
    relay(rows_copy, 0)
    relay_weight(0, 3)
    relay(rows_copy, 1)
    relay(rows_copy, 2)
    relay_weight(1, 1)
    relay_weight(1, 2)
    relay(rows_copy, 3)
    relay_weight(1, 3)

    def rows_arrived(part_index, carry):
        for step in range(chips):
            rows_copy(part_index, step, True).wait_recv()
        return carry

    lax.fori_loop(0, LINES, rows_arrived, 0)

    def share_copy(stage, slot):
        return pltpu.make_async_remote_copy(
            src_ref=shares_out[stage].at[slot],
            dst_ref=shares_in[stage].at[me],
            send_sem=share_send.at[stage, slot],
            recv_sem=share_recv.at[stage, me],
            device_id={"seq": source(slot)},
            device_id_type=MESH,
        )

    def share_arrival(stage, column):
        return pltpu.make_async_remote_copy(
            src_ref=shares_out[stage].at[0],
            dst_ref=shares_in[stage].at[column],
            send_sem=share_send.at[stage, 0],
            recv_sem=share_recv.at[stage, column],
            device_id={"seq": source(1)},
            device_id_type=MESH,
        )

    starts = (0, weight_first.shape[1])
    for stage in range(STAGES):
        breadth = weights[stage].shape[1]
        columns_here = slice(starts[stage], starts[stage] + breadth)

        def project(index, carry):
            step = (index + 1) // 2
            at = line + jnp.where(lax.rem(index, 2) == 0, step, -step)

            @pl.when((at >= 0) & (at < LINES))
            def _():
                for shift in range(1, inner):
                    weight_arrival(stage, at * inner + lax.rem(place + shift, inner)).wait_recv()
                product = jnp.dot(
                    rows[at].reshape(ring * row_count, part),
                    weights[stage][pl.ds(pl.multiple_of(at * part, part), part), :],
                    preferred_element_type=full,
                )
                total[:, columns_here] += product

            return carry

        total[:, columns_here] = jnp.zeros((ring * row_count, breadth), full)
        lax.fori_loop(0, 2 * LINES - 1, project, 0)

        def hand_out(index, carry):
            slot = ring - 1 - index
            shares_out[stage][slot] = total[
                pl.ds(pl.multiple_of(slot * row_count, row_count), row_count), columns_here
            ].astype(half)

            @pl.when(slot > 0)
            def _():
                share_copy(stage, slot).start()

            return carry

        lax.fori_loop(0, ring, hand_out, 0)
        shares_in[stage][me] = shares_out[stage][0]

    for index in (10, 11):
        locals_[index].wait()
    squares = jnp.zeros((row_count, 1), full)
    for stage in range(STAGES):
        breadth = weights[stage].shape[1]

        def mix(index, squares):
            @pl.when(index != me)
            def _():
                share_arrival(stage, index).wait_recv()

            column = pl.multiple_of(index * share + starts[stage], LANES)
            values = (
                residual_ref[:, pl.ds(column, breadth)].astype(full)
                + row_scale * shares_in[stage][index].astype(full)
            ).astype(half)
            mixed_ref[:, pl.ds(column, breadth)] = values
            wide = values.astype(full)
            return squares + jnp.sum(wide * wide, axis=1, keepdims=True)

        squares = lax.fori_loop(0, ring, mix, squares)
    scale = lax.rsqrt(squares * (1.0 / width) + EPSILON)
    for tile in range(width // LANES):
        local = tile % tiles * LANES
        line_rows[line, tile // tiles, :, local : local + LANES] = (
            mixed_ref[:, tile * LANES : (tile + 1) * LANES].astype(full)
            * scale
            * gain_ref[tile : tile + 1, :]
        ).astype(half)

    def row_copy(at, up, index):
        return pltpu.make_async_remote_copy(
            src_ref=line_rows.at[at, index],
            dst_ref=line_rows.at[at, index],
            send_sem=row_send.at[at, 0 if up else 1, index],
            recv_sem=row_recv.at[at, index],
            device_id={"grp": mine + (inner if up else -inner)},
            device_id_type=MESH,
        )

    def slots_of(owner):
        return pl.ds(pl.multiple_of(owner * capacity, capacity), capacity)

    def across_copy(source, target, sends, recvs, at, shift, index):
        other = lax.rem(place + shift, inner)
        return pltpu.make_async_remote_copy(
            src_ref=source.at[at, index, slots_of(other)],
            dst_ref=target.at[at, index, slots_of(place)],
            send_sem=sends.at[at, shift, index],
            recv_sem=recvs.at[at, place, index],
            device_id={"grp": line * inner + other},
            device_id_type=MESH,
        )

    def across_arrival(source, target, sends, recvs, at, shift, index):
        other = lax.rem(place + shift, inner)
        return pltpu.make_async_remote_copy(
            src_ref=source.at[at, index, slots_of(other)],
            dst_ref=target.at[at, index, slots_of(other)],
            send_sem=sends.at[at, shift, index],
            recv_sem=recvs.at[at, other, index],
            device_id={"grp": line * inner + other},
            device_id_type=MESH,
        )

    pick_parts = (outgoing, arrived, pick_send, pick_recv)
    made_parts = (result, returned, made_send, made_recv)

    sum_rows = row_count // SPLIT
    sum_pieces = SPLIT * LINES

    def sum_part(ref, index):
        return ref.at[index // SPLIT, pl.ds(pl.multiple_of(lax.rem(index, SPLIT) * sum_rows, 16), sum_rows)]

    def sum_copy(to, up, index):
        way = 0 if up else 1
        return pltpu.make_async_remote_copy(
            src_ref=sum_part(sums_out.at[to], index),
            dst_ref=sum_part(sums_in.at[way, to], index),
            send_sem=sum_send.at[to, index],
            recv_sem=sum_recv.at[way, to, index],
            device_id={"grp": mine + (inner if up else -inner)},
            device_id_type=MESH,
        )

    def sum_arrival(to, up, index):
        way = 0 if up else 1
        return pltpu.make_async_remote_copy(
            src_ref=sum_part(sums_out.at[to], index),
            dst_ref=sum_part(sums_in.at[way, to], index),
            send_sem=sum_send.at[to, index],
            recv_sem=sum_recv.at[way, to, index],
            device_id={"grp": mine},
            device_id_type=MESH,
        )

    def take_plan(shift, carry):
        plan_arrival(lax.rem(mine + shift, experts)).wait_recv()
        return carry

    lax.fori_loop(1, experts, take_plan, 0)
    slot_count = inner * capacity
    slot_ids = lax.broadcasted_iota(jnp.int32, (slot_count, row_count), 0)

    at_end = (line == 0) | (line == LINES - 1)

    def forward(at, up, index):
        @pl.when((at <= line) & (line < LINES - 1) if up else (at >= line) & (line > 0))
        def _():
            row_copy(at, up, index).start()

    def plan_rows(at):
        plan = plans[at * inner + place]
        slot_of = (slot_ids + line * slot_count).astype(full)
        picks = jnp.where(plan[0:1] == slot_of, 1.0, 0.0) + jnp.where(plan[1:2] == slot_of, 1.0, 0.0)
        place_back[at] = picks.T.astype(half)
        pick_rows[at] = picks.astype(half)

    def take_piece(at, step, index):
        @pl.when(step > 0)
        def _():
            row_copy(at, True, index).wait_recv()

        forward(at, True, index)
        forward(at, False, index)
        outgoing[at, index] = jnp.dot(
            pick_rows[at], line_rows[at, index], preferred_element_type=full
        ).astype(half)
        for shift in range(1, inner):
            across_copy(*pick_parts, at, shift, index).start()
        arrived[at, index, slots_of(place)] = outgoing[at, index, slots_of(place)]

    def made_arrived(to, index):
        for shift in range(1, inner):
            across_arrival(*made_parts, to, shift, index).wait_recv()

    def send_sums(to, up, index):
        way = 0 if up else 1
        column = index // SPLIT
        some = pl.ds(pl.multiple_of(lax.rem(index, SPLIT) * sum_rows, 16), sum_rows)

        @pl.when(lax.rem(index, SPLIT) == 0)
        def _():
            made_arrived(to, column)

        share = jnp.dot(place_back[to, some], returned[to, column], preferred_element_type=full)
        behind = (line > 0) if up else (line < LINES - 1)

        @pl.when(behind)
        def _():
            sum_arrival(to, up, index).wait_recv()
            sums_out[to, column, some] = (share + sums_in[way, to, column, some].astype(full)).astype(half)

        @pl.when(jnp.logical_not(behind))
        def _():
            sums_out[to, column, some] = share.astype(half)

        sum_copy(to, up, index).start()

    def run_expert(at):
        scales = []
        own_ids = lax.broadcasted_iota(jnp.int32, (capacity, row_count), 0) + mine * capacity
        for origin in range(inner):
            plan = plans[at * inner + origin]
            own_slots = own_ids.astype(full)
            scales.append(
                jnp.sum(
                    jnp.where(plan[0:1] == own_slots, plan[2:3], 0.0)
                    + jnp.where(plan[1:2] == own_slots, plan[3:4], 0.0),
                    axis=1,
                    keepdims=True,
                )
            )
        scale = jnp.concatenate(scales, axis=0)
        gate_part = jnp.zeros((slot_count, expert_gate.shape[1]), full)
        up_part = gate_part
        for index in range(LINES):
            for shift in range(1, inner):
                across_arrival(*pick_parts, at, shift, index).wait_recv()
            rows_here = arrived[at, index]
            depth_here = slice(index * part, (index + 1) * part)
            gate_part = gate_part + jnp.dot(
                rows_here, expert_gate[depth_here, :], preferred_element_type=full
            )
            up_part = up_part + jnp.dot(
                rows_here, expert_up[depth_here, :], preferred_element_type=full
            )
        hidden = (gate_part * jax.nn.sigmoid(gate_part) * up_part).astype(half)
        for index in range(LINES):
            made = jnp.dot(
                hidden, expert_down[:, index * part : (index + 1) * part], preferred_element_type=full
            )
            result[at, index] = (made * scale).astype(half)
            for shift in range(1, inner):
                across_copy(*made_parts, at, shift, index).start()
            returned[at, index, slots_of(place)] = result[at, index, slots_of(place)]

    def plan_block(at, carry):
        plan_rows(at)
        return carry

    lax.fori_loop(0, LINES, plan_block, 0)

    def round_trip(step, carry):
        def take(turn, carry):
            ahead, index = step + turn // LINES, lax.rem(turn, LINES)
            for at, wanted in ((line - ahead, True), (line + ahead, ahead > 0)):

                @pl.when((at >= 0) & (at < LINES) & wanted)
                def _():
                    take_piece(at, ahead, index)

            return carry

        steps_here = jnp.where(at_end | (step == 0), 1, jnp.where(step == 1, LINES - 2, 0))
        lax.fori_loop(0, steps_here * LINES, take, 0)

        @pl.when(step == 0)
        def _():
            for copy in locals_[12:]:
                copy.wait()

        def turn(way, carry):
            at = line + jnp.where(line >= LINES // 2, 1, -1) * jnp.where(way == 0, -step, step)

            @pl.when((at >= 0) & (at < LINES) & ((way == 0) | (step > 0)))
            def _():
                run_expert(at)

            return carry

        lax.fori_loop(0, 2, turn, 0)

        lag = jnp.where(line >= LINES // 2, 0, 2)

        def pass_on(index, carry):
            down_index, up_index = index - lag, index - 2 + lag

            between = step > 0

            @pl.when(between & (LINES - 1 - step < line) & (down_index >= 0) & (down_index < sum_pieces))
            def _():
                send_sums(LINES - 1 - step, False, down_index)

            @pl.when(between & (step > line) & (up_index >= 0) & (up_index < sum_pieces))
            def _():
                send_sums(step, True, up_index)

            return carry

        lax.fori_loop(0, sum_pieces + 2, pass_on, 0)
        return carry

    lax.fori_loop(0, LINES, round_trip, 0)

    for index in range(LINES):
        columns = slice(index * part, (index + 1) * part)
        made_arrived(line, index)
        sum_here[...] = mixed_ref[:, columns].astype(full) + jnp.dot(
            place_back[line], returned[line, index], preferred_element_type=full
        )

        @pl.when(line > 0)
        def _():
            for turn in range(SPLIT):
                sum_arrival(line, True, index * SPLIT + turn).wait_recv()
            sum_here[...] += sums_in[0, line, index].astype(full)

        @pl.when(line < LINES - 1)
        def _():
            for turn in range(SPLIT):
                sum_arrival(line, False, index * SPLIT + turn).wait_recv()
            sum_here[...] += sums_in[1, line, index].astype(full)

        out_ref[:, columns] = sum_here[...].astype(half)

    @pl.when(me < ring - 1)
    def _():
        halo_copy(me + 1).wait_send()

    for shift in range(1, ring):
        total_copy(shift).wait_send()
        for stage in range(STAGES):
            share_copy(stage, shift).wait_send()

    def sent_plan(shift, carry):
        plan_copy(shift).wait_send()
        return carry

    lax.fori_loop(1, experts, sent_plan, 0)
    drain_ring(state_copy)
    drain_ring(rows_copy)

    def weight_left(at, carry):
        for stage in range(STAGES):
            drain_weight(stage, at)
        return carry

    lax.fori_loop(0, LINES, weight_left, 0)

    def drain(at, carry):
        def piece(index, carry):
            @pl.when((at <= line) & (line < LINES - 1))
            def _():
                row_copy(at, True, index).wait_send()

            @pl.when((at >= line) & (line > 0))
            def _():
                row_copy(at, False, index).wait_send()

            for shift in range(1, inner):
                across_copy(*pick_parts, at, shift, index).wait_send()
                across_copy(*made_parts, at, shift, index).wait_send()

            return carry

        def sum_piece(index, carry):
            @pl.when(at != line)
            def _():
                sum_copy(at, True, index).wait_send()

            return carry

        lax.fori_loop(0, sum_pieces, sum_piece, 0)

        lax.fori_loop(0, LINES, piece, 0)
        return carry

    lax.fori_loop(0, LINES, drain, 0)


def on_device(
    conv_input,
    conv_weight,
    step_raw,
    rate_log,
    skip_gain,
    gate_input,
    norm_gain,
    out_weight,
    residual,
    moe_gain,
    w_gate,
    w_up,
    w_down,
    routes,
    route_weights,
):
    half = jnp.bfloat16
    full = jnp.float32
    ring = lax.axis_size("seq")
    experts = lax.axis_size("grp")
    share = -(-out_weight.shape[1] // (ring * LANES)) * LANES
    extra = ring * share - out_weight.shape[1]
    row_count, channel_count = conv_input.shape[1:]
    tap_count = conv_weight.shape[0]
    head_count = rate_log.shape[0]
    inner_width = gate_input.shape[2]
    state_width = (channel_count - inner_width) // 2
    model_width = residual.shape[2]
    hidden_width = w_gate.shape[2]
    capacity = 4 * row_count // experts
    part = inner_width // LINES
    padded_residual, padded_weight = residual[0], out_weight
    if extra:
        padded_residual = jnp.pad(padded_residual, ((0, 0), (0, extra)))
        padded_weight = jnp.pad(padded_weight, ((0, 0), (0, extra)))
    vmem = pl.BlockSpec(memory_space=pltpu.VMEM)
    smem = pl.BlockSpec(memory_space=pltpu.SMEM)
    anywhere = pl.BlockSpec(memory_space=pl.ANY)
    inner = experts // LINES
    slot_count = inner * capacity
    row_slab = pltpu.VMEM((LINES, LINES, row_count, part), half)
    slot_slab = pltpu.VMEM((LINES, LINES, slot_count, part), half)
    pieces = [pltpu.VMEM((ring, row_count, breadth), half) for breadth in column_groups(share)]
    square = pltpu.VMEM((row_count, LANES), full)
    dma = pltpu.SemaphoreType.DMA
    layer_out = pl.pallas_call(
        functools.partial(layer_kernel, ring, experts),
        out_shape=jax.ShapeDtypeStruct((row_count, model_width), half),
        in_specs=[anywhere] * 4 + [smem] + [anywhere] * 10,
        out_specs=vmem,
        scratch_shapes=[
            pltpu.VMEM((row_count, channel_count), half),
            pltpu.VMEM((tap_count, channel_count), full),
            pltpu.VMEM((head_count, row_count), full),
            pltpu.VMEM((1, head_count), full),
            pltpu.VMEM((row_count, inner_width), half),
            pltpu.VMEM((inner_width // LANES, LANES), full),
            pltpu.VMEM((row_count, ring * share), half),
            pltpu.VMEM((model_width // LANES, LANES), full),
            pltpu.VMEM((model_width, hidden_width), half),
            pltpu.VMEM((model_width, hidden_width), half),
            pltpu.VMEM((hidden_width, model_width), half),
            pltpu.VMEM((2, row_count), jnp.int32),
            pltpu.VMEM((2, row_count), full),
            pltpu.VMEM((16, channel_count), half),
            pltpu.VMEM((part // LANES, row_count + 8, LANES), full),
            pltpu.VMEM((row_count, inner_width), half),
            pltpu.VMEM((row_count, inner_width), full),
            square,
            pltpu.VMEM((row_count, state_width), half),
            pltpu.VMEM((state_width, row_count), half),
            square,
            pltpu.VMEM((head_count, row_count), full),
            pltpu.VMEM((head_count, row_count), full),
            square,
            square,
            pltpu.VMEM((8, LANES), full),
            pltpu.VMEM((ring, 8, LANES), full),
            pltpu.VMEM((LINES, ring, state_width, part), half),
            pltpu.VMEM((LINES, ring, row_count, part), half),
            *[pltpu.VMEM((inner_width, breadth), half) for breadth in column_groups(share)],
            pltpu.VMEM((ring * row_count, share), full),
            *pieces,
            *pieces,
            pltpu.VMEM((row_count, ring * share), half),
            pltpu.VMEM((experts, 8, row_count), full),
            pltpu.VMEM((LINES, slot_count, row_count), half),
            pltpu.VMEM((LINES, row_count, slot_count), half),
            row_slab,
            slot_slab,
            slot_slab,
            slot_slab,
            slot_slab,
            row_slab,
            pltpu.VMEM((2, LINES, LINES, row_count, part), half),
            pltpu.VMEM((row_count, part), full),
            dma((15,)),
            dma((1,)),
            dma((1,)),
            dma((ring,)),
            dma((ring,)),
            dma((LINES, ring // 2)),
            dma((LINES, ring // 2)),
            dma((LINES, ring)),
            dma((LINES, ring // 2)),
            dma((LINES, ring // 2)),
            dma((LINES, ring)),
            dma((STAGES, LINES, 2)),
            dma((STAGES, LINES, experts // LINES)),
            dma((STAGES, experts)),
            dma((STAGES, ring)),
            dma((STAGES, ring)),
            dma((experts,)),
            dma((experts,)),
            dma((LINES, 2, LINES)),
            dma((LINES, LINES)),
            dma((LINES, inner, LINES)),
            dma((LINES, inner, LINES)),
            dma((LINES, inner, LINES)),
            dma((LINES, inner, LINES)),
            dma((LINES, SPLIT * LINES)),
            dma((2, LINES, SPLIT * LINES)),
        ],
        compiler_params=pltpu.CompilerParams(
            collective_id=0, has_side_effects=True, vmem_limit_bytes=56 * 1024 * 1024
        ),
        cost_estimate=pl.CostEstimate(
            flops=6 * 1024 * 1024 * 1024, bytes_accessed=64 * 1024 * 1024, transcendentals=0
        ),
    )(
        conv_input[0],
        conv_weight,
        step_raw[0].T,
        rate_log[None, :],
        skip_gain,
        gate_input[0],
        norm_gain.reshape(-1, LANES),
        padded_weight,
        padded_residual,
        moe_gain.reshape(-1, LANES),
        w_gate[0],
        w_up[0],
        w_down[0],
        routes[0].T,
        route_weights[0].T,
    )
    return layer_out[None]


def solution(mesh):
    in_specs = (
        P("grp", "seq", None),
        P(),
        P("grp", "seq", None),
        P(),
        P(),
        P("grp", "seq", None),
        P(),
        P("grp", None),
        P("grp", "seq", None),
        P(),
        P("grp", None, None),
        P("grp", None, None),
        P("grp", None, None),
        P("grp", "seq", None),
        P("grp", "seq", None),
    )
    out_specs = P("grp", "seq", None)
    return jax.shard_map(
        on_device, mesh=mesh, in_specs=in_specs, out_specs=out_specs, check_vma=False
    )
```

```python
import functools

import jax
import jax.numpy as jnp
from jax import lax
from jax.experimental import pallas as pl
from jax.experimental.pallas import tpu as pltpu
from jax.sharding import PartitionSpec as P

EPSILON = 1e-05
LANES = 128
LINES = 4
SPLIT = 1
STAGES = 2
MESH = pl.DeviceIdType.MESH


def column_groups(share):
    tiles = share // LANES
    first = max(1, (tiles * 4) // 5)
    return [first * LANES, (tiles - first) * LANES]


def layer_kernel(
    ring,
    experts,
    conv_hbm,
    taps_hbm,
    steps_hbm,
    rates_hbm,
    skip_ref,
    gate_hbm,
    norm_hbm,
    weight_hbm,
    residual_hbm,
    gain_hbm,
    expert_gate_hbm,
    expert_up_hbm,
    expert_down_hbm,
    routes_hbm,
    pair_hbm,
    out_ref,
    conv_ref,
    taps_ref,
    steps_ref,
    rates_ref,
    gate_ref,
    norm_ref,
    residual_ref,
    gain_ref,
    expert_gate,
    expert_up,
    expert_down,
    routes_ref,
    pair_ref,
    halo,
    padded,
    signal,
    base,
    scores_ref,
    c_ref,
    bt_ref,
    square,
    step_rows,
    cum_rows,
    cum_cols,
    tail_cols,
    reach_ref,
    totals,
    states,
    rows,
    weight_first,
    weight_second,
    total,
    share_out_first,
    share_out_second,
    share_in_first,
    share_in_second,
    mixed_ref,
    plans,
    pick_rows,
    place_back,
    line_rows,
    outgoing,
    arrived,
    result,
    returned,
    sums_out,
    sums_in,
    sum_here,
    local_sem,
    halo_send,
    halo_recv,
    total_send,
    total_recv,
    near_state_send,
    far_state_send,
    state_recv,
    near_rows_send,
    far_rows_send,
    rows_recv,
    line_send,
    inner_send,
    weight_recv,
    share_send,
    share_recv,
    plan_send,
    plan_recv,
    row_send,
    row_recv,
    pick_send,
    pick_recv,
    made_send,
    made_recv,
    sum_send,
    sum_recv,
):
    half = jnp.bfloat16
    full = jnp.float32
    me = lax.axis_index("seq")
    mine = lax.axis_index("grp")
    chips = ring // 2
    chip, core = me // 2, lax.rem(me, 2)
    twin = chip * 2 + 1 - core
    inner = experts // LINES
    line, place = mine // inner, lax.rem(mine, inner)

    row_count, width = gate_ref.shape
    head_count = step_rows.shape[0]
    head_width = width // head_count
    per_tile = LANES // head_width
    state_width = states.shape[2]
    part = width // LINES
    tiles = part // LANES
    weights = (weight_first, weight_second)
    shares_out = (share_out_first, share_out_second)
    shares_in = (share_in_first, share_in_second)
    depth = weight_first.shape[0] // experts
    share = total.shape[1]
    tap_count = taps_ref.shape[0]

    share_column = pl.multiple_of(me * share, LANES)
    locals_ = [
        pltpu.make_async_copy(source, target, local_sem.at[index])
        for index, (source, target) in enumerate(
            (
                *(
                    (
                        weight_hbm.at[:, pl.ds(share_column + start, ref.shape[1])],
                        ref.at[pl.ds(mine * depth, depth)],
                    )
                    for start, ref in zip((0, weight_first.shape[1]), weights)
                ),
                (steps_hbm, steps_ref),
                (rates_hbm, rates_ref),
                (conv_hbm, conv_ref),
                (taps_hbm, taps_ref),
                (routes_hbm, routes_ref),
                (pair_hbm, pair_ref),
                (gate_hbm, gate_ref),
                (norm_hbm, norm_ref),
                (residual_hbm, residual_ref),
                (gain_hbm, gain_ref),
                (expert_gate_hbm, expert_gate),
                (expert_up_hbm, expert_up),
                (expert_down_hbm, expert_down),
            )
        )
    ]
    for copy in locals_[:12]:
        copy.start()

    barrier = pltpu.get_barrier_semaphore()

    def greet(axis, own, count):
        def step(shift, carry):
            pl.semaphore_signal(
                barrier,
                inc=1,
                device_id={axis: lax.rem(own + shift, count)},
                device_id_type=MESH,
            )
            return carry

        lax.fori_loop(1, count, step, 0)

    greet("seq", me, ring)
    greet("grp", mine, experts)


    def far(step):
        return lax.rem(chip + step, chips) * 2 + core

    def source(slot):
        return lax.rem(chip + chips - slot // 2, chips) * 2 + lax.rem(me + slot, 2)

    def ring_copy(slots, sends, part_index, step, near):
        near_send, far_send, recv = sends
        return pltpu.make_async_remote_copy(
            src_ref=slots.at[part_index, 2 * step if near else 0],
            dst_ref=slots.at[part_index, 2 * step + 1 if near else 2 * step],
            send_sem=(near_send if near else far_send).at[part_index, step],
            recv_sem=recv.at[part_index, 2 * step + 1 if near else 2 * step],
            device_id={"seq": twin if near else far(step)},
            device_id_type=MESH,
        )

    state_copy = functools.partial(
        ring_copy, states, (near_state_send, far_state_send, state_recv)
    )
    rows_copy = functools.partial(ring_copy, rows, (near_rows_send, far_rows_send, rows_recv))

    def launch(copy, part_index):
        for step in range(1, chips):
            copy(part_index, step, False).start()
        copy(part_index, 0, True).start()

    def relay(copy, part_index):
        for step in range(1, chips):
            copy(part_index, step, False).wait_recv()
            copy(part_index, step, True).start()

    def drain_ring(copy):
        def body(part_index, carry):
            for step in range(1, chips):
                copy(part_index, step, False).wait_send()
            for step in range(chips):
                copy(part_index, step, True).wait_send()
            return carry

        lax.fori_loop(0, LINES, body, 0)

    def halo_copy(target):
        return pltpu.make_async_remote_copy(
            src_ref=conv_ref.at[pl.ds(row_count - 16, 16)],
            dst_ref=halo,
            send_sem=halo_send.at[0],
            recv_sem=halo_recv.at[0],
            device_id={"seq": target},
            device_id_type=MESH,
        )

    def total_copy(shift):
        return pltpu.make_async_remote_copy(
            src_ref=totals.at[me],
            dst_ref=totals.at[me],
            send_sem=total_send.at[shift],
            recv_sem=total_recv.at[me],
            device_id={"seq": lax.rem(me + shift, ring)},
            device_id_type=MESH,
        )

    def total_arrival(origin):
        return pltpu.make_async_remote_copy(
            src_ref=totals.at[origin],
            dst_ref=totals.at[origin],
            send_sem=total_send.at[0],
            recv_sem=total_recv.at[origin],
            device_id={"seq": twin},
            device_id_type=MESH,
        )

    def weight_copy(stage, block, target, send_sem):
        block_rows = weights[stage].at[pl.ds(block * depth, depth)]
        return pltpu.make_async_remote_copy(
            src_ref=block_rows,
            dst_ref=block_rows,
            send_sem=send_sem,
            recv_sem=weight_recv.at[stage, block],
            device_id={"grp": target},
            device_id_type=MESH,
        )

    def line_copy(stage, at, up):
        step = 1 if up else -1
        return weight_copy(
            stage,
            at * inner + place,
            mine + step * inner,
            line_send.at[stage, at, 0 if up else 1],
        )

    def inner_copy(stage, at, shift):
        return weight_copy(
            stage,
            at * inner + place,
            line * inner + lax.rem(place + shift, inner),
            inner_send.at[stage, at, shift],
        )

    def weight_arrival(stage, block):
        return weight_copy(stage, block, mine, line_send.at[stage, 0, 0])

    def each_weight_copy(do):
        def visit(stage, at):
            @pl.when((at <= line) & (line < LINES - 1))
            def _():
                do(line_copy(stage, at, True))

            @pl.when((at >= line) & (line > 0))
            def _():
                do(line_copy(stage, at, False))

            for shift in range(1, inner):
                do(inner_copy(stage, at, shift))

        return visit

    start_weight = each_weight_copy(lambda copy: copy.start())
    drain_weight = each_weight_copy(lambda copy: copy.wait_send())

    def relay_weight(stage, step):
        for at in (line - step, line + step):

            @pl.when((at >= 0) & (at < LINES))
            def _():
                weight_arrival(stage, at * inner + place).wait_recv()
                start_weight(stage, at)


    down = lax.broadcasted_iota(jnp.int32, (row_count, row_count), 0)
    across = lax.broadcasted_iota(jnp.int32, (row_count, row_count), 1)
    for index in (2, 3):
        locals_[index].wait()
    rate_square = jnp.where(
        down[:head_count, :head_count] == across[:head_count, :head_count], rates_ref[...], 0.0
    )
    rate = jnp.exp(jnp.sum(rate_square, axis=1, keepdims=True))
    raw = steps_ref[...]
    step_size = jnp.maximum(raw, 0.0) + jnp.log1p(jnp.exp(-jnp.abs(raw)))
    step_rows[...] = step_size
    log_decay = -step_size * rate
    cumulative = jnp.dot(
        log_decay,
        (down <= across).astype(full),
        preferred_element_type=full,
        precision=lax.Precision.HIGHEST,
    )
    cum_rows[...] = cumulative
    square[...] = jnp.zeros_like(square)
    square[:head_count, :] = cumulative
    cum_cols[...] = square[...].T
    totals[me] = jnp.broadcast_to(cum_cols[row_count - 1 : row_count, :], totals.shape[1:])
    square[:head_count, :] = jnp.exp(cumulative[:, row_count - 1 : row_count] - cumulative) * step_size
    tail_cols[...] = square[...].T
    for index in (0, 1, 4):
        locals_[index].wait()
    pl.semaphore_wait(barrier, ring - 1 + experts - 1)
    start_weight(0, line)
    for copy in locals_[12:]:
        copy.start()

    @pl.when(me < ring - 1)
    def _():
        halo_copy(me + 1).start()

    for shift in range(1, ring):
        total_copy(shift).start()
    for index in (5, 6, 7):
        locals_[index].wait()

    capacity = 4 * row_count // experts
    names = lax.broadcasted_iota(jnp.int32, (experts, row_count), 0)
    members = [(names == routes_ref[k : k + 1, :]).astype(full) for k in range(2)]
    rank = jnp.dot(
        (members[0] + members[1]).astype(half),
        (down < across).astype(half),
        preferred_element_type=full,
    ) + (names * capacity).astype(full)
    plans[mine] = jnp.zeros_like(plans[mine])
    for k in range(2):
        plans[mine, k : k + 1, :] = jnp.sum(members[k] * rank, axis=0, keepdims=True)
        plans[mine, 2 + k : 3 + k, :] = pair_ref[k : k + 1, :]

    def plan_copy(shift):
        return pltpu.make_async_remote_copy(
            src_ref=plans.at[mine],
            dst_ref=plans.at[mine],
            send_sem=plan_send.at[shift],
            recv_sem=plan_recv.at[mine],
            device_id={"grp": lax.rem(mine + shift, experts)},
            device_id_type=MESH,
        )

    def plan_arrival(origin):
        return pltpu.make_async_remote_copy(
            src_ref=plans.at[origin],
            dst_ref=plans.at[origin],
            send_sem=plan_send.at[0],
            recv_sem=plan_recv.at[origin],
            device_id={"grp": lax.rem(mine + 1, experts)},
            device_id_type=MESH,
        )

    def send_plan(shift, carry):
        plan_copy(shift).start()
        return carry

    lax.fori_loop(1, experts, send_plan, 0)

    @pl.when(me > 0)
    def _():
        halo_copy(me).wait_recv()

    first_half = lax.broadcasted_iota(jnp.int32, (row_count, LANES), 1) < head_width
    offset = 8

    def convolve(column, padded):
        columns = pl.ds(column, LANES)
        before = halo[:, columns].astype(full)[16 - offset :]
        padded[:offset, :] = jnp.where(me > 0, before, 0.0)
        padded[offset:, :] = conv_ref[:, columns].astype(full)
        taps = taps_ref[:, columns]
        start = offset - tap_count + 1
        summed = taps[0:1] * padded[start : start + row_count, :]
        for k in range(1, tap_count):
            summed = summed + taps[k : k + 1] * padded[start + k : start + k + row_count, :]
        return (summed * jax.nn.sigmoid(summed)).astype(half)

    def by_head(columns_of_heads, pair):
        shifted = pltpu.roll(columns_of_heads, lax.rem(LANES - per_tile * pair, LANES), axis=1)
        return shifted[:, 0:1], shifted[:, 1:2]

    bc = convolve(width, padded.at[0]).astype(full)
    bt_ref[...] = bc.T[:state_width].astype(half)
    c_part = pltpu.roll(bc, LANES - state_width, axis=1)[:, :state_width].astype(half)
    c_ref[...] = c_part
    scores_ref[...] = jnp.dot(c_part, bt_ref[...], preferred_element_type=full)

    def take_in(part_index, carry):
        def tile(index, carry):
            pair = part_index * tiles + index
            column = pl.multiple_of(pair * LANES, LANES)
            x = convolve(column, padded.at[index])
            signal[:, pl.ds(column, LANES)] = x
            left, right = by_head(tail_cols[...], pair)
            scaled = (x.astype(full) * jnp.where(first_half, left, right)).astype(half)
            states[part_index, 0, :, pl.ds(pl.multiple_of(index * LANES, LANES), LANES)] = jnp.dot(
                bt_ref[...], scaled, preferred_element_type=full
            ).astype(half)
            return carry

        lax.fori_loop(0, tiles, tile, 0, unroll=True)
        launch(state_copy, part_index)
        return carry

    lax.fori_loop(0, LINES, take_in, 0)

    def within(part_index, carry):
        def tile(index, carry):
            pair = part_index * tiles + index
            column = pl.multiple_of(pair * LANES, LANES)
            cum = by_head(cum_cols[...], pair)
            mixing = []
            for turn in range(2):
                head = per_tile * pair + turn
                gap = cum[turn] - cum_rows[pl.ds(head, 1), :]
                decay = jnp.exp(jnp.where(down >= across, gap, -1e30))
                mixing.append(scores_ref[...] * decay * step_rows[pl.ds(head, 1), :])
            x = signal[:, pl.ds(column, LANES)].astype(full)
            stacked = jnp.concatenate(
                [jnp.where(first_half, x, 0.0), jnp.where(first_half, 0.0, x)], axis=0
            ).astype(half)
            skip = jnp.where(first_half, skip_ref[per_tile * pair], skip_ref[per_tile * pair + 1])
            base[:, pl.ds(column, LANES)] = (
                jnp.dot(
                    jnp.concatenate(mixing, axis=1).astype(half), stacked, preferred_element_type=full
                )
                + skip * x
            )
            return carry

        lax.fori_loop(0, tiles, tile, 0, unroll=True)
        relay(state_copy, part_index)
        return carry

    lax.fori_loop(0, 1, within, 0)
    relay_weight(0, 1)
    lax.fori_loop(1, LINES, within, 0)

    for shift in range(1, ring):
        total_arrival(lax.rem(me + shift, ring)).wait_recv()
    for slot in range(1, ring):
        origin = source(slot)
        passed = jnp.zeros((1, LANES), full)
        for between in range(ring):
            passed = passed + jnp.where(
                (between > origin) & (between < me), totals[between, 0:1, :], 0.0
            )
        reach_ref[slot : slot + 1, :] = jnp.where(origin < me, jnp.exp(passed), 0.0)
    reach_ref[0:1, :] = jnp.zeros((1, LANES), full)
    for index in (8, 9):
        locals_[index].wait()

    def gather_in(part_index, squares):
        for step in range(chips):
            state_copy(part_index, step, True).wait_recv()

        def tile(index, squares):
            pair = part_index * tiles + index
            column = pl.multiple_of(pair * LANES, LANES)
            columns = pl.ds(column, LANES)
            local = pl.ds(pl.multiple_of(index * LANES, LANES), LANES)
            left, right = by_head(reach_ref[...], pair)
            reach = jnp.where(first_half[: reach_ref.shape[0]], left, right)
            entering = jnp.zeros((state_width, LANES), full)
            for slot in range(1, ring):
                entering = entering + reach[slot : slot + 1] * states[
                    part_index, slot, :, local
                ].astype(full)
            carried = jnp.dot(c_ref[...], entering.astype(half), preferred_element_type=full)
            left, right = by_head(cum_cols[...], pair)
            fade = jnp.exp(jnp.where(first_half, left, right))
            gate = gate_ref[:, columns].astype(full)
            value = (base[:, columns] + carried * fade) * (gate * jax.nn.sigmoid(gate))
            rows[part_index, 0, :, local] = (value * norm_ref[pl.ds(pair, 1), :]).astype(half)
            return squares + jnp.sum(value * value, axis=1, keepdims=True)

        squares = lax.fori_loop(0, tiles, tile, squares, unroll=True)
        launch(rows_copy, part_index)
        return squares

    squares = lax.fori_loop(0, LINES, gather_in, jnp.zeros((row_count, 1), full))
    row_scale = lax.rsqrt(squares * (1.0 / width) + EPSILON)

    relay_weight(0, 2)
    start_weight(1, line)
    relay(rows_copy, 0)
    relay_weight(0, 3)
    relay(rows_copy, 1)
    relay(rows_copy, 2)
    relay_weight(1, 1)
    relay_weight(1, 2)
    relay(rows_copy, 3)
    relay_weight(1, 3)

    def rows_arrived(part_index, carry):
        for step in range(chips):
            rows_copy(part_index, step, True).wait_recv()
        return carry

    lax.fori_loop(0, LINES, rows_arrived, 0)

    def share_copy(stage, slot):
        return pltpu.make_async_remote_copy(
            src_ref=shares_out[stage].at[slot],
            dst_ref=shares_in[stage].at[me],
            send_sem=share_send.at[stage, slot],
            recv_sem=share_recv.at[stage, me],
            device_id={"seq": source(slot)},
            device_id_type=MESH,
        )

    def share_arrival(stage, column):
        return pltpu.make_async_remote_copy(
            src_ref=shares_out[stage].at[0],
            dst_ref=shares_in[stage].at[column],
            send_sem=share_send.at[stage, 0],
            recv_sem=share_recv.at[stage, column],
            device_id={"seq": source(1)},
            device_id_type=MESH,
        )

    starts = (0, weight_first.shape[1])
    for stage in range(STAGES):
        breadth = weights[stage].shape[1]
        columns_here = slice(starts[stage], starts[stage] + breadth)

        def project(index, carry):
            step = (index + 1) // 2
            at = line + jnp.where(lax.rem(index, 2) == 0, step, -step)

            @pl.when((at >= 0) & (at < LINES))
            def _():
                for shift in range(1, inner):
                    weight_arrival(stage, at * inner + lax.rem(place + shift, inner)).wait_recv()
                product = jnp.dot(
                    rows[at].reshape(ring * row_count, part),
                    weights[stage][pl.ds(pl.multiple_of(at * part, part), part), :],
                    preferred_element_type=full,
                )
                total[:, columns_here] += product

            return carry

        total[:, columns_here] = jnp.zeros((ring * row_count, breadth), full)
        lax.fori_loop(0, 2 * LINES - 1, project, 0)

        def hand_out(index, carry):
            slot = ring - 1 - index
            shares_out[stage][slot] = total[
                pl.ds(pl.multiple_of(slot * row_count, row_count), row_count), columns_here
            ].astype(half)

            @pl.when(slot > 0)
            def _():
                share_copy(stage, slot).start()

            return carry

        lax.fori_loop(0, ring, hand_out, 0)
        shares_in[stage][me] = shares_out[stage][0]

    for index in (10, 11):
        locals_[index].wait()
    squares = jnp.zeros((row_count, 1), full)
    for stage in range(STAGES):
        breadth = weights[stage].shape[1]

        def mix(index, squares):
            @pl.when(index != me)
            def _():
                share_arrival(stage, index).wait_recv()

            column = pl.multiple_of(index * share + starts[stage], LANES)
            values = (
                residual_ref[:, pl.ds(column, breadth)].astype(full)
                + row_scale * shares_in[stage][index].astype(full)
            ).astype(half)
            mixed_ref[:, pl.ds(column, breadth)] = values
            wide = values.astype(full)
            return squares + jnp.sum(wide * wide, axis=1, keepdims=True)

        squares = lax.fori_loop(0, ring, mix, squares)
    scale = lax.rsqrt(squares * (1.0 / width) + EPSILON)
    for tile in range(width // LANES):
        local = tile % tiles * LANES
        line_rows[line, tile // tiles, :, local : local + LANES] = (
            mixed_ref[:, tile * LANES : (tile + 1) * LANES].astype(full)
            * scale
            * gain_ref[tile : tile + 1, :]
        ).astype(half)

    def row_copy(at, up, index):
        return pltpu.make_async_remote_copy(
            src_ref=line_rows.at[at, index],
            dst_ref=line_rows.at[at, index],
            send_sem=row_send.at[at, 0 if up else 1, index],
            recv_sem=row_recv.at[at, index],
            device_id={"grp": mine + (inner if up else -inner)},
            device_id_type=MESH,
        )

    def slots_of(owner):
        return pl.ds(pl.multiple_of(owner * capacity, capacity), capacity)

    def across_copy(source, target, sends, recvs, at, shift, index):
        other = lax.rem(place + shift, inner)
        return pltpu.make_async_remote_copy(
            src_ref=source.at[at, index, slots_of(other)],
            dst_ref=target.at[at, index, slots_of(place)],
            send_sem=sends.at[at, shift, index],
            recv_sem=recvs.at[at, place, index],
            device_id={"grp": line * inner + other},
            device_id_type=MESH,
        )

    def across_arrival(source, target, sends, recvs, at, shift, index):
        other = lax.rem(place + shift, inner)
        return pltpu.make_async_remote_copy(
            src_ref=source.at[at, index, slots_of(other)],
            dst_ref=target.at[at, index, slots_of(other)],
            send_sem=sends.at[at, shift, index],
            recv_sem=recvs.at[at, other, index],
            device_id={"grp": line * inner + other},
            device_id_type=MESH,
        )

    pick_parts = (outgoing, arrived, pick_send, pick_recv)
    made_parts = (result, returned, made_send, made_recv)

    sum_rows = row_count // SPLIT
    sum_pieces = SPLIT * LINES

    def sum_part(ref, index):
        return ref.at[index // SPLIT, pl.ds(pl.multiple_of(lax.rem(index, SPLIT) * sum_rows, 16), sum_rows)]

    def sum_copy(to, up, index):
        way = 0 if up else 1
        return pltpu.make_async_remote_copy(
            src_ref=sum_part(sums_out.at[to], index),
            dst_ref=sum_part(sums_in.at[way, to], index),
            send_sem=sum_send.at[to, index],
            recv_sem=sum_recv.at[way, to, index],
            device_id={"grp": mine + (inner if up else -inner)},
            device_id_type=MESH,
        )

    def sum_arrival(to, up, index):
        way = 0 if up else 1
        return pltpu.make_async_remote_copy(
            src_ref=sum_part(sums_out.at[to], index),
            dst_ref=sum_part(sums_in.at[way, to], index),
            send_sem=sum_send.at[to, index],
            recv_sem=sum_recv.at[way, to, index],
            device_id={"grp": mine},
            device_id_type=MESH,
        )

    def take_plan(shift, carry):
        plan_arrival(lax.rem(mine + shift, experts)).wait_recv()
        return carry

    lax.fori_loop(1, experts, take_plan, 0)
    slot_count = inner * capacity
    slot_ids = lax.broadcasted_iota(jnp.int32, (slot_count, row_count), 0)

    at_end = (line == 0) | (line == LINES - 1)

    def forward(at, up, index):
        @pl.when((at <= line) & (line < LINES - 1) if up else (at >= line) & (line > 0))
        def _():
            row_copy(at, up, index).start()

    def plan_rows(at):
        plan = plans[at * inner + place]
        slot_of = (slot_ids + line * slot_count).astype(full)
        picks = jnp.where(plan[0:1] == slot_of, 1.0, 0.0) + jnp.where(plan[1:2] == slot_of, 1.0, 0.0)
        place_back[at] = picks.T.astype(half)
        pick_rows[at] = picks.astype(half)

    def take_piece(at, step, index):
        @pl.when(step > 0)
        def _():
            row_copy(at, True, index).wait_recv()

        forward(at, True, index)
        forward(at, False, index)
        outgoing[at, index] = jnp.dot(
            pick_rows[at], line_rows[at, index], preferred_element_type=full
        ).astype(half)
        for shift in range(1, inner):
            across_copy(*pick_parts, at, shift, index).start()
        arrived[at, index, slots_of(place)] = outgoing[at, index, slots_of(place)]

    def made_arrived(to, index):
        for shift in range(1, inner):
            across_arrival(*made_parts, to, shift, index).wait_recv()

    def send_sums(to, up, index):
        way = 0 if up else 1
        column = index // SPLIT
        some = pl.ds(pl.multiple_of(lax.rem(index, SPLIT) * sum_rows, 16), sum_rows)

        @pl.when(lax.rem(index, SPLIT) == 0)
        def _():
            made_arrived(to, column)

        share = jnp.dot(place_back[to, some], returned[to, column], preferred_element_type=full)
        behind = (line > 0) if up else (line < LINES - 1)

        @pl.when(behind)
        def _():
            sum_arrival(to, up, index).wait_recv()
            sums_out[to, column, some] = (share + sums_in[way, to, column, some].astype(full)).astype(half)

        @pl.when(jnp.logical_not(behind))
        def _():
            sums_out[to, column, some] = share.astype(half)

        sum_copy(to, up, index).start()

    def run_expert(at):
        scales = []
        own_ids = lax.broadcasted_iota(jnp.int32, (capacity, row_count), 0) + mine * capacity
        for origin in range(inner):
            plan = plans[at * inner + origin]
            own_slots = own_ids.astype(full)
            scales.append(
                jnp.sum(
                    jnp.where(plan[0:1] == own_slots, plan[2:3], 0.0)
                    + jnp.where(plan[1:2] == own_slots, plan[3:4], 0.0),
                    axis=1,
                    keepdims=True,
                )
            )
        scale = jnp.concatenate(scales, axis=0)
        gate_part = jnp.zeros((slot_count, expert_gate.shape[1]), full)
        up_part = gate_part
        for index in range(LINES):
            for shift in range(1, inner):
                across_arrival(*pick_parts, at, shift, index).wait_recv()
            rows_here = arrived[at, index]
            depth_here = slice(index * part, (index + 1) * part)
            gate_part = gate_part + jnp.dot(
                rows_here, expert_gate[depth_here, :], preferred_element_type=full
            )
            up_part = up_part + jnp.dot(
                rows_here, expert_up[depth_here, :], preferred_element_type=full
            )
        hidden = (gate_part * jax.nn.sigmoid(gate_part) * up_part).astype(half)
        for index in range(LINES):
            made = jnp.dot(
                hidden, expert_down[:, index * part : (index + 1) * part], preferred_element_type=full
            )
            result[at, index] = (made * scale).astype(half)
            for shift in range(1, inner):
                across_copy(*made_parts, at, shift, index).start()
            returned[at, index, slots_of(place)] = result[at, index, slots_of(place)]

    def plan_block(at, carry):
        plan_rows(at)
        return carry

    lax.fori_loop(0, LINES, plan_block, 0)

    def round_trip(step, carry):
        def take(turn, carry):
            ahead, index = step + turn // LINES, lax.rem(turn, LINES)
            for at, wanted in ((line - ahead, True), (line + ahead, ahead > 0)):

                @pl.when((at >= 0) & (at < LINES) & wanted)
                def _():
                    take_piece(at, ahead, index)

            return carry

        steps_here = jnp.where(at_end | (step == 0), 1, jnp.where(step == 1, LINES - 2, 0))
        lax.fori_loop(0, steps_here * LINES, take, 0)

        @pl.when(step == 0)
        def _():
            for copy in locals_[12:]:
                copy.wait()

        def turn(way, carry):
            at = line + jnp.where(line >= LINES // 2, 1, -1) * jnp.where(way == 0, -step, step)

            @pl.when((at >= 0) & (at < LINES) & ((way == 0) | (step > 0)))
            def _():
                run_expert(at)

            return carry

        lax.fori_loop(0, 2, turn, 0)

        lag = jnp.where(line >= LINES // 2, 0, 3)

        def pass_on(index, carry):
            down_index, up_index = index - lag, index - 3 + lag

            between = step > 0

            @pl.when(between & (LINES - 1 - step < line) & (down_index >= 0) & (down_index < sum_pieces))
            def _():
                send_sums(LINES - 1 - step, False, down_index)

            @pl.when(between & (step > line) & (up_index >= 0) & (up_index < sum_pieces))
            def _():
                send_sums(step, True, up_index)

            return carry

        lax.fori_loop(0, sum_pieces + 3, pass_on, 0)
        return carry

    lax.fori_loop(0, LINES, round_trip, 0)

    for index in range(LINES):
        columns = slice(index * part, (index + 1) * part)
        made_arrived(line, index)
        sum_here[...] = mixed_ref[:, columns].astype(full) + jnp.dot(
            place_back[line], returned[line, index], preferred_element_type=full
        )

        @pl.when(line > 0)
        def _():
            for turn in range(SPLIT):
                sum_arrival(line, True, index * SPLIT + turn).wait_recv()
            sum_here[...] += sums_in[0, line, index].astype(full)

        @pl.when(line < LINES - 1)
        def _():
            for turn in range(SPLIT):
                sum_arrival(line, False, index * SPLIT + turn).wait_recv()
            sum_here[...] += sums_in[1, line, index].astype(full)

        out_ref[:, columns] = sum_here[...].astype(half)

    @pl.when(me < ring - 1)
    def _():
        halo_copy(me + 1).wait_send()

    for shift in range(1, ring):
        total_copy(shift).wait_send()
        for stage in range(STAGES):
            share_copy(stage, shift).wait_send()

    def sent_plan(shift, carry):
        plan_copy(shift).wait_send()
        return carry

    lax.fori_loop(1, experts, sent_plan, 0)
    drain_ring(state_copy)
    drain_ring(rows_copy)

    def weight_left(at, carry):
        for stage in range(STAGES):
            drain_weight(stage, at)
        return carry

    lax.fori_loop(0, LINES, weight_left, 0)

    def drain(at, carry):
        def piece(index, carry):
            @pl.when((at <= line) & (line < LINES - 1))
            def _():
                row_copy(at, True, index).wait_send()

            @pl.when((at >= line) & (line > 0))
            def _():
                row_copy(at, False, index).wait_send()

            for shift in range(1, inner):
                across_copy(*pick_parts, at, shift, index).wait_send()
                across_copy(*made_parts, at, shift, index).wait_send()

            return carry

        def sum_piece(index, carry):
            @pl.when(at != line)
            def _():
                sum_copy(at, True, index).wait_send()

            return carry

        lax.fori_loop(0, sum_pieces, sum_piece, 0)

        lax.fori_loop(0, LINES, piece, 0)
        return carry

    lax.fori_loop(0, LINES, drain, 0)


def on_device(
    conv_input,
    conv_weight,
    step_raw,
    rate_log,
    skip_gain,
    gate_input,
    norm_gain,
    out_weight,
    residual,
    moe_gain,
    w_gate,
    w_up,
    w_down,
    routes,
    route_weights,
):
    half = jnp.bfloat16
    full = jnp.float32
    ring = lax.axis_size("seq")
    experts = lax.axis_size("grp")
    share = -(-out_weight.shape[1] // (ring * LANES)) * LANES
    extra = ring * share - out_weight.shape[1]
    row_count, channel_count = conv_input.shape[1:]
    tap_count = conv_weight.shape[0]
    head_count = rate_log.shape[0]
    inner_width = gate_input.shape[2]
    state_width = (channel_count - inner_width) // 2
    model_width = residual.shape[2]
    hidden_width = w_gate.shape[2]
    capacity = 4 * row_count // experts
    part = inner_width // LINES
    padded_residual, padded_weight = residual[0], out_weight
    if extra:
        padded_residual = jnp.pad(padded_residual, ((0, 0), (0, extra)))
        padded_weight = jnp.pad(padded_weight, ((0, 0), (0, extra)))
    vmem = pl.BlockSpec(memory_space=pltpu.VMEM)
    smem = pl.BlockSpec(memory_space=pltpu.SMEM)
    anywhere = pl.BlockSpec(memory_space=pl.ANY)
    inner = experts // LINES
    slot_count = inner * capacity
    row_slab = pltpu.VMEM((LINES, LINES, row_count, part), half)
    slot_slab = pltpu.VMEM((LINES, LINES, slot_count, part), half)
    pieces = [pltpu.VMEM((ring, row_count, breadth), half) for breadth in column_groups(share)]
    square = pltpu.VMEM((row_count, LANES), full)
    dma = pltpu.SemaphoreType.DMA
    layer_out = pl.pallas_call(
        functools.partial(layer_kernel, ring, experts),
        out_shape=jax.ShapeDtypeStruct((row_count, model_width), half),
        in_specs=[anywhere] * 4 + [smem] + [anywhere] * 10,
        out_specs=vmem,
        scratch_shapes=[
            pltpu.VMEM((row_count, channel_count), half),
            pltpu.VMEM((tap_count, channel_count), full),
            pltpu.VMEM((head_count, row_count), full),
            pltpu.VMEM((1, head_count), full),
            pltpu.VMEM((row_count, inner_width), half),
            pltpu.VMEM((inner_width // LANES, LANES), full),
            pltpu.VMEM((row_count, ring * share), half),
            pltpu.VMEM((model_width // LANES, LANES), full),
            pltpu.VMEM((model_width, hidden_width), half),
            pltpu.VMEM((model_width, hidden_width), half),
            pltpu.VMEM((hidden_width, model_width), half),
            pltpu.VMEM((2, row_count), jnp.int32),
            pltpu.VMEM((2, row_count), full),
            pltpu.VMEM((16, channel_count), half),
            pltpu.VMEM((part // LANES, row_count + 8, LANES), full),
            pltpu.VMEM((row_count, inner_width), half),
            pltpu.VMEM((row_count, inner_width), full),
            square,
            pltpu.VMEM((row_count, state_width), half),
            pltpu.VMEM((state_width, row_count), half),
            square,
            pltpu.VMEM((head_count, row_count), full),
            pltpu.VMEM((head_count, row_count), full),
            square,
            square,
            pltpu.VMEM((8, LANES), full),
            pltpu.VMEM((ring, 8, LANES), full),
            pltpu.VMEM((LINES, ring, state_width, part), half),
            pltpu.VMEM((LINES, ring, row_count, part), half),
            *[pltpu.VMEM((inner_width, breadth), half) for breadth in column_groups(share)],
            pltpu.VMEM((ring * row_count, share), full),
            *pieces,
            *pieces,
            pltpu.VMEM((row_count, ring * share), half),
            pltpu.VMEM((experts, 8, row_count), full),
            pltpu.VMEM((LINES, slot_count, row_count), half),
            pltpu.VMEM((LINES, row_count, slot_count), half),
            row_slab,
            slot_slab,
            slot_slab,
            slot_slab,
            slot_slab,
            row_slab,
            pltpu.VMEM((2, LINES, LINES, row_count, part), half),
            pltpu.VMEM((row_count, part), full),
            dma((15,)),
            dma((1,)),
            dma((1,)),
            dma((ring,)),
            dma((ring,)),
            dma((LINES, ring // 2)),
            dma((LINES, ring // 2)),
            dma((LINES, ring)),
            dma((LINES, ring // 2)),
            dma((LINES, ring // 2)),
            dma((LINES, ring)),
            dma((STAGES, LINES, 2)),
            dma((STAGES, LINES, experts // LINES)),
            dma((STAGES, experts)),
            dma((STAGES, ring)),
            dma((STAGES, ring)),
            dma((experts,)),
            dma((experts,)),
            dma((LINES, 2, LINES)),
            dma((LINES, LINES)),
            dma((LINES, inner, LINES)),
            dma((LINES, inner, LINES)),
            dma((LINES, inner, LINES)),
            dma((LINES, inner, LINES)),
            dma((LINES, SPLIT * LINES)),
            dma((2, LINES, SPLIT * LINES)),
        ],
        compiler_params=pltpu.CompilerParams(
            collective_id=0, has_side_effects=True, vmem_limit_bytes=56 * 1024 * 1024
        ),
        cost_estimate=pl.CostEstimate(
            flops=6 * 1024 * 1024 * 1024, bytes_accessed=64 * 1024 * 1024, transcendentals=0
        ),
    )(
        conv_input[0],
        conv_weight,
        step_raw[0].T,
        rate_log[None, :],
        skip_gain,
        gate_input[0],
        norm_gain.reshape(-1, LANES),
        padded_weight,
        padded_residual,
        moe_gain.reshape(-1, LANES),
        w_gate[0],
        w_up[0],
        w_down[0],
        routes[0].T,
        route_weights[0].T,
    )
    return layer_out[None]


def solution(mesh):
    in_specs = (
        P("grp", "seq", None),
        P(),
        P("grp", "seq", None),
        P(),
        P(),
        P("grp", "seq", None),
        P(),
        P("grp", None),
        P("grp", "seq", None),
        P(),
        P("grp", None, None),
        P("grp", None, None),
        P("grp", None, None),
        P("grp", "seq", None),
        P("grp", "seq", None),
    )
    out_specs = P("grp", "seq", None)
    return jax.shard_map(
        on_device, mesh=mesh, in_specs=in_specs, out_specs=out_specs, check_vma=False
    )
```
